32 devices in a mesh: rows: 4 (over y, x), wide: 8 (over z, core).
Axes of the slice: x: 2, y: 2, z: 4, core: 2. Of those that a mesh axis runs over, the one named last changes fastest.
Arguments:
- tokens: bfloat16 [4, 4096, 768], P('rows', 'wide'), may hold values from -6 to 6
- segments: int32 [4, 4096], P('rows'), may hold values from 0 to 3, never falling along the last dimension, each value on 1 to 2048 neighbouring positions
- ln1_gain: bfloat16 [768], P(('rows', 'wide')), may hold values from 0.25 to 1.75
- ln1_bias: bfloat16 [768], P(('rows', 'wide')), may hold values from -1.75 to 1.75
- ln2_gain: bfloat16 [768], P(('rows', 'wide')), may hold values from 0.25 to 1.75
- ln2_bias: bfloat16 [768], P(('rows', 'wide')), may hold values from -1.75 to 1.75
- q_weight: bfloat16 [768, 768], P(('rows', 'wide')), may hold values from -0.21875 to 0.21875
- q_bias: bfloat16 [768], P(('rows', 'wide')), may hold values from -3 to 3
- kv_weight: bfloat16 [768, 128], P(('rows', 'wide')), may hold values from -0.21875 to 0.21875
- k_bias: bfloat16 [64], replicated, may hold values from -3 to 3
- out_weight: bfloat16 [768, 768], P(('rows', 'wide')), may hold values from -1.75 to 1.75
- out_bias: bfloat16 [768], P(('rows', 'wide')), may hold values from -3 to 3
- up_weight: bfloat16 [768, 3072], P(('rows', 'wide')), may hold values from -0.21875 to 0.21875
- up_bias: bfloat16 [3072], P(('rows', 'wide')), may hold values from -3 to 3
- down_weight: bfloat16 [3072, 768], P(('rows', 'wide')), may hold values from -0.109375 to 0.109375
- cotangent: bfloat16 [4, 4096, 768], P('rows', 'wide'), may hold values from -8 to 8
Outputs:
- layer_out: bfloat16 [4, 4096, 768], P('rows', 'wide')
- input_grad: float32 [4, 4096, 768], P('rows', 'wide')
- grad_ln1_gain: float32 [768], P(('rows', 'wide'))
- grad_ln1_bias: float32 [768], P(('rows', 'wide'))
- grad_ln2_gain: float32 [768], P(('rows', 'wide'))
- grad_ln2_bias: float32 [768], P(('rows', 'wide'))
- grad_q_weight: float32 [768, 768], P(('rows', 'wide'))
- grad_q_bias: float32 [768], P(('rows', 'wide'))
- grad_kv_weight: float32 [768, 128], P(('rows', 'wide'))
- grad_k_bias: float32 [64], replicated
- grad_out_weight: float32 [768, 768], P(('rows', 'wide'))
- grad_out_bias: float32 [768], P(('rows', 'wide'))
- grad_up_weight: float32 [768, 3072], P(('rows', 'wide'))
- grad_up_bias: float32 [3072], P(('rows', 'wide'))
- grad_down_weight: float32 [3072, 768], P(('rows', 'wide'))
The draws below stay inside these ranges and needn't reach their ends.
Inputs may be any that keep to these rules, and one draw needn't show every extreme that they name: `segments`: along each row segment numbers never fall and start at 0; each document holds 1 to 2048 tokens and some document holds exactly 2048.
All inputs are finite; a program needn't handle non-finite values.
Results may differ from the reference program's by a relative error of at most 0.015.
The reference program's roundings to bfloat16 on the way count: a program that leaves them out, or rounds other values in their place, can miss the bound.
Values may be sent and summed in bfloat16 or wider, within the bound.
No kernel may reach another device: no remote copies, remote signals or barrier semaphores. Data moves between devices by JAX's collectives and lax.ppermute only.
A program may use at most 192 MiB of HBM per device.

```python
import math
import jax
import jax.numpy as jnp
import numpy as np
from jax import lax

D = 768
HEADS = 12
HD = 64
ROT = 16
FF = 3072
DOC = 2048
ROWS = 4
ROW = 4096
SEGS = 4


def spiked(array, stream_key, source, target, parts, factor):
    def block_of(position):
        return (jnp.arange(array.shape[position]) // (array.shape[position] // parts)).reshape((-1,) + (1,) * (array.ndim - 1 - position))

    near = jax.random.permutation(stream_key, parts)[block_of(target)]
    far = (block_of(target) + parts // 2) % parts
    return jnp.where((block_of(source) == near) | (block_of(source) == far), factor * array, array)


def steps_of(own_key, extent, split, low, high):
    factor_of, own = 1.0, jax.random.fold_in(own_key, 6)
    for position, parts in split:
        heights = jnp.exp(jax.random.uniform(jax.random.fold_in(own, position), (parts,), jnp.float32, low / len(split), high / len(split)))
        factor_of = factor_of * jnp.repeat(heights, extent[position] // parts).reshape([-1 if axis == position else 1 for axis in range(len(extent))])
    return factor_of


def profile(amount, total, reach, skew):
    weights = [(1 << 20) // math.isqrt(grade ** skew) + 1 for grade in range(2, amount + 1)]
    rest, holding = total - reach - (amount - 1), [1] * (amount - 1)
    while rest > 0:
        free = [i for i in range(amount - 1) if holding[i] < reach]
        pool, remaining = sum([weights[i] for i in free]), rest
        for i in free:
            extra = min(reach - holding[i], max(1, remaining * weights[i] // pool), rest)
            holding[i] = holding[i] + extra
            rest = rest - extra
    return np.array([reach] + holding)


def uneven_parts(stream_key, number_of, total, limit, lean):
    if number_of == 2:
        one = jax.random.randint(stream_key, (), max(1, total - limit), min(limit, total - 1) + 1)
        return jnp.stack([one, total - one])
    sizes = jnp.asarray(profile(number_of, total, limit, lean), jnp.int32)
    couples = (number_of - 1) // 2
    giver, sink = sizes[1:1 + 2 * couples:2], sizes[2:2 + 2 * couples:2]
    slack = jnp.minimum(giver - 1, limit - sink)
    passed = jax.random.randint(jax.random.fold_in(stream_key, 1), (couples,), 0, 1 << 20) % (slack + 1)
    sizes = sizes.at[1:1 + 2 * couples:2].set(giver - passed).at[2:2 + 2 * couples:2].set(sink + passed)
    return sizes[jax.random.permutation(jax.random.fold_in(stream_key, 2), number_of)]


def bell_draw(own_key, extent, width, most, shards=(), kind=jnp.bfloat16):
    entries = width * jax.random.normal(own_key, extent, jnp.float32)
    if shards:
        entries = entries * steps_of(own_key, extent, shards, -0.22, 0.18)
    return jnp.clip(entries, -most, most).astype(kind)


def bell_draw_with(stream_key, shape, width, most, pieces, heavy, held_as=jnp.bfloat16):
    values = width * jax.random.normal(stream_key, shape, jnp.float32)
    if pieces:
        values = values * steps_of(stream_key, shape, pieces, -0.22, 0.18)
    return jnp.clip(spiked(values, jax.random.fold_in(stream_key, 3), *heavy), -most, most).astype(held_as)


def setup_inputs(seed: int = 0) -> dict:
    key_of = jax.random.split(jax.random.key(seed), 17)
    return {
        "tokens": bell_draw(key_of[0], (ROWS, ROW, D), 1.0, 6.0, ((0, 4), (1, 8))),
        "segments": jax.vmap(lambda own: jnp.searchsorted(jnp.cumsum(uneven_parts(own, SEGS, ROW, DOC, 2)), jnp.arange(ROW), side="right"))(jax.random.split(key_of[1], ROWS)).reshape((ROWS, ROW)).astype(jnp.int32),
        "ln1_gain": jnp.clip(1.0 + 0.15 * jax.random.normal(key_of[2], (D,), jnp.float32), 0.25, 1.75).astype(jnp.bfloat16),
        "ln1_bias": bell_draw(key_of[3], (D,), 0.3, 1.75, ((0, 32),)),
        "ln2_gain": jnp.clip(1.0 + 0.15 * jax.random.normal(key_of[4], (D,), jnp.float32), 0.25, 1.75).astype(jnp.bfloat16),
        "ln2_bias": bell_draw(key_of[5], (D,), 0.3, 1.75, ((0, 32),)),
        "q_weight": bell_draw(key_of[6], (D, D), D ** -0.5, 0.21875, ((0, 32),)),
        "q_bias": bell_draw(key_of[7], (D,), 0.5, 3.0, ((0, 32),)),
        "kv_weight": bell_draw(key_of[8], (D, 2 * HD), D ** -0.5, 0.21875, ((0, 32),)),
        "k_bias": bell_draw(key_of[9], (HD,), 0.5, 3.0),
        "out_weight": bell_draw(key_of[10], (D, D), (D // 64) ** -0.5, 1.75, ((0, 32),)),
        "out_bias": bell_draw(key_of[11], (D,), 0.5, 3.0, ((0, 32),)),
        "up_weight": bell_draw(key_of[12], (D, FF), D ** -0.5, 0.21875, ((0, 32),)),
        "up_bias": bell_draw(key_of[13], (FF,), 0.5, 3.0, ((0, 32),)),
        "down_weight": bell_draw(key_of[14], (FF, D), FF ** -0.5, 0.109375, ((0, 32),)),
        "cotangent": bell_draw_with(key_of[15], (ROWS, ROW, D), 1.0, 8.0, ((0, 4), (1, 8)), (1, 2, 8, 2.0)),
    }


@jax.custom_vjp
def low(v):
    return lax.optimization_barrier(v.astype(jnp.bfloat16)).astype(jnp.float32)

@jax.custom_vjp
def low_back(v):
    return v

def low_keep(v):
    return (low(v), None)

def low_pass(kept, grad):
    return (grad,)

def back_keep(v):
    return (v, None)

def back_low(kept, grad):
    return (low(grad),)
low.defvjp(low_keep, low_pass)
low_back.defvjp(back_keep, back_low)
norm_eps = 1e-05
highest = lax.Precision.HIGHEST

def both_round(values):
    return low(low_back(values))

def layer_norm(values, scale_vec, shift_vec):
    center = values - lax.optimization_barrier(jnp.mean(values, axis=-1, keepdims=True))
    spread = lax.optimization_barrier(jnp.mean(center * center, axis=-1, keepdims=True))
    return center * lax.rsqrt(spread + norm_eps) * scale_vec + shift_vec

def doc_positions(segments):
    places = jnp.arange(ROW, dtype=jnp.int32)
    doc_begins = jnp.concatenate([jnp.ones((segments.shape[0], 1), bool), segments[:, 1:] != segments[:, :-1]], axis=1)
    firsts = lax.cummax(jnp.where(doc_begins, places[None, :], jnp.zeros((), jnp.int32)), axis=1)
    return (places[None, :] - firsts).astype(jnp.int32)

def rotate(values, cosine_table, sine_table, direction):
    half_rot = ROT // 2
    lower_part = values[..., :half_rot]
    upper_part = values[..., half_rot:ROT]
    turned_a = lower_part * cosine_table - direction * upper_part * sine_table
    turned_b = upper_part * cosine_table + direction * lower_part * sine_table
    return jnp.concatenate([turned_a, turned_b, values[..., ROT:]], axis=-1)

def attention(query, keys, values, segments):
    row_count = query.shape[0]
    block_rows = min(512, ROW)
    block_count = ROW // block_rows
    window_rows = DOC + block_rows
    score_scale = HD ** (-0.5)
    keys_padded = jnp.concatenate([jnp.zeros((row_count, DOC, HD), jnp.float32), keys], axis=1)
    values_padded = jnp.concatenate([jnp.zeros((row_count, DOC, HD), jnp.float32), values], axis=1)
    segs_padded = jnp.concatenate([jnp.full((row_count, DOC), -1, jnp.int32), segments.astype(jnp.int32)], axis=1)

    def one_block(block_index):
        zero_index = jnp.zeros((), jnp.int32)
        row_id = (block_index // block_count).astype(jnp.int32)
        block_pos = (block_index % block_count).astype(jnp.int32)
        first_row = (block_pos * block_rows).astype(jnp.int32)
        query_block = lax.dynamic_slice(query, (row_id, first_row, zero_index, zero_index), (1, block_rows, HEADS, HD))[0]
        key_block = lax.dynamic_slice(keys_padded, (row_id, first_row, zero_index), (1, window_rows, HD))[0]
        value_block = lax.dynamic_slice(values_padded, (row_id, first_row, zero_index), (1, window_rows, HD))[0]
        seg_keys = lax.dynamic_slice(segs_padded, (row_id, first_row), (1, window_rows))[0]
        seg_query = lax.dynamic_slice(segments.astype(jnp.int32), (row_id, first_row), (1, block_rows))[0]
        query_places = first_row + jnp.arange(block_rows, dtype=jnp.int32)
        key_places = first_row - DOC + jnp.arange(window_rows, dtype=jnp.int32)
        allowed = (seg_query[:, None] == seg_keys[None, :]) & (key_places[None, :] <= query_places[:, None])
        scores = jnp.einsum('qhd,kd->hqk', query_block, key_block, precision=highest) * score_scale
        scores = low_back(jnp.where(allowed[None], scores, -1e+30))
        soft_weights = low(jax.nn.softmax(scores, axis=-1))
        return jnp.einsum('hqk,kd->qhd', soft_weights, value_block, precision=highest)
    blocks_out = lax.map(jax.checkpoint(one_block), jnp.arange(row_count * block_count, dtype=jnp.int32))
    return blocks_out.reshape(row_count, ROW, HEADS, HD)

def forward(tokens_f, gain_one, shift_one, gain_two, shift_two, query_weight, query_bias, pair_weight, key_bias, proj_weight, proj_bias, hidden_weight, hidden_bias, back_weight, segments, relative):
    row_count = tokens_f.shape[0]
    normed_one = low(layer_norm(tokens_f, gain_one, shift_one))
    normed_two = low(layer_norm(tokens_f, gain_two, shift_two))
    query_pre = low_back(jnp.dot(normed_one, query_weight, precision=highest) + query_bias)
    pair_proj = jnp.dot(normed_one, pair_weight, precision=highest)
    key_pre = low_back(pair_proj[..., :HD] + key_bias)
    value_rows = both_round(pair_proj[..., HD:])
    frequency = 10000.0 ** (-(jnp.arange(ROT // 2, dtype=jnp.float32) * 2.0 / ROT))
    angles = relative.astype(jnp.float32)[..., None] * frequency
    cosine_table = jnp.cos(angles)
    sine_table = jnp.sin(angles)
    query_rows = both_round(rotate(query_pre.reshape(row_count, ROW, HEADS, HD), cosine_table[:, :, None, :], sine_table[:, :, None, :], 1.0))
    key_rows = both_round(rotate(key_pre, cosine_table, sine_table, 1.0))
    attended = both_round(attention(query_rows, key_rows, value_rows, segments))
    attn_out = jnp.dot(attended.reshape(row_count, ROW, D), proj_weight, precision=highest)
    hidden = low(jax.nn.gelu(low_back(jnp.dot(normed_two, hidden_weight, precision=highest) + hidden_bias), approximate=False))
    mlp_out = jnp.dot(hidden, back_weight, precision=highest)
    return tokens_f + attn_out + mlp_out + proj_bias

def reference(tokens, segments, ln1_gain, ln1_bias, ln2_gain, ln2_bias, q_weight, q_bias, kv_weight, k_bias, out_weight, out_bias, up_weight, up_bias, down_weight, cotangent):
    relative = doc_positions(segments)
    params = (tokens, ln1_gain, ln1_bias, ln2_gain, ln2_bias, q_weight, q_bias, kv_weight, k_bias, out_weight, out_bias, up_weight, up_bias, down_weight)
    params_f = tuple((item.astype(jnp.float32) for item in params))

    def closed(*inner):
        return forward(*inner, segments, relative)
    result, pullback = jax.vjp(closed, *params_f)
    grads = pullback(cotangent.astype(jnp.float32))
    return (result.astype(jnp.bfloat16), grads[0], grads[1], grads[2], grads[3], grads[4], grads[5], grads[6], grads[7], grads[8], grads[9], grads[10], grads[11], grads[12], grads[13])
```

```python
import jax
import jax.numpy as jnp
from jax import lax
from jax.experimental import pallas as pl
from jax.experimental.pallas import tpu as pltpu
from jax.sharding import Mesh, PartitionSpec as P

D = 768
HEADS = 12
HD = 64
ROT = 16
DOC = 2048
FF = 3072
MAX_SEGS = 32
norm_eps = 1e-05
BF = jnp.bfloat16
F32 = jnp.float32
HALF = HEADS // 2 * HD
BLK = 256
GROUP = 3


def dot(left, right, dims):
    return lax.dot_general(left, right, (dims, ((), ())), preferred_element_type=F32)


def core_swap(value):
    return lax.ppermute(value, "core", [(0, 1), (1, 0)])


def rows_swap(value, bit):
    return lax.ppermute(value, "rows", [(r, r ^ bit) for r in range(4)])


def chip_shift(value, by, wrap):
    count = lax.axis_size("chip")
    pairs = [(s, (s + by) % count) for s in range(count) if wrap or 0 <= s + by < count]
    return lax.ppermute(value, "chip", pairs)


def square_line():
    return lax.axis_size("rows") == 4 and lax.axis_size("chip") == 4


def place_kernel(lines_ref, flat_ref, cross_ref, low_ref, high_ref, out_ref, sems):
    row, chip = lax.axis_index("rows"), lax.axis_index("chip")
    piece = out_ref.shape[0] // 16
    copies = []
    for turn in range(4):
        for step in range(4):
            source = (lines_ref, flat_ref, cross_ref, low_ref if step < 2 else high_ref)[turn]
            offset = (step if turn < 3 else step % 2) * piece
            spot = ((row ^ turn) * 4 + lax.rem(chip + step, 4)) * piece
            copies.append(
                pltpu.make_async_copy(
                    source.at[pl.ds(offset, piece)],
                    out_ref.at[pl.ds(pl.multiple_of(spot, piece), piece)],
                    sems.at[turn * 4 + step],
                )
            )
    for copy in copies:
        copy.start()
    for copy in copies:
        copy.wait()


def gather_chips(piece):
    if not square_line():
        return lax.all_gather(piece, ("rows", "chip"), axis=0, tiled=True)
    size = piece.shape[0]
    lines = jnp.concatenate([piece] + [chip_shift(piece, -k, True) for k in (1, 2, 3)], axis=0)
    flat, cross = rows_swap(lines, 1), rows_swap(lines, 2)
    low = rows_swap(flat[: 2 * size], 2)
    high = rows_swap(cross[2 * size :], 1)
    return pl.pallas_call(
        place_kernel,
        out_shape=jax.ShapeDtypeStruct((16 * size,) + piece.shape[1:], piece.dtype),
        in_specs=[pl.BlockSpec(memory_space=pl.ANY)] * 5,
        out_specs=pl.BlockSpec(memory_space=pl.ANY),
        scratch_shapes=[pltpu.SemaphoreType.DMA((16,))],
        cost_estimate=pl.CostEstimate(
            flops=0, transcendentals=0, bytes_accessed=64 * size * piece.shape[1]
        ),
        name="place",
    )(lines, flat, cross, low, high)


def reduce_chips(terms):
    if not square_line():
        return lax.psum_scatter(
            terms.astype(F32), ("rows", "chip"), scatter_dimension=0, tiled=True
        )
    row, chip = lax.axis_index("rows"), lax.axis_index("chip")
    size = terms.shape[0] // 16
    grid = terms.reshape((4, 4, size) + terms.shape[1:])

    def plane(bit):
        return lax.dynamic_index_in_dim(grid, row ^ bit, 0, keepdims=False)

    far, flat, cross = plane(3), plane(1), plane(2)
    from_flat = rows_swap(far[:2], 1)
    from_cross = rows_swap(far[2:], 2)
    to_flat = jnp.concatenate(
        [flat[:2], (flat[2:].astype(F32) + from_cross.astype(F32)).astype(BF)], axis=0
    )
    to_cross = jnp.concatenate(
        [(cross[:2].astype(F32) + from_flat.astype(F32)).astype(BF), cross[2:]], axis=0
    )
    got_flat, got_cross = rows_swap(to_flat, 1), rows_swap(to_cross, 2)
    own = plane(0)

    def line(step):
        spot = lax.rem(chip + step, 4)
        pick = [
            lax.dynamic_index_in_dim(part, spot, 0, keepdims=False).astype(F32)
            for part in (own, got_flat, got_cross)
        ]
        return pick[0] + pick[1] + pick[2]

    total = line(0)
    for step in (1, 2, 3):
        total = total + chip_shift(line(step).astype(BF), step, True).astype(F32)
    return total


def sum_everywhere(value):
    if not square_line():
        return lax.psum(value, ("rows", "chip", "core"))
    value = value + core_swap(value)
    for bit in (1, 2):
        value = value + lax.ppermute(value, "chip", [(s, s ^ bit) for s in range(4)])
    for bit in (1, 2):
        value = value + rows_swap(value, bit)
    return value


def by_core(core, own, other, axis):
    return jnp.where(
        core == 0,
        jnp.concatenate([own, other], axis=axis),
        jnp.concatenate([other, own], axis=axis),
    )


def attn_kernel(
    scal_ref, q_ref, g_ref, pos_ref, kv_ref, kvt_ref, o_ref, dq_ref, dkv_ref, s_ref, r_ref
):
    group, block = pl.program_id(0), pl.program_id(1)
    core = scal_ref[0]
    low, high, edge = (scal_ref[1 + 3 * block + i] for i in range(3))
    half_blocks = kv_ref.shape[0] // 2 // BLK

    @pl.when((group == 0) & (block == 0))
    def _():
        dkv_ref[...] = jnp.zeros_like(dkv_ref)

    def spot(key_block):
        per_core = scal_ref[1 + 3 * pl.num_programs(1)]
        pair = key_block // (2 * per_core)
        side = lax.rem(key_block // per_core, 2) ^ core
        place = (pair * 2 + side) * per_core + lax.rem(key_block, per_core)
        return pl.multiple_of(place * BLK, BLK)

    starts, places = pos_ref[0:1, :], pos_ref[1:2, :]
    blank = jnp.zeros((HD, BLK), BF)
    queries, grads = [], []
    for h in range(GROUP):
        query = (q_ref[h * HD : (h + 1) * HD, :].astype(F32) * HD**-0.5).astype(BF)
        grad = g_ref[h * HD : (h + 1) * HD, :]
        queries.append(jnp.concatenate([query, blank], axis=0))
        grads.append(jnp.concatenate([blank, grad], axis=0))
        r_ref[:, h * BLK : (h + 1) * BLK] = queries[h]
        r_ref[:, (GROUP + h) * BLK : (GROUP + h + 1) * BLK] = grads[h]

    def scores(key_block, peaks):
        keys = kv_ref[pl.ds(spot(key_block), BLK), :]
        key_places = key_block * BLK + lax.broadcasted_iota(jnp.int32, (BLK, BLK), 0)
        allowed = (key_places >= starts) & (key_places <= places)
        new = []
        for h in range(GROUP):
            s = dot(keys, queries[h], ((1,), (0,)))
            s = jnp.where(allowed, s, -1e30)
            s_ref[h, pl.ds(pl.multiple_of((key_block - low) * BLK, BLK), BLK), :] = s
            new.append(jnp.maximum(peaks[h], jnp.max(s, axis=0, keepdims=True)))
        return tuple(new)

    peaks = lax.fori_loop(
        low, high, scores, tuple(jnp.full((1, BLK), -1e30, F32) for _ in range(GROUP))
    )

    def expo(key_block, carry):
        values = kvt_ref[HD:, pl.ds(spot(key_block), BLK)]
        new = []
        for h in range(GROUP):
            rows = pl.ds(pl.multiple_of((key_block - low) * BLK, BLK), BLK)
            e = jnp.exp(s_ref[h, rows, :] - peaks[h])
            s_ref[h, rows, :] = e
            total, out = carry[h]
            new.append(
                (
                    total + jnp.sum(e, axis=0, keepdims=True),
                    out + dot(values, e.astype(BF), ((1,), (0,))),
                )
            )
        return tuple(new)

    sums = lax.fori_loop(
        low,
        high,
        expo,
        tuple((jnp.zeros((1, BLK), F32), jnp.zeros((HD, BLK), F32)) for _ in range(GROUP)),
    )
    inverse, delta = [], []
    for h in range(GROUP):
        total, out = sums[h]
        inverse.append(1.0 / total)
        out = out * inverse[h]
        o_ref[h * HD : (h + 1) * HD, :] = out.astype(BF)
        delta.append(jnp.sum(out * grads[h][HD:, :].astype(F32), axis=0, keepdims=True))

    def back(key_block, dqs):
        where = spot(key_block)
        pairs = kv_ref[pl.ds(where, BLK), :]
        keys = kvt_ref[:HD, pl.ds(where, BLK)]
        new, soft, grad_scores = [], [], []
        for h in range(GROUP):
            rows = pl.ds(pl.multiple_of((key_block - low) * BLK, BLK), BLK)
            p = s_ref[h, rows, :] * inverse[h]
            dp = dot(pairs, grads[h], ((1,), (0,)))
            ds = (p * (dp - delta[h])).astype(BF)
            soft.append(p.astype(BF))
            grad_scores.append(ds)
            new.append(dqs[h] + dot(keys, ds, ((1,), (0,))))
        left = jnp.concatenate(grad_scores + soft, axis=1)
        dkv_ref[pl.ds(where, BLK), :] += dot(left, r_ref[...], ((1,), (1,)))
        return tuple(new)

    dqs = lax.fori_loop(
        low, high, back, tuple(jnp.zeros((HD, BLK), F32) for _ in range(GROUP))
    )
    for h in range(GROUP):
        dq_ref[h * HD : (h + 1) * HD, :] = (dqs[h] * HD**-0.5).astype(BF)


def attention(scal, query_t, grad_t, pos, kv, kv_t):
    features, tokens = query_t.shape
    blocks, window = tokens // BLK, kv.shape[0]
    width = GROUP * HD
    tile = pl.BlockSpec((width, BLK), lambda g, b, s: (g, b))
    return pl.pallas_call(
        attn_kernel,
        out_shape=(
            jax.ShapeDtypeStruct((features, tokens), BF),
            jax.ShapeDtypeStruct((features, tokens), BF),
            jax.ShapeDtypeStruct((window, 2 * HD), F32),
        ),
        grid_spec=pltpu.PrefetchScalarGridSpec(
            num_scalar_prefetch=1,
            grid=(features // width, blocks),
            in_specs=[
                tile,
                tile,
                pl.BlockSpec((8, BLK), lambda g, b, s: (0, b)),
                pl.BlockSpec((window, 2 * HD), lambda g, b, s: (0, 0)),
                pl.BlockSpec((2 * HD, window), lambda g, b, s: (0, 0)),
            ],
            out_specs=(
                tile,
                tile,
                pl.BlockSpec((window, 2 * HD), lambda g, b, s: (0, 0)),
            ),
            scratch_shapes=[
                pltpu.VMEM((GROUP, DOC + BLK, BLK), F32),
                pltpu.VMEM((2 * HD, 2 * GROUP * BLK), BF),
            ],
        ),
        compiler_params=pltpu.CompilerParams(
            dimension_semantics=("arbitrary", "arbitrary"), vmem_limit_bytes=40 << 20
        ),
        cost_estimate=pl.CostEstimate(
            flops=12 * features * tokens * DOC * 3 // 4,
            transcendentals=features // HD * tokens * DOC * 3 // 4,
            bytes_accessed=8 * features * tokens,
        ),
        name="attention",
    )(scal, query_t, grad_t, pos, kv, kv_t)


def turn(values, cosine, sine, direction):
    half = ROT // 2
    a, b = values[..., :half, :], values[..., half:ROT, :]
    return jnp.concatenate(
        [
            a * cosine - direction * b * sine,
            b * cosine + direction * a * sine,
            values[..., ROT:, :],
        ],
        axis=-2,
    )


def shards(
    tokens,
    segments,
    ln1_gain,
    ln1_bias,
    ln2_gain,
    ln2_bias,
    q_weight,
    q_bias,
    kv_weight,
    k_bias,
    out_weight,
    out_bias,
    up_weight,
    up_bias,
    down_weight,
    cotangent,
):
    core, chip = lax.axis_index("core"), lax.axis_index("chip")
    chips = lax.axis_size("rows") * lax.axis_size("chip")
    own = tokens.shape[1]
    both = 2 * own
    rows = q_weight.shape[0]
    hidden = up_bias.shape[0]
    back_chips = DOC // both

    def half_columns(array, which):
        return lax.dynamic_slice_in_dim(
            array, which * (array.shape[1] // 2), array.shape[1] // 2, 1
        )

    vectors = jnp.concatenate(
        [
            jnp.stack([ln1_gain, ln1_bias, ln2_gain, ln2_bias, q_bias, out_bias], axis=1),
            up_bias.reshape(rows, hidden // rows),
        ],
        axis=1,
    )
    vectors = jnp.pad(vectors, ((0, 0), (0, 128 - vectors.shape[1])))

    def first(which):
        return jnp.concatenate([half_columns(q_weight, which), kv_weight, vectors], axis=1)

    gathered = gather_chips(by_core(core, first(core), core_swap(first(1 - core)), 0))
    query_weight, pair_weight = gathered[:, :HALF], gathered[:, HALF : HALF + 2 * HD]
    vector_part = gathered[:, HALF + 2 * HD :].astype(F32)
    rows_of = vector_part[:, :6].T
    gain_one, shift_one, gain_two, shift_two = (rows_of[i : i + 1] for i in range(4))
    proj_bias = rows_of[5:6]
    query_bias = lax.dynamic_slice(vector_part, (core * HALF, 4), (HALF, 1))
    hidden_bias = lax.dynamic_index_in_dim(
        vector_part[:, 6 : 6 + hidden // rows].reshape(chips, 2, rows, hidden // rows),
        core,
        1,
        keepdims=False,
    ).reshape(1, FF // 2)

    columns = gather_chips(
        by_core(
            core,
            half_columns(out_weight, core),
            core_swap(half_columns(out_weight, 1 - core)),
            0,
        )
    )
    proj_weight = by_core(
        core,
        lax.dynamic_slice_in_dim(columns, core * HALF, HALF, 0),
        core_swap(lax.dynamic_slice_in_dim(columns, (1 - core) * HALF, HALF, 0)),
        1,
    )
    up_blocks = up_weight.reshape(rows, chips, 2, hidden)

    def up_half(which):
        return lax.dynamic_index_in_dim(up_blocks, which, 2, keepdims=False).reshape(rows, FF // 2)

    hidden_weight = gather_chips(by_core(core, up_half(core), core_swap(up_half(1 - core)), 0))
    back_weight = gather_chips(down_weight)

    own_tokens, own_grad = tokens[0], cotangent[0]
    features = jnp.concatenate([own_tokens, core_swap(own_tokens)], axis=0).astype(F32)
    grad_out = jnp.concatenate([own_grad, core_swap(own_grad)], axis=0)
    center = features - jnp.mean(features, axis=-1, keepdims=True)
    spread = lax.rsqrt(jnp.mean(center * center, axis=-1, keepdims=True) + norm_eps)
    unit = center * spread
    normed_one = (unit * gain_one + shift_one).astype(BF)
    normed_two = (unit * gain_two + shift_two).astype(BF)

    segrow = segments
    ids = lax.broadcasted_iota(jnp.int32, (MAX_SEGS, 1), 0)
    doc_starts = jnp.sum((segrow < ids).astype(jnp.int32), axis=1, keepdims=True)
    first_place, second_place = (chip * 2 + core) * own, (chip * 2 + 1 - core) * own
    span = lax.broadcasted_iota(jnp.int32, (1, own), 1)
    places = jnp.concatenate([first_place + span, second_place + span], axis=1)
    segs = jnp.concatenate(
        [
            lax.dynamic_slice(segrow, (0, first_place), (1, own)),
            lax.dynamic_slice(segrow, (0, second_place), (1, own)),
        ],
        axis=1,
    )
    starts = jnp.sum(jnp.where(segs == ids, doc_starts, 0), axis=0, keepdims=True)
    relative = places - starts
    frequency = 10000.0 ** (-(jnp.arange(ROT // 2, dtype=F32) * 2.0 / ROT))
    angles = relative.astype(F32) * frequency[:, None]
    cosine, sine = jnp.cos(angles), jnp.sin(angles)
    window_start = (chip - back_chips) * both
    pos = jnp.concatenate(
        [starts - window_start, places - window_start, jnp.zeros((6, both), jnp.int32)], axis=0
    )
    firsts, lasts = pos[:, ::BLK], pos[:, BLK - 1 :: BLK]
    scal = jnp.concatenate(
        [
            core.reshape(1),
            jnp.stack([firsts[0] // BLK, lasts[1] // BLK + 1, lasts[0]], axis=1).reshape(-1),
            jnp.full((1,), own // BLK, jnp.int32),
        ]
    ).astype(jnp.int32)

    query_t = dot(query_weight, normed_one, ((0,), (1,))) + query_bias
    query_t = turn(query_t.reshape(HEADS // 2, HD, both), cosine, sine, 1.0).astype(BF)
    query_t = query_t.reshape(HALF, both)
    pair_t = dot(pair_weight, normed_one[:own], ((0,), (1,)))
    key_t = turn(
        pair_t[:HD] + k_bias.astype(F32)[:, None], cosine[:, :own], sine[:, :own], 1.0
    ).astype(BF)
    own_pairs = jnp.concatenate([key_t, pair_t[HD:].astype(BF)], axis=0).T
    behind = jnp.concatenate(
        [chip_shift(own_pairs, k, False)[None] for k in range(back_chips, 0, -1)]
        + [own_pairs[None]],
        axis=0,
    )
    pairs = jnp.stack([behind, core_swap(behind)], axis=1).reshape(-1, 2 * HD)

    grad_t = dot(proj_weight, grad_out, ((1,), (1,))).astype(BF)
    out_t, grad_query_t, grad_pairs = attention(scal, query_t, grad_t, pos, pairs, pairs.T)

    hidden_pre = dot(normed_two, hidden_weight, ((1,), (0,))) + hidden_bias
    hidden_f, gelu_pull = jax.vjp(lambda z: jax.nn.gelu(z, approximate=False), hidden_pre)
    hidden_act = hidden_f.astype(BF)
    grad_back = dot(hidden_act, grad_out, ((0,), (0,))).astype(BF)
    grad_hidden = dot(grad_out, back_weight, ((1,), (1,)))
    grad_pre_f = gelu_pull(grad_hidden)[0]
    grad_pre = grad_pre_f.astype(BF)
    grad_up = dot(normed_two, grad_pre, ((0,), (0,))).astype(BF)
    grad_hidden_bias = jnp.sum(grad_pre.astype(F32), axis=0)
    back_sum = reduce_chips(grad_back)
    up_sum = reduce_chips(grad_up)
    grad_two = dot(grad_pre, hidden_weight, ((1,), (1,)))

    part = dot(out_t, proj_weight, ((0,), (0,))) + dot(hidden_act, back_weight, ((1,), (0,)))
    layer_out = (features[:own] + part[:own] + core_swap(part[own:]) + proj_bias).astype(BF)

    sides = grad_pairs.reshape(back_chips + 1, 2, own, 2 * HD)
    side_sum = sides[:, 0] + core_swap(sides[:, 1])
    pair_sum = side_sum[back_chips]
    for k in range(1, back_chips + 1):
        pair_sum = pair_sum + chip_shift(
            side_sum[back_chips - k].astype(BF), -k, False
        ).astype(F32)
    pair_sum_t = pair_sum.astype(BF).T
    key_pre_t = turn(
        pair_sum_t[:HD].astype(F32), cosine[:, :own], sine[:, :own], -1.0
    ).astype(BF)
    pair_grad_t = jnp.concatenate([key_pre_t, pair_sum_t[HD:]], axis=0)
    query_pre_t = (
        turn(grad_query_t.astype(F32).reshape(HEADS // 2, HD, both), cosine, sine, -1.0)
        .astype(BF)
        .reshape(HALF, both)
    )
    grad_query_weight = dot(normed_one, query_pre_t, ((0,), (1,))).astype(BF)
    grad_pair_weight = dot(normed_one[:own], pair_grad_t, ((0,), (1,))).astype(BF)
    grad_proj = dot(out_t, grad_out, ((1,), (0,))).astype(BF)
    grad_proj = by_core(
        core, half_columns(grad_proj, core), core_swap(half_columns(grad_proj, 1 - core)), 0
    )
    grad_one = dot(query_pre_t, query_weight, ((0,), (1,)))
    grad_one = grad_one + jnp.concatenate(
        [
            dot(pair_grad_t, pair_weight, ((0,), (1,))),
            jnp.zeros((own, D), F32),
        ],
        axis=0,
    )

    scaled = grad_one * gain_one + grad_two * gain_two
    scaled = scaled[:own] + core_swap(scaled[own:])
    own_unit = unit[:own]
    input_grad = own_grad.astype(F32) + spread[:own] * (
        scaled
        - jnp.mean(scaled, axis=-1, keepdims=True)
        - own_unit * jnp.mean(scaled * own_unit, axis=-1, keepdims=True)
    )

    query_bias_part = lax.dynamic_update_slice(
        jnp.zeros((D,), F32), jnp.sum(query_pre_t.astype(F32), axis=1), (core * HALF,)
    )
    table = jnp.stack(
        [
            jnp.sum(grad_one * unit, axis=0),
            jnp.sum(grad_one, axis=0),
            jnp.sum(grad_two * unit, axis=0),
            jnp.sum(grad_two, axis=0),
            query_bias_part,
            jnp.sum(own_grad.astype(F32), axis=0),
        ],
        axis=0,
    )
    two = hidden // (2 * rows)
    up_rows = grad_hidden_bias.reshape(chips, two, 2 * rows).transpose(1, 0, 2).reshape(two, D)
    table = jnp.concatenate([table, up_rows], axis=0)
    table = jnp.pad(table, ((0, 128 - table.shape[0]), (0, 0))).T.astype(BF)
    attn_sum = reduce_chips(
        jnp.concatenate([grad_query_weight, grad_proj, grad_pair_weight, table], axis=1)
    )
    mine = lax.dynamic_slice_in_dim(attn_sum, core * rows, rows, 0)
    theirs = core_swap(lax.dynamic_slice_in_dim(attn_sum, (1 - core) * rows, rows, 0))
    query_out = by_core(core, mine[:, :HALF], theirs[:, :HALF], 1)
    proj_out = by_core(core, mine[:, HALF : 2 * HALF], theirs[:, HALF : 2 * HALF], 1)
    rest = mine[:, 2 * HALF :] + theirs[:, 2 * HALF :]
    pair_out, vector_out = rest[:, : 2 * HD], rest[:, 2 * HD :]
    up_bias_out = attn_sum[:, 2 * HALF + 2 * HD + 6 : 2 * HALF + 2 * HD + 6 + two].T.reshape(hidden)
    key_bias_out = sum_everywhere(jnp.sum(key_pre_t.astype(F32), axis=1))

    mine = lax.dynamic_slice_in_dim(up_sum, core * rows, rows, 0)
    theirs = core_swap(lax.dynamic_slice_in_dim(up_sum, (1 - core) * rows, rows, 0))
    mine, theirs = mine.reshape(rows, chips, 1, hidden), theirs.reshape(rows, chips, 1, hidden)
    up_out = by_core(core, mine, theirs, 2).reshape(rows, FF)
    return (
        layer_out[None],
        input_grad[None],
        vector_out[:, 0],
        vector_out[:, 1],
        vector_out[:, 2],
        vector_out[:, 3],
        query_out,
        vector_out[:, 4],
        pair_out,
        key_bias_out,
        proj_out,
        vector_out[:, 5],
        up_out,
        up_bias_out,
        back_sum,
    )


def solution(mesh):
    devices = mesh.devices.reshape(mesh.shape["rows"], mesh.shape["wide"] // 2, 2)
    every, wide = ("rows", "chip", "core"), ("chip", "core")
    matrix, vector, sequence = P(every, None), P(every), P("rows", wide, None)
    return jax.shard_map(
        shards,
        mesh=Mesh(devices, every),
        in_specs=(
            sequence,
            P("rows", None),
            vector,
            vector,
            vector,
            vector,
            matrix,
            vector,
            matrix,
            P(),
            matrix,
            vector,
            matrix,
            vector,
            matrix,
            sequence,
        ),
        out_specs=(
            sequence,
            sequence,
            vector,
            vector,
            vector,
            vector,
            matrix,
            vector,
            matrix,
            P(),
            matrix,
            vector,
            matrix,
            vector,
            matrix,
        ),
        check_vma=False,
    )
```

```python
import functools
import math

import jax
import jax.numpy as jnp
from jax import lax
from jax.experimental import pallas as pl
from jax.experimental.pallas import tpu as pltpu
from jax.sharding import Mesh, PartitionSpec as P

D = 768
HEADS = 12
HD = 64
ROT = 16
DOC = 2048
FF = 3072
MAX_SEGS = 32
norm_eps = 1e-05
BF = jnp.bfloat16
F32 = jnp.float32
HALF = HEADS // 2 * HD
BLK = 256
GROUP = 6


def dot(left, right, dims):
    return lax.dot_general(left, right, (dims, ((), ())), preferred_element_type=F32)


def core_swap(value):
    return lax.ppermute(value, "core", [(0, 1), (1, 0)])


def rows_swap(value, bit):
    return lax.ppermute(value, "rows", [(r, r ^ bit) for r in range(4)])


def chip_shift(value, by, wrap):
    count = lax.axis_size("chip")
    pairs = [(s, (s + by) % count) for s in range(count) if wrap or 0 <= s + by < count]
    return lax.ppermute(value, "chip", pairs)


def square_line():
    return lax.axis_size("rows") == 4 and lax.axis_size("chip") == 4


def place_kernel(parts, lines_ref, flat_ref, cross_ref, far_ref, *rest):
    outs, sems = rest[:-1], rest[-1]
    row, chip = lax.axis_index("rows"), lax.axis_index("chip")
    size = lines_ref.shape[0] // 4
    copies = []
    for turn, source in enumerate((lines_ref, flat_ref, cross_ref, far_ref)):
        for step in range(4):
            place = (row ^ turn) * 4 + lax.rem(chip + step, 4)
            for first, count, out, stride, offset in parts:
                copies.append(
                    pltpu.make_async_copy(
                        source.at[pl.ds(step * size + first, count)],
                        outs[out].at[pl.ds(pl.multiple_of(place * stride + offset, 8), count)],
                        sems.at[len(copies)],
                    )
                )
    for copy in copies:
        copy.start()
    for copy in copies:
        copy.wait()


def gather_line(piece):
    return [piece] + [chip_shift(piece, -k, True) for k in (1, 2, 3)]


def gather_rows(lines):
    return lines, rows_swap(lines, 1), rows_swap(lines, 2), rows_swap(lines, 3)


def gather_place(lines, parts, shapes):
    return pl.pallas_call(
        functools.partial(place_kernel, parts),
        out_shape=tuple(jax.ShapeDtypeStruct(shape, BF) for shape in shapes),
        in_specs=[pl.BlockSpec(memory_space=pl.ANY)] * 4,
        out_specs=tuple(pl.BlockSpec(memory_space=pltpu.VMEM) for _ in shapes),
        scratch_shapes=[pltpu.SemaphoreType.DMA((16 * len(parts),))],
        cost_estimate=pl.CostEstimate(
            flops=0, transcendentals=0, bytes_accessed=4 * sum(a * b for a, b in shapes)
        ),
        name="place",
    )(*lines)


def gather_whole(piece):
    return lax.all_gather(piece, ("rows", "chip"), axis=0, tiled=True)


def reduce_first(terms):
    row = lax.axis_index("rows")
    grid = terms.reshape((4, 4, terms.shape[0] // 16) + terms.shape[1:])
    planes = [lax.dynamic_index_in_dim(grid, row ^ bit, 0, keepdims=False) for bit in range(4)]
    return planes, (rows_swap(planes[3][:2], 1), rows_swap(planes[3][2:], 2))


def reduce_second(planes, arrived):
    _, flat, cross, _ = planes
    from_flat, from_cross = arrived
    to_flat = jnp.concatenate(
        [flat[:2], (flat[2:].astype(F32) + from_cross.astype(F32)).astype(BF)], axis=0
    )
    to_cross = jnp.concatenate(
        [(cross[:2].astype(F32) + from_flat.astype(F32)).astype(BF), cross[2:]], axis=0
    )
    return rows_swap(to_flat, 1), rows_swap(to_cross, 2)


def reduce_third(planes, arrived):
    chip = lax.axis_index("chip")

    def line(step):
        spot = lax.rem(chip + step, 4)
        pick = [
            lax.dynamic_index_in_dim(part, spot, 0, keepdims=False).astype(F32)
            for part in (planes[0], *arrived)
        ]
        return pick[0] + pick[1] + pick[2]

    return line(0), [chip_shift(line(step).astype(BF), step, True) for step in (1, 2, 3)]


def reduce_last(own, arrived):
    return own + arrived[0].astype(F32) + arrived[1].astype(F32) + arrived[2].astype(F32)


def reduce_whole(terms):
    return lax.psum_scatter(terms.astype(F32), ("rows", "chip"), scatter_dimension=0, tiled=True)


def after(value, *others):
    return lax.optimization_barrier((value, others))[0]


def sum_everywhere(value):
    if not square_line():
        return lax.psum(value, ("rows", "chip", "core"))
    value = value + core_swap(value)
    for bit in (1, 2):
        value = value + lax.ppermute(value, "chip", [(s, s ^ bit) for s in range(4)])
    for bit in (1, 2):
        value = value + rows_swap(value, bit)
    return value


def by_core(core, own, other, axis):
    return jnp.where(
        core == 0,
        jnp.concatenate([own, other], axis=axis),
        jnp.concatenate([other, own], axis=axis),
    )


def vector_kernel(v_ref, rows_ref, bias_ref):
    core = lax.axis_index("core")
    count = v_ref.shape[0]
    lane = lax.broadcasted_iota(jnp.int32, (128, D), 0)
    place = lax.broadcasted_iota(jnp.int32, (128, D), 1)
    pick = jnp.where(lane == lax.rem(place, 24), 1.0, 0.0).astype(BF)
    spread = dot(v_ref[...], pick, ((1,), (0,)))
    row = lax.broadcasted_iota(jnp.int32, (count, D), 0)
    spot = lax.broadcasted_iota(jnp.int32, (count, D), 1)
    own = jnp.where(row // 16 == spot // 24, spread, 0.0).astype(BF)
    kind = lax.rem(lax.broadcasted_iota(jnp.int32, (8, count), 1), 16)
    which = lax.broadcasted_iota(jnp.int32, (8, count), 0)
    rows_ref[...] = dot(jnp.where(kind == which, 1.0, 0.0).astype(BF), own, ((1,), (0,)))
    bias_ref[...] = jnp.zeros_like(bias_ref)
    start = (2 * (spot // 48) + core) * 16 + 6 + lax.rem(spot, 48) // 24
    for k in range(2):
        bias_ref[k : k + 1, :] = jnp.sum(
            jnp.where(row == start + 2 * k, spread, 0.0), axis=0, keepdims=True
        )


def turn(values, cosine, sine, direction):
    half = ROT // 2
    a, b = values[:half, :], values[half:ROT, :]
    return jnp.concatenate(
        [a * cosine - direction * b * sine, b * cosine + direction * a * sine, values[ROT:, :]],
        axis=0,
    )


def standard(tokens):
    values = tokens.astype(F32)
    center = values - jnp.mean(values, axis=-1, keepdims=True)
    spread = lax.rsqrt(jnp.mean(center * center, axis=-1, keepdims=True) + norm_eps)
    return center * spread, spread


def front_kernel(
    own_ref, other_ref, w_ref, rows_ref, kbias_ref, cos_ref, sin_ref,
    h1_ref, h2_ref, h2t_ref, q_ref, pairs_ref, keep_ref, send_ref,
):
    core = lax.axis_index("core")
    count = own_ref.shape[0]
    gain_one, shift_one, gain_two, shift_two = (rows_ref[i : i + 1, :] for i in range(4))
    for part, ref in enumerate((own_ref, other_ref)):
        unit, _ = standard(ref[...])
        spot = pl.ds(part * count, count)
        h1_ref[spot, :] = (unit * gain_one + shift_one).astype(BF)
        normed = (unit * gain_two + shift_two).astype(BF)
        h2_ref[spot, :] = normed
        h2t_ref[:, part * count : (part + 1) * count] = normed.T
    pair = dot(w_ref[:, 2 * HALF :], h1_ref[:count, :], ((0,), (1,)))
    key = turn(
        pair[:HD] + kbias_ref[...], cos_ref[:, :count], sin_ref[:, :count], 1.0
    ).astype(BF)
    pairs_ref[...] = jnp.concatenate([key, pair[HD:].astype(BF)], axis=0).T
    query = dot(w_ref[:, :HALF], h1_ref[...], ((0,), (1,)))
    bias = jnp.where(core == 0, rows_ref[4:5, :HALF], rows_ref[4:5, HALF:])
    query = query + jnp.broadcast_to(bias, (8, HALF)).T[:, :1]
    for h in range(HEADS // 2):
        q_ref[h * HD : (h + 1) * HD, :] = turn(
            query[h * HD : (h + 1) * HD, :], cos_ref[...], sin_ref[...], 1.0
        ).astype(BF)
    for index, ref in ((core, keep_ref), (1 - core, send_ref)):
        spot = pl.ds(pl.multiple_of(index * HALF, HALF), HALF)
        ref[...] = w_ref[spot, HALF : 2 * HALF]


def front(own, other, weights, rows, k_bias, cosine, sine):
    both = 2 * own.shape[0]
    return pl.pallas_call(
        front_kernel,
        out_shape=(
            jax.ShapeDtypeStruct((both, D), BF),
            jax.ShapeDtypeStruct((both, D), BF),
            jax.ShapeDtypeStruct((D, both), BF),
            jax.ShapeDtypeStruct((HALF, both), BF),
            jax.ShapeDtypeStruct((own.shape[0], 2 * HD), BF),
            jax.ShapeDtypeStruct((HALF, HALF), BF),
            jax.ShapeDtypeStruct((HALF, HALF), BF),
        ),
        compiler_params=pltpu.CompilerParams(vmem_limit_bytes=48 << 20),
        cost_estimate=pl.CostEstimate(
            flops=2 * both * D * (HALF + 2 * HD), transcendentals=both, bytes_accessed=8 * both * D
        ),
        name="front",
    )(own, other, weights, rows, k_bias, cosine, sine)


def attn_kernel(
    scal_ref, q_ref, grad_ref, keep_ref, got_ref, pos_ref, cos_ref, sin_ref, mine_ref, theirs_ref,
    o_ref, dq_ref, dmine_ref, dtheirs_ref,
    kv_ref, kvt_ref, dkv_ref, g_ref, s_ref, r_ref, rt_ref,
):
    block = pl.program_id(0)
    core = scal_ref[0]
    low, high, edge = (scal_ref[1 + 3 * block + i] for i in range(3))
    wide = GROUP * BLK
    half = kv_ref.shape[0] // 2
    own_blocks = pl.num_programs(0) // 2

    @pl.when(block == 0)
    def _():
        dkv_ref[...] = jnp.zeros_like(dkv_ref)
        for part, ref in enumerate((mine_ref, theirs_ref)):
            kv_ref[part * half : (part + 1) * half, :] = ref[...]
            kvt_ref[: 2 * HD, part * half : (part + 1) * half] = ref[...].T
        kvt_ref[2 * HD :, :] = jnp.ones((16, 2 * half), BF)

    def spot(key_block):
        side = lax.rem(key_block // own_blocks, 2) ^ core
        place = (key_block // (2 * own_blocks)) * own_blocks + lax.rem(key_block, own_blocks)
        return pl.multiple_of(side * half + place * BLK, BLK)

    def slot(key_block):
        return pl.ds(pl.multiple_of((key_block - low) * BLK, BLK), BLK)

    near = pl.ds(pl.multiple_of(core * HALF, HALF), HALF)
    away = pl.ds(pl.multiple_of((1 - core) * HALF, HALF), HALF)
    g_ref[...] = (
        dot(keep_ref[...], grad_ref[:, near], ((1,), (1,)))
        + dot(got_ref[...], grad_ref[:, away], ((1,), (1,)))
    ).astype(BF)
    starts = jnp.concatenate([pos_ref[0:1, :]] * GROUP, axis=1)
    places = jnp.concatenate([pos_ref[1:2, :]] * GROUP, axis=1)
    blank = jnp.zeros((HD, BLK), BF)
    for h in range(GROUP):
        query = (q_ref[h * HD : (h + 1) * HD, :].astype(F32) * HD**-0.5).astype(BF)
        grad = g_ref[h * HD : (h + 1) * HD, :]
        query = jnp.concatenate([query, blank], axis=0)
        grad = jnp.concatenate([blank, grad], axis=0)
        r_ref[0, :, h * BLK : (h + 1) * BLK] = query
        r_ref[1, :, h * BLK : (h + 1) * BLK] = grad
        rt_ref[h * BLK : (h + 1) * BLK, :] = query.T
        rt_ref[(GROUP + h) * BLK : (GROUP + h + 1) * BLK, :] = grad.T

    def scores(masked, key_block, peak):
        keys = kv_ref[pl.ds(spot(key_block), BLK), :]
        s = dot(keys, r_ref[0], ((1,), (0,)))
        if masked:
            key_places = key_block * BLK + lax.broadcasted_iota(jnp.int32, (BLK, wide), 0)
            s = jnp.where((key_places >= starts) & (key_places <= places), s, -1e30)
        s_ref[slot(key_block), :] = s
        return jnp.maximum(peak, jnp.max(s, axis=0, keepdims=True))

    clear = jnp.minimum((edge + BLK - 1) // BLK, high - 1)
    peak = jnp.full((1, wide), -1e30, F32)
    peak = lax.fori_loop(low, clear, functools.partial(scores, True), peak)
    peak = lax.fori_loop(clear, high - 1, functools.partial(scores, False), peak)
    peak = scores(True, high - 1, peak)

    def expo(key_block, out):
        values = kvt_ref[HD:, pl.ds(spot(key_block), BLK)]
        e = jnp.exp(s_ref[slot(key_block), :] - peak)
        s_ref[slot(key_block), :] = e
        return out + dot(values, e.astype(BF), ((1,), (0,)))

    out = lax.fori_loop(low, high, expo, jnp.zeros((HD + 16, wide), F32))
    inverse = 1.0 / out[HD : HD + 1, :]
    out = out[:HD] * inverse
    deltas = []
    for h in range(GROUP):
        part = out[:, h * BLK : (h + 1) * BLK]
        o_ref[h * HD : (h + 1) * HD, :] = part.astype(BF)
        deltas.append(
            jnp.sum(part * g_ref[h * HD : (h + 1) * HD, :].astype(F32), axis=0, keepdims=True)
        )
    delta = jnp.concatenate(deltas, axis=1)

    def back(key_block, dq):
        where = spot(key_block)
        pairs = kv_ref[pl.ds(where, BLK), :]
        keys = kvt_ref[:HD, pl.ds(where, BLK)]
        p = s_ref[slot(key_block), :] * inverse
        dp = dot(pairs, r_ref[1], ((1,), (0,)))
        ds = (p * (dp - delta)).astype(BF)
        left = jnp.concatenate([ds, p.astype(BF)], axis=1)
        dkv_ref[pl.ds(where, BLK), :] += dot(left, rt_ref[...], ((1,), (0,)))
        return dq + dot(keys, ds, ((1,), (0,)))

    dq = lax.fori_loop(low, high, back, jnp.zeros((HD, wide), F32)) * HD**-0.5
    for h in range(GROUP):
        part = dq[:, h * BLK : (h + 1) * BLK].astype(BF).astype(F32)
        dq_ref[h * HD : (h + 1) * HD, :] = turn(part, cos_ref[...], sin_ref[...], -1.0).astype(BF)

    @pl.when(block == pl.num_programs(0) - 1)
    def _():
        dmine_ref[...] = dkv_ref[:half, :]
        dtheirs_ref[...] = dkv_ref[half:, :]


def attention(scal, query_t, grad_out, keep, got, pos, cosine, sine, mine, theirs):
    features, tokens = query_t.shape
    blocks, half = tokens // BLK, mine.shape[0]
    tile = pl.BlockSpec((features, BLK), lambda b, s: (0, b))
    small = pl.BlockSpec((8, BLK), lambda b, s: (0, b))

    def whole(rows, columns):
        return pl.BlockSpec((rows, columns), lambda b, s: (0, 0))

    return pl.pallas_call(
        attn_kernel,
        out_shape=(
            jax.ShapeDtypeStruct((features, tokens), BF),
            jax.ShapeDtypeStruct((features, tokens), BF),
            jax.ShapeDtypeStruct((half, 2 * HD), F32),
            jax.ShapeDtypeStruct((half, 2 * HD), F32),
        ),
        grid_spec=pltpu.PrefetchScalarGridSpec(
            num_scalar_prefetch=1,
            grid=(blocks,),
            in_specs=[
                tile,
                pl.BlockSpec((BLK, D), lambda b, s: (b, 0)),
                whole(HALF, HALF),
                whole(HALF, HALF),
                small,
                small,
                small,
                whole(half, 2 * HD),
                whole(half, 2 * HD),
            ],
            out_specs=(tile, tile, whole(half, 2 * HD), whole(half, 2 * HD)),
            scratch_shapes=[
                pltpu.VMEM((2 * half, 2 * HD), BF),
                pltpu.VMEM((2 * HD + 16, 2 * half), BF),
                pltpu.VMEM((2 * half, 2 * HD), F32),
                pltpu.VMEM((features, BLK), BF),
                pltpu.VMEM((DOC + BLK, GROUP * BLK), F32),
                pltpu.VMEM((2, 2 * HD, GROUP * BLK), BF),
                pltpu.VMEM((2 * GROUP * BLK, 2 * HD), BF),
            ],
        ),
        compiler_params=pltpu.CompilerParams(
            dimension_semantics=("arbitrary",), vmem_limit_bytes=48 << 20
        ),
        cost_estimate=pl.CostEstimate(
            flops=12 * features * tokens * DOC * 3 // 4,
            transcendentals=features // HD * tokens * DOC * 3 // 4,
            bytes_accessed=8 * features * tokens,
        ),
        name="attention",
    )(scal, query_t, grad_out, keep, got, pos, cosine, sine, mine, theirs)


def heads_kernel(
    o_ref, dq_ref, h1_ref, grad_ref, w_ref, keep_ref, got_ref,
    part_ref, dh_ref, gq_ref, keep_out_ref, send_out_ref, sums_ref,
):
    core = lax.axis_index("core")
    near = pl.ds(pl.multiple_of(core * HALF, HALF), HALF)
    away = pl.ds(pl.multiple_of((1 - core) * HALF, HALF), HALF)
    keep_out_ref[...] = dot(o_ref[...], grad_ref[:, near], ((1,), (0,))).astype(BF)
    send_out_ref[...] = dot(o_ref[...], grad_ref[:, away], ((1,), (0,))).astype(BF)
    gq_ref[...] = dot(dq_ref[...], h1_ref[...], ((1,), (0,))).T.astype(BF)
    heads = o_ref[...].T
    part_ref[:, near] = dot(heads, keep_ref[...], ((1,), (0,)))
    part_ref[:, away] = dot(heads, got_ref[...], ((1,), (0,)))
    dh_ref[...] = dot(dq_ref[...].T, w_ref[...], ((1,), (1,)))
    ones = jnp.ones((8, dq_ref.shape[1]), BF)
    sums_ref[...] = jnp.zeros_like(sums_ref)
    sums_ref[0:8, near] = dot(ones, dq_ref[...], ((1,), (1,)))
    count = grad_ref.shape[0] // 2
    sums_ref[8:16, :] = dot(ones[:, :count], grad_ref[:count, :], ((1,), (0,)))


def after_heads(out_t, dq_t, normed, grad_out, query_weight, keep, got):
    both = normed.shape[0]
    return pl.pallas_call(
        heads_kernel,
        out_shape=(
            jax.ShapeDtypeStruct((both, D), F32),
            jax.ShapeDtypeStruct((both, D), F32),
            jax.ShapeDtypeStruct((D, HALF), BF),
            jax.ShapeDtypeStruct((HALF, HALF), BF),
            jax.ShapeDtypeStruct((HALF, HALF), BF),
            jax.ShapeDtypeStruct((16, D), F32),
        ),
        compiler_params=pltpu.CompilerParams(vmem_limit_bytes=48 << 20),
        cost_estimate=pl.CostEstimate(
            flops=8 * both * D * HALF, transcendentals=0, bytes_accessed=12 * both * D
        ),
        name="after_heads",
    )(out_t, dq_t, normed, grad_out, query_weight, keep, got)


def pairs_kernel(
    own_ref, near_ref, far_ref, h1_ref, w_ref, cos_ref, sin_ref, gw_ref, dh_ref, gbias_ref
):
    total = own_ref[...] + near_ref[...].astype(F32) + far_ref[...].astype(F32)
    total = total.astype(BF).astype(F32).T
    key = turn(total[:HD], cos_ref[...], sin_ref[...], -1.0)
    grad = jnp.concatenate([key, total[HD:]], axis=0).astype(BF)
    gw_ref[...] = dot(grad, h1_ref[...], ((1,), (0,))).T.astype(BF)
    dh_ref[...] = dot(grad.T, w_ref[...], ((1,), (1,)))
    ones = jnp.ones((8, grad.shape[1]), BF)
    gbias_ref[...] = dot(ones, grad, ((1,), (1,)))


def after_pairs(own, near, far, normed, pair_weight, cosine, sine):
    count = own.shape[0]

    def whole(rows, columns):
        return pl.BlockSpec((rows, columns), lambda i: (0, 0))

    return pl.pallas_call(
        pairs_kernel,
        out_shape=(
            jax.ShapeDtypeStruct((D, 2 * HD), BF),
            jax.ShapeDtypeStruct((count, D), F32),
            jax.ShapeDtypeStruct((8, 2 * HD), F32),
        ),
        grid=(1,),
        in_specs=[
            whole(count, 2 * HD),
            whole(count, 2 * HD),
            whole(count, 2 * HD),
            whole(count, D),
            whole(D, 2 * HD),
            whole(8, count),
            whole(8, count),
        ],
        out_specs=(whole(D, 2 * HD), whole(count, D), whole(8, 2 * HD)),
        compiler_params=pltpu.CompilerParams(vmem_limit_bytes=32 << 20),
        cost_estimate=pl.CostEstimate(
            flops=8 * count * D * HD, transcendentals=0, bytes_accessed=8 * count * D
        ),
        name="after_pairs",
    )(own, near, far, normed, pair_weight, cosine, sine)


def ffn_units(step, h_ref, ht_ref, g_ref, up_ref, bias_ref, down_ref, grad_ref, act_ref, dz_ref):
    spot = pl.ds(pl.multiple_of(step * BLK, BLK), BLK)
    up, down = up_ref[:, spot], down_ref[spot, :]
    z = dot(h_ref[...], up, ((1,), (0,))) + bias_ref[:, spot]
    below = 0.5 * (1.0 + lax.erf(z * 0.5**0.5))
    slope = below + z * (jnp.exp(-0.5 * z * z) * (0.5 / math.pi) ** 0.5)
    act = (z * below).astype(BF)
    grad = (dot(g_ref[...], down, ((1,), (1,))) * slope).astype(BF)
    grad_ref[:, spot] = dot(ht_ref[...], grad, ((1,), (0,))).astype(BF)
    grad_ref[spot, D : 2 * D] = dot(act, g_ref[...], ((0,), (0,))).astype(BF)
    act_ref[:, spot] = act
    dz_ref[:, spot] = grad
    return jnp.sum(grad.astype(F32), axis=0, keepdims=True), spot


def ffn_first_kernel(
    h_ref, ht_ref, g_ref, up_ref, bias_ref, down_ref, part_ref,
    out_ref, dh_ref, grad_ref, gbias_ref,
    act_ref, dz_ref,
):
    step = pl.program_id(0)
    units = up_ref.shape[1] // BLK

    @pl.when(step < units)
    def _():
        gbias, spot = ffn_units(
            step, h_ref, ht_ref, g_ref, up_ref, bias_ref, down_ref, grad_ref, act_ref, dz_ref
        )
        gbias_ref[:, spot] = gbias

    @pl.when(step >= units)
    def _():
        spot = pl.ds(pl.multiple_of((step - units) * BLK, BLK), BLK)
        out_ref[...] = part_ref[...] + dot(act_ref[spot, :], down_ref[...], ((1,), (0,)))
        dh_ref[...] = dot(dz_ref[spot, :], up_ref[...], ((1,), (1,)))


def ffn_second_kernel(
    h_ref, ht_ref, g_ref, up_ref, bias_ref, down_ref,
    part_ref, dh_in_ref, x_ref, one_ref, pair_ref, rows_ref, sums_ref, bias0_ref, gpair_ref,
    keep_ref, send_ref, tkeep_ref, tsend_ref, grad_ref,
    act_ref, dz_ref, table_ref,
):
    step = pl.program_id(0)
    units = up_ref.shape[1] // BLK
    blocks = pl.num_programs(0) - units

    @pl.when(step == 0)
    def _():
        table_ref[...] = jnp.zeros_like(table_ref)
        table_ref[4:5, :] = sums_ref[0:1, :]
        table_ref[5:6, :] = sums_ref[8:9, :]
        table_ref[6:7, :] = bias0_ref[...]
        grad_ref[:, 2 * D : 2 * D + 2 * HD] = gpair_ref[...]

    @pl.when(step < units)
    def _():
        gbias, spot = ffn_units(
            step, h_ref, ht_ref, g_ref, up_ref, bias_ref, down_ref, grad_ref, act_ref, dz_ref
        )
        table_ref[7:8, spot] = gbias

    def tokens(first):
        spot = pl.ds(pl.multiple_of((step - units) * BLK, BLK), BLK)
        out = part_ref[...] + dot(act_ref[spot, :], down_ref[...], ((1,), (0,)))
        two = dh_in_ref[...] + dot(dz_ref[spot, :], up_ref[...], ((1,), (1,)))
        one = one_ref[...]
        if first:
            one = one + pair_ref[...]
        unit, _ = standard(x_ref[...])
        scaled = one * rows_ref[0:1, :] + two * rows_ref[2:3, :]
        for ref, value in (
            ((keep_ref, out), (tkeep_ref, scaled)) if first else ((send_ref, out), (tsend_ref, scaled))
        ):
            ref[...] = value
        for i, value in enumerate((one * unit, one, two * unit, two)):
            table_ref[i : i + 1, :] += jnp.sum(value, axis=0, keepdims=True)

    @pl.when((step >= units) & (step < units + blocks // 2))
    def _():
        tokens(True)

    @pl.when(step >= units + blocks // 2)
    def _():
        tokens(False)

    @pl.when(step == pl.num_programs(0) - 1)
    def _():
        grad_ref[:, 2 * D + 2 * HD :] = table_ref[...].T.astype(BF)


def feed_forward(normed, normed_t, grad_out, up, bias, down, part, more=None):
    tokens, width = normed.shape
    hidden = up.shape[1]
    units, blocks = hidden // BLK, tokens // BLK

    def whole(rows, columns):
        return pl.BlockSpec((rows, columns), lambda i: (0, 0))

    def block(first, last):
        return pl.BlockSpec((BLK, width), lambda i: (jnp.clip(i - units - first, 0, last - first), 0))

    every, own, other = block(0, blocks - 1), block(0, blocks // 2 - 1), block(blocks // 2, blocks - 1)
    in_specs = [
        whole(tokens, width),
        whole(width, tokens),
        whole(tokens, width),
        whole(width, hidden),
        whole(1, hidden),
        whole(hidden, width),
        every,
    ]
    rows = jax.ShapeDtypeStruct((tokens, width), F32)
    side = jax.ShapeDtypeStruct((tokens // 2, width), F32)
    scratch = [pltpu.VMEM((tokens, hidden), BF), pltpu.VMEM((tokens, hidden), BF)]
    if more is None:
        kernel, operands = ffn_first_kernel, ()
        shapes = (
            rows,
            rows,
            jax.ShapeDtypeStruct((width, 2 * width), BF),
            jax.ShapeDtypeStruct((1, hidden), F32),
        )
        out_specs = (every, every, whole(width, 2 * width), whole(1, hidden))
    else:
        kernel, operands = ffn_second_kernel, more
        in_specs += [
            every,
            every,
            every,
            own,
            whole(8, width),
            whole(16, width),
            whole(1, hidden),
            whole(width, 2 * HD),
        ]
        wide = 2 * width + 2 * HD + 128
        shapes = (side, side, side, side, jax.ShapeDtypeStruct((width, wide), BF))
        out_specs = (own, other, own, other, whole(width, wide))
        scratch.append(pltpu.VMEM((128, width), F32))
    return pl.pallas_call(
        kernel,
        out_shape=shapes,
        grid=(units + blocks,),
        in_specs=in_specs,
        out_specs=out_specs,
        scratch_shapes=scratch,
        compiler_params=pltpu.CompilerParams(
            dimension_semantics=("arbitrary",), vmem_limit_bytes=56 << 20
        ),
        cost_estimate=pl.CostEstimate(
            flops=12 * tokens * width * hidden,
            transcendentals=2 * tokens * hidden,
            bytes_accessed=8 * width * hidden + 20 * tokens * width,
        ),
        name="ffn",
    )(normed, normed_t, grad_out, up, bias, down, part, *operands)


def shards(
    tokens,
    segments,
    ln1_gain,
    ln1_bias,
    ln2_gain,
    ln2_bias,
    q_weight,
    q_bias,
    kv_weight,
    k_bias,
    out_weight,
    out_bias,
    up_weight,
    up_bias,
    down_weight,
    cotangent,
):
    core, chip = lax.axis_index("core"), lax.axis_index("chip")
    chips = lax.axis_size("rows") * lax.axis_size("chip")
    own = tokens.shape[1]
    both = 2 * own
    rows = q_weight.shape[0]
    hidden = up_bias.shape[0]
    half = hidden // 2
    back_chips = DOC // both
    own_tokens, own_grad = tokens[0], cotangent[0]

    def half_columns(array, which):
        return lax.dynamic_slice_in_dim(
            array, which * (array.shape[1] // 2), array.shape[1] // 2, 1
        )

    def first(which):
        return jnp.concatenate(
            [half_columns(q_weight, which), half_columns(out_weight, which), kv_weight], axis=1
        )

    up_blocks = up_weight.reshape(rows, chips, 2, 2, half)

    def up_half(which):
        block = lax.dynamic_index_in_dim(up_blocks, which, 2, keepdims=False)
        return block.transpose(0, 2, 1, 3).reshape(rows, FF // 2)

    flat = (ln1_gain, ln1_bias, ln2_gain, ln2_bias, q_bias, out_bias)
    if square_line():
        wide = 2 * HALF + 2 * HD
        line = jnp.concatenate(
            [vector.reshape(1, rows) for vector in flat] + [up_bias.reshape(hidden // rows, rows)]
        )
        line = jnp.pad(line, ((0, 16 - line.shape[0]), (0, wide - rows)))
        mine = jnp.concatenate([first(core), line], axis=0)
        theirs = jnp.concatenate([first(1 - core), line], axis=0)
        attn_line = jnp.concatenate(gather_line(by_core(core, mine, core_swap(theirs), 0)))
        attn_rows = gather_rows(attn_line)
        up_piece = by_core(core, up_half(core), core_swap(up_half(1 - core)), 0)
        ff_piece = jnp.concatenate([up_piece[:, :D], up_piece[:, D:], down_weight], axis=0)
        ff_line = gather_line(after(ff_piece, attn_line))
        other_tokens = core_swap(own_tokens)
        features = jnp.concatenate([own_tokens, other_tokens], axis=0)
        grad_out = jnp.concatenate([own_grad, core_swap(own_grad)], axis=0)
        attn_rows, ff_line, grad_out, features = lax.optimization_barrier(
            (attn_rows, ff_line, grad_out, features)
        )
        step = rows + 16
        weights, vectors = gather_place(
            attn_rows,
            (
                (0, rows, 0, 2 * rows, 0),
                (step, rows, 0, 2 * rows, rows),
                (rows, 16, 1, 32, 0),
                (step + rows, 16, 1, 32, 16),
            ),
            ((D, wide), (32 * chips, wide)),
        )
        vector_rows, hidden_bias = pl.pallas_call(
            vector_kernel,
            grid=(1,),
            in_specs=[pl.BlockSpec((32 * chips, 128), lambda i: (0, 0))],
            out_specs=(
                pl.BlockSpec((8, D), lambda i: (0, 0)),
                pl.BlockSpec((8, D), lambda i: (0, 0)),
            ),
            out_shape=(jax.ShapeDtypeStruct((8, D), F32), jax.ShapeDtypeStruct((8, D), F32)),
            name="vectors",
        )(vectors)
    else:
        weights = gather_whole(by_core(core, first(core), core_swap(first(1 - core)), 0))
        every = ("rows", "chip", "core")
        table = lax.all_gather(jnp.stack(flat), every, axis=1, tiled=True).astype(F32)
        vector_rows = jnp.pad(table, ((0, 2), (0, 0)))
        bias = gather_whole(up_bias).astype(F32).reshape(chips, 2, half)
        hidden_bias = jnp.pad(bias.transpose(1, 0, 2).reshape(2, D), ((0, 6), (0, 0)))

    if not square_line():
        other_tokens = core_swap(own_tokens)
        features = jnp.concatenate([own_tokens, other_tokens], axis=0)
        grad_out = jnp.concatenate([own_grad, core_swap(own_grad)], axis=0)

    ids = lax.broadcasted_iota(jnp.int32, (MAX_SEGS, 1), 0)
    doc_starts = jnp.sum((segments < ids).astype(jnp.int32), axis=1, keepdims=True)
    first_place, second_place = (chip * 2 + core) * own, (chip * 2 + 1 - core) * own
    span = lax.broadcasted_iota(jnp.int32, (1, own), 1)
    places = jnp.concatenate([first_place + span, second_place + span], axis=1)
    segs = jnp.concatenate(
        [
            lax.dynamic_slice(segments, (0, first_place), (1, own)),
            lax.dynamic_slice(segments, (0, second_place), (1, own)),
        ],
        axis=1,
    )
    starts = jnp.sum(jnp.where(segs == ids, doc_starts, 0), axis=0, keepdims=True)
    relative = places - starts
    frequency = 10000.0 ** (-(jnp.arange(ROT // 2, dtype=F32) * 2.0 / ROT))
    angles = relative.astype(F32) * frequency[:, None]
    cosine, sine = jnp.cos(angles), jnp.sin(angles)
    window_start = (chip - back_chips) * both
    pos = jnp.concatenate(
        [starts - window_start, places - window_start, jnp.zeros((6, both), jnp.int32)], axis=0
    )
    firsts, lasts = pos[:, ::BLK], pos[:, BLK - 1 :: BLK]
    scal = jnp.concatenate(
        [
            core.reshape(1),
            jnp.stack([firsts[0] // BLK, lasts[1] // BLK + 1, lasts[0]], axis=1).reshape(-1),
        ]
    ).astype(jnp.int32)


    normed_one, normed_two, normed_two_t, query_t, own_pairs, keep, send = front(
        own_tokens, other_tokens, weights, vector_rows, k_bias.astype(F32)[:, None], cosine, sine
    )
    got = core_swap(send)
    if square_line():
        ff_line = jnp.concatenate(ff_line)
    mine = jnp.concatenate(
        [chip_shift(own_pairs, k, False) for k in range(back_chips, 0, -1)] + [own_pairs], axis=0
    )
    theirs = core_swap(mine)

    if square_line():
        ff_rows = gather_rows(after(ff_line, attn_rows))

    out_t, grad_query_t, pair_mine, pair_theirs = attention(
        scal, query_t, grad_out, keep, got, pos, cosine, sine, mine, theirs
    )
    if square_line():
        (out_t, grad_query_t, pair_mine, pair_theirs), ff_rows = lax.optimization_barrier(
            ((out_t, grad_query_t, pair_mine, pair_theirs), ff_rows)
        )
    part, grad_one, grad_query, proj_keep, proj_send, sums = after_heads(
        out_t, grad_query_t, normed_one, grad_out, weights[:, :HALF], keep, got
    )
    pair_got = core_swap(pair_theirs)
    if square_line():
        part, grad_one, grad_query, proj_keep, proj_send, sums = after(
            (part, grad_one, grad_query, proj_keep, proj_send, sums), pair_got
        )
    grad_proj = by_core(core, proj_keep, core_swap(proj_send), 0)
    attn_terms = jnp.concatenate([grad_query, grad_proj], axis=1)

    pair_sum = (pair_mine + pair_got).reshape(back_chips + 1, own, 2 * HD)
    arrived = [
        chip_shift(pair_sum[back_chips - k].astype(BF), -k, False) for k in range(1, back_chips + 1)
    ]
    pair_weight = weights[:, 2 * HALF : 2 * HALF + 2 * HD]
    grad_pair, grad_one_pair, key_bias = after_pairs(
        pair_sum[back_chips], *arrived, normed_one, pair_weight, cosine, sine
    )

    if square_line():
        ups_downs = gather_place(
            ff_rows,
            tuple((i * 2 * rows, 2 * rows, i, 2 * rows, 0) for i in range(4)),
            ((D, D),) * 4,
        )
    else:
        up_whole = gather_whole(by_core(core, up_half(core), core_swap(up_half(1 - core)), 0))
        down_whole = gather_whole(down_weight).reshape(chips, 2, half, D)
        down_whole = down_whole.transpose(1, 0, 2, 3).reshape(2, D, D)
        ups_downs = (up_whole[:, :D], up_whole[:, D:], down_whole[0], down_whole[1])
    first = (normed_two, normed_two_t, grad_out, ups_downs[0], hidden_bias[0:1], ups_downs[2])
    second = (normed_two, normed_two_t, grad_out, ups_downs[1], hidden_bias[1:2], ups_downs[3])
    if square_line():
        attn_planes, attn_one = reduce_first(attn_terms)
    part, dh, terms0, gbias = feed_forward(*first, part)
    if square_line():
        part, dh, terms0, gbias = after((part, dh, terms0, gbias), attn_one, arrived)
        attn_two = reduce_second(attn_planes, attn_one)
        planes0, one0 = reduce_first(terms0)
    more = (dh, features, grad_one, grad_one_pair, vector_rows, sums, gbias, grad_pair)
    second_out = feed_forward(*second, part, more)
    if square_line():
        second_out = after(second_out, attn_two, one0)
    part, part_send, scaled, scaled_send, terms1 = second_out
    part_got, scaled_got = core_swap(part_send), core_swap(scaled_send)

    def finish(part_got, scaled_got):
        layer_out = own_tokens.astype(F32) + part + part_got + vector_rows[5:6]
        total = scaled + scaled_got
        unit, spread = standard(own_tokens)
        input_grad = own_grad.astype(F32) + spread * (
            total
            - jnp.mean(total, axis=-1, keepdims=True)
            - unit * jnp.mean(total * unit, axis=-1, keepdims=True)
        )
        return layer_out.astype(BF), input_grad

    def split(value):
        return (
            lax.dynamic_slice_in_dim(value, core * rows, rows, 0),
            core_swap(lax.dynamic_slice_in_dim(value, (1 - core) * rows, rows, 0)),
        )

    if square_line():
        two0 = reduce_second(planes0, one0)
        planes1, one1 = reduce_first(terms1)
        attn_own, attn_three = reduce_third(attn_planes, attn_two)
        one1, part_got, scaled_got, attn_three = lax.optimization_barrier(
            (one1, part_got, scaled_got, attn_three)
        )
        two1 = reduce_second(planes1, one1)
        own0, three0 = reduce_third(planes0, two0)
        layer_out, input_grad = finish(part_got, scaled_got)
        attn_sum = reduce_last(attn_own, attn_three)
        mine, theirs = split(attn_sum)
        two1, layer_out, input_grad, three0, theirs = lax.optimization_barrier(
            (two1, layer_out, input_grad, three0, theirs)
        )
        own1, three1 = reduce_third(planes1, two1)
        sum0 = reduce_last(own0, three0)
        up_first = split(sum0[:, :D])
        query_out = by_core(core, mine[:, :HALF], theirs[:, :HALF], 1)
        proj_out = by_core(core, mine[:, HALF:], theirs[:, HALF:], 1)
        key_bias_out = sum_everywhere(key_bias[0, :HD])
        own1 = after(own1, query_out, proj_out, up_first, key_bias_out)
        sum1 = reduce_last(own1, three1)
    else:
        layer_out, input_grad = finish(part_got, scaled_got)
        sum0, sum1 = reduce_whole(terms0), reduce_whole(terms1)
        mine, theirs = split(reduce_whole(attn_terms))
        query_out = by_core(core, mine[:, :HALF], theirs[:, :HALF], 1)
        proj_out = by_core(core, mine[:, HALF:], theirs[:, HALF:], 1)
        up_first = split(sum0[:, :D])
        key_bias_out = sum_everywhere(key_bias[0, :HD])
    mine, theirs = split(jnp.concatenate([sum1[:, :D], sum1[:, 2 * D :]], axis=1))
    up_second = (mine[:, :D], theirs[:, :D])
    rest = mine[:, D:] + theirs[:, D:]
    pair_out, vector_out = rest[:, : 2 * HD], rest[:, 2 * HD :]
    up_bias_out = sum1[:, 2 * D + 2 * HD + 6 : 2 * D + 2 * HD + 8].T.reshape(hidden)

    def blocks(first_half, second_half):
        return jnp.stack(
            [value.reshape(rows, chips, half) for value in (first_half, second_half)], axis=2
        ).reshape(rows, chips, 1, hidden)

    mine, theirs = blocks(up_first[0], up_second[0]), blocks(up_first[1], up_second[1])
    up_out = by_core(core, mine, theirs, 2).reshape(rows, FF)
    down_out = jnp.concatenate([sum0[:, D:], sum1[:, D : 2 * D]], axis=0)
    return (
        layer_out[None],
        input_grad[None],
        vector_out[:, 0],
        vector_out[:, 1],
        vector_out[:, 2],
        vector_out[:, 3],
        query_out,
        vector_out[:, 4],
        pair_out,
        key_bias_out,
        proj_out,
        vector_out[:, 5],
        up_out,
        up_bias_out,
        down_out,
    )


def solution(mesh):
    devices = mesh.devices.reshape(mesh.shape["rows"], mesh.shape["wide"] // 2, 2)
    every, wide = ("rows", "chip", "core"), ("chip", "core")
    matrix, vector, sequence = P(every, None), P(every), P("rows", wide, None)
    return jax.shard_map(
        shards,
        mesh=Mesh(devices, every),
        in_specs=(
            sequence,
            P("rows", None),
            vector,
            vector,
            vector,
            vector,
            matrix,
            vector,
            matrix,
            P(),
            matrix,
            vector,
            matrix,
            vector,
            matrix,
            sequence,
        ),
        out_specs=(
            sequence,
            sequence,
            vector,
            vector,
            vector,
            vector,
            matrix,
            vector,
            matrix,
            P(),
            matrix,
            vector,
            matrix,
            vector,
            matrix,
        ),
        check_vma=False,
    )
```

```python
import functools
import math

import jax
import jax.numpy as jnp
from jax import lax
from jax.experimental import pallas as pl
from jax.experimental.pallas import tpu as pltpu
from jax.sharding import Mesh, PartitionSpec as P

D = 768
HEADS = 12
HD = 64
ROT = 16
DOC = 2048
FF = 3072
MAX_SEGS = 32
norm_eps = 1e-05
BF = jnp.bfloat16
F32 = jnp.float32
HALF = HEADS // 2 * HD
BLK = 256
GROUP = 6


def dot(left, right, dims):
    return lax.dot_general(left, right, (dims, ((), ())), preferred_element_type=F32)


def core_swap(value):
    return lax.ppermute(value, "core", [(0, 1), (1, 0)])


def rows_swap(value, bit):
    return lax.ppermute(value, "rows", [(r, r ^ bit) for r in range(4)])


def chip_shift(value, by, wrap):
    count = lax.axis_size("chip")
    pairs = [(s, (s + by) % count) for s in range(count) if wrap or 0 <= s + by < count]
    return lax.ppermute(value, "chip", pairs)


def square_line():
    return lax.axis_size("rows") == 4 and lax.axis_size("chip") == 4


def place_copies(parts, sources, outs, sems):
    row, chip = lax.axis_index("rows"), lax.axis_index("chip")
    size = sources[0].shape[0] // 4
    copies = []
    for first, count, out in parts:
        for turn, source in enumerate(sources):
            for step in range(4):
                place = (row ^ turn) * 4 + lax.rem(chip + step, 4)
                copies.append(
                    pltpu.make_async_copy(
                        source.at[pl.ds(step * size + first, count)],
                        outs[out].at[pl.ds(pl.multiple_of(place * count, 8), count)],
                        sems.at[len(copies)],
                    )
                )
    return copies


def gather_line(piece):
    return [piece] + [chip_shift(piece, -k, True) for k in (1, 2, 3)]


def gather_rows(lines):
    return lines, rows_swap(lines, 1), rows_swap(lines, 2), rows_swap(lines, 3)


def gather_whole(piece):
    return lax.all_gather(piece, ("rows", "chip"), axis=0, tiled=True)


def reduce_first(terms):
    row = lax.axis_index("rows")
    grid = terms.reshape((4, 4, terms.shape[0] // 16) + terms.shape[1:])
    planes = [lax.dynamic_index_in_dim(grid, row ^ bit, 0, keepdims=False) for bit in range(4)]
    return planes, (rows_swap(planes[3][:2], 1), rows_swap(planes[3][2:], 2))


def reduce_rows(terms):
    row = lax.axis_index("rows")
    grid = terms.reshape((4, 4, terms.shape[0] // 16) + terms.shape[1:])
    planes = [lax.dynamic_index_in_dim(grid, row ^ bit, 0, keepdims=False) for bit in range(4)]
    return planes[0], [rows_swap(planes[bit], bit) for bit in (3, 1, 2)]


def reduce_second(planes, arrived):
    _, flat, cross, _ = planes
    from_flat, from_cross = arrived
    to_flat = jnp.concatenate(
        [flat[:2], (flat[2:].astype(F32) + from_cross.astype(F32)).astype(BF)], axis=0
    )
    to_cross = jnp.concatenate(
        [(cross[:2].astype(F32) + from_flat.astype(F32)).astype(BF), cross[2:]], axis=0
    )
    return rows_swap(to_flat, 1), rows_swap(to_cross, 2)


def reduce_third(own, arrived):
    chip = lax.axis_index("chip")

    def line(step):
        spot = lax.rem(chip + step, 4)
        pick = [
            lax.dynamic_index_in_dim(part, spot, 0, keepdims=False).astype(F32)
            for part in (own, *arrived)
        ]
        return sum(pick[1:], pick[0])

    return line(0), [chip_shift(line(step).astype(BF), step, True) for step in (1, 2, 3)]


def reduce_last(own, arrived):
    return own + arrived[0].astype(F32) + arrived[1].astype(F32) + arrived[2].astype(F32)


def reduce_whole(terms):
    return lax.psum_scatter(terms.astype(F32), ("rows", "chip"), scatter_dimension=0, tiled=True)


def after(value, *others):
    return lax.optimization_barrier((value, others))[0]


def line_swap(value, bit):
    return lax.ppermute(value, "chip", [(s, s ^ bit) for s in range(4)])


def by_core(core, own, other, axis):
    return jnp.where(
        core == 0,
        jnp.concatenate([own, other], axis=axis),
        jnp.concatenate([other, own], axis=axis),
    )


def pack_kernel(q_ref, out_ref, kv_ref, vectors_ref, mine_ref, theirs_ref):
    core = lax.axis_index("core")
    rows = q_ref.shape[0]
    pick = lax.broadcasted_iota(jnp.int32, (16, 128), 0) == lax.broadcasted_iota(
        jnp.int32, (16, 128), 1
    )
    columns = dot(vectors_ref[...], jnp.where(pick, 1.0, 0.0).astype(BF), ((0,), (0,))).astype(BF)
    for which, ref in ((core, mine_ref), (1 - core, theirs_ref)):
        spot = pl.ds(pl.multiple_of(which * HALF, HALF), HALF)
        ref[:, :HALF] = q_ref[:, spot]
        ref[:, HALF : 2 * HALF] = out_ref[:, spot]
        ref[:, 2 * HALF : 2 * HALF + 2 * HD] = kv_ref[...]
        ref[:, 2 * HALF + 2 * HD :] = columns


def pack(q_weight, out_weight, kv_weight, vectors):
    rows = q_weight.shape[0]
    side = jax.ShapeDtypeStruct((rows, 2 * HALF + 2 * HD + 128), BF)
    return pl.pallas_call(
        pack_kernel,
        out_shape=(side, side),
        cost_estimate=pl.CostEstimate(flops=0, transcendentals=0, bytes_accessed=8 * rows * D),
        name="pack",
    )(q_weight, out_weight, kv_weight, vectors)


def turn(values, cosine, sine, direction):
    half = ROT // 2
    a, b = values[:half, :], values[half:ROT, :]
    return jnp.concatenate(
        [a * cosine - direction * b * sine, b * cosine + direction * a * sine, values[ROT:, :]],
        axis=0,
    )


def standard(tokens):
    values = tokens.astype(F32)
    center = values - jnp.mean(values, axis=-1, keepdims=True)
    spread = lax.rsqrt(jnp.mean(center * center, axis=-1, keepdims=True) + norm_eps)
    return center * spread, spread


def front_rest(
    own_ref, other_ref, kbias_ref, cos_ref, sin_ref, w_ref, rows_ref,
    h1_ref, h2_ref, h2t_ref, q_ref, pairs_ref, keep_ref, send_ref,
):
    core = lax.axis_index("core")
    count = own_ref.shape[0]
    gain_one, shift_one, gain_two, shift_two = (rows_ref[i : i + 1, :] for i in range(4))

    def norm(part, ref):
        unit, _ = standard(ref[...])
        spot = pl.ds(part * count, count)
        h1_ref[spot, :] = (unit * gain_one + shift_one).astype(BF)
        normed = (unit * gain_two + shift_two).astype(BF)
        h2_ref[spot, :] = normed
        h2t_ref[:, part * count : (part + 1) * count] = normed.T

    norm(0, own_ref)
    pair = dot(w_ref[:, 2 * HALF : 2 * HALF + 2 * HD], h1_ref[:count, :], ((0,), (1,)))
    key = turn(
        pair[:HD] + kbias_ref[...], cos_ref[:, :count], sin_ref[:, :count], 1.0
    ).astype(BF)
    pairs_ref[...] = jnp.concatenate([key, pair[HD:].astype(BF)], axis=0).T
    norm(1, other_ref)
    query = dot(w_ref[:, :HALF], h1_ref[...], ((0,), (1,)))
    bias = jnp.where(core == 0, rows_ref[4:5, :HALF], rows_ref[4:5, HALF:])
    query = query + jnp.broadcast_to(bias, (8, HALF)).T[:, :1]
    for h in range(HEADS // 2):
        q_ref[h * HD : (h + 1) * HD, :] = turn(
            query[h * HD : (h + 1) * HD, :], cos_ref[...], sin_ref[...], 1.0
        ).astype(BF)
    for index, ref in ((core, keep_ref), (1 - core, send_ref)):
        spot = pl.ds(pl.multiple_of(index * HALF, HALF), HALF)
        ref[...] = w_ref[spot, HALF : 2 * HALF]


def front_kernel(
    lines_ref, flat_ref, cross_ref, far_ref, own_ref, other_ref, kbias_ref, cos_ref, sin_ref,
    w_ref, rows_ref, bias_ref, h1_ref, h2_ref, h2t_ref, q_ref, pairs_ref, keep_ref, send_ref, sems,
):
    core = lax.axis_index("core")
    copies = place_copies(
        ((0, w_ref.shape[0] // 16, 0),), (lines_ref, flat_ref, cross_ref, far_ref), (w_ref,), sems
    )
    for copy in copies:
        copy.start()
    for copy in copies:
        copy.wait()
    table = w_ref[:, 2 * HALF + 2 * HD :].astype(F32).T
    rows_ref[...] = table[:8, :]
    half = lax.rem(lax.broadcasted_iota(jnp.int32, (1, D), 1), 48) // 24
    for k in range(2):
        low, high = table[6 + 2 * k : 7 + 2 * k, :], table[7 + 2 * k : 8 + 2 * k, :]
        first = jnp.where(half == 0, low, pltpu.roll(jnp.broadcast_to(high, (8, D)), 24, 1)[:1])
        second = jnp.where(
            half == 1, high, pltpu.roll(jnp.broadcast_to(low, (8, D)), D - 24, 1)[:1]
        )
        bias_ref[k : k + 1, :] = jnp.where(core == 0, first, second)
    bias_ref[2:8, :] = jnp.zeros((6, D), F32)
    front_rest(
        own_ref, other_ref, kbias_ref, cos_ref, sin_ref, w_ref, rows_ref,
        h1_ref, h2_ref, h2t_ref, q_ref, pairs_ref, keep_ref, send_ref,
    )


def front_plain_kernel(
    w_ref, rows_ref, own_ref, other_ref, kbias_ref, cos_ref, sin_ref, *outs
):
    front_rest(own_ref, other_ref, kbias_ref, cos_ref, sin_ref, w_ref, rows_ref, *outs)


def front(pieces, own, other, k_bias, cosine, sine):
    both = 2 * own.shape[0]
    placed = len(pieces) == 4
    wide = pieces[0].shape[1]
    shapes = (
        jax.ShapeDtypeStruct((both, D), BF),
        jax.ShapeDtypeStruct((both, D), BF),
        jax.ShapeDtypeStruct((D, both), BF),
        jax.ShapeDtypeStruct((HALF, both), BF),
        jax.ShapeDtypeStruct((own.shape[0], 2 * HD), BF),
        jax.ShapeDtypeStruct((HALF, HALF), BF),
        jax.ShapeDtypeStruct((HALF, HALF), BF),
    )
    here = pl.BlockSpec(memory_space=pltpu.VMEM)
    if placed:
        shapes = (
            jax.ShapeDtypeStruct((D, wide), BF),
            jax.ShapeDtypeStruct((8, D), F32),
            jax.ShapeDtypeStruct((8, D), F32),
        ) + shapes
    return pl.pallas_call(
        front_kernel if placed else front_plain_kernel,
        out_shape=shapes,
        in_specs=[pl.BlockSpec(memory_space=pl.ANY) if placed else here] * len(pieces) + [here] * 5,
        out_specs=tuple(here for _ in shapes),
        scratch_shapes=[pltpu.SemaphoreType.DMA((16,))] if placed else [],
        compiler_params=pltpu.CompilerParams(vmem_limit_bytes=48 << 20),
        cost_estimate=pl.CostEstimate(
            flops=2 * both * D * (HALF + 2 * HD), transcendentals=both, bytes_accessed=8 * both * D
        ),
        name="front",
    )(*pieces, own, other, k_bias, cosine, sine)


def attn_kernel(
    scal_ref, q_ref, grad_ref, keep_in_ref, got_in_ref, pos_ref, cos_ref, sin_ref, mine_ref, theirs_ref,
    o_ref, dq_ref, dmine_ref, dtheirs_ref,
    keep_ref, got_ref, kv_ref, kvt_ref, dkv_ref, g_ref, s_ref, r_ref, rt_ref, sems,
):
    block = pl.program_id(0)
    core = scal_ref[0]
    low, high, edge = (scal_ref[1 + 3 * block + i] for i in range(3))
    wide = GROUP * BLK
    half = kv_ref.shape[0] // 2
    own_blocks = pl.num_programs(0) // 2

    @pl.when(block == 0)
    def _():
        dkv_ref[...] = jnp.zeros_like(dkv_ref)
        copies = [
            pltpu.make_async_copy(source, target, sems.at[i])
            for i, (source, target) in enumerate(
                (
                    (mine_ref, kv_ref.at[pl.ds(0, half)]),
                    (theirs_ref, kv_ref.at[pl.ds(half, half)]),
                    (keep_in_ref, keep_ref),
                    (got_in_ref, got_ref),
                )
            )
        ]
        for copy in copies:
            copy.start()
        for copy in copies:
            copy.wait()
        for part in range(2):
            kvt_ref[: 2 * HD, part * half : (part + 1) * half] = kv_ref[
                part * half : (part + 1) * half, :
            ].T
        kvt_ref[2 * HD :, :] = jnp.ones((16, 2 * half), BF)

    def spot(key_block):
        side = lax.rem(key_block // own_blocks, 2) ^ core
        place = (key_block // (2 * own_blocks)) * own_blocks + lax.rem(key_block, own_blocks)
        return pl.multiple_of(side * half + place * BLK, BLK)

    first, pairs_end, single = low // 2, high // 2, lax.rem(high, 2)
    last = pairs_end - 1 + single
    clear = jnp.clip((edge + 2 * BLK - 1) // (2 * BLK), first, last)

    def slot(key_block, size):
        return pl.ds(pl.multiple_of((key_block - 2 * first) * BLK, BLK), size)

    def over_keys(body, carry):
        def double(masked):
            return lambda i, c: body(masked, 2 * i, 2 * BLK, c)

        carry = lax.fori_loop(first, clear, double(True), carry)
        carry = lax.fori_loop(clear, last, double(False), carry)
        carry = lax.fori_loop(last, pairs_end, double(True), carry)
        return lax.fori_loop(
            0, single, lambda i, c: body(True, 2 * pairs_end + i, BLK, c), carry
        )

    def over_all(body, carry):
        carry = lax.fori_loop(first, pairs_end, lambda i, c: body(2 * i, 2 * BLK, c), carry)
        return lax.fori_loop(0, single, lambda i, c: body(2 * pairs_end + i, BLK, c), carry)

    near = pl.ds(pl.multiple_of(core * HALF, HALF), HALF)
    away = pl.ds(pl.multiple_of((1 - core) * HALF, HALF), HALF)
    g_ref[...] = (
        dot(keep_ref[...], grad_ref[:, near], ((1,), (1,)))
        + dot(got_ref[...], grad_ref[:, away], ((1,), (1,)))
    ).astype(BF)
    starts = jnp.concatenate([pos_ref[0:1, :]] * GROUP, axis=1)
    places = jnp.concatenate([pos_ref[1:2, :]] * GROUP, axis=1)
    blank = jnp.zeros((HD, BLK), BF)
    for h in range(GROUP):
        query = (q_ref[h * HD : (h + 1) * HD, :].astype(F32) * HD**-0.5).astype(BF)
        grad = g_ref[h * HD : (h + 1) * HD, :]
        query = jnp.concatenate([query, blank], axis=0)
        grad = jnp.concatenate([blank, grad], axis=0)
        r_ref[0, :, h * BLK : (h + 1) * BLK] = query
        r_ref[1, :, h * BLK : (h + 1) * BLK] = grad
        rt_ref[h * BLK : (h + 1) * BLK, :] = query.T
        rt_ref[(GROUP + h) * BLK : (GROUP + h + 1) * BLK, :] = grad.T

    def scores(masked, key_block, size, peak):
        keys = kv_ref[pl.ds(spot(key_block), size), :]
        s = dot(keys, r_ref[0], ((1,), (0,)))
        if masked:
            key_places = key_block * BLK + lax.broadcasted_iota(jnp.int32, (size, wide), 0)
            s = jnp.where((key_places >= starts) & (key_places <= places), s, -1e30)
        s_ref[slot(key_block, size), :] = s
        return jnp.maximum(peak, jnp.max(s, axis=0, keepdims=True))

    peak = over_keys(scores, jnp.full((1, wide), -1e30, F32))

    def expo(key_block, size, out):
        values = kvt_ref[HD:, pl.ds(spot(key_block), size)]
        e = jnp.exp(s_ref[slot(key_block, size), :] - peak)
        s_ref[slot(key_block, size), :] = e
        return out + dot(values, e.astype(BF), ((1,), (0,)))

    out = over_all(expo, jnp.zeros((HD + 16, wide), F32))
    inverse = 1.0 / out[HD : HD + 1, :]
    out = out[:HD] * inverse
    deltas = []
    for h in range(GROUP):
        part = out[:, h * BLK : (h + 1) * BLK]
        o_ref[h * HD : (h + 1) * HD, :] = part.astype(BF)
        deltas.append(
            jnp.sum(part * g_ref[h * HD : (h + 1) * HD, :].astype(F32), axis=0, keepdims=True)
        )
    delta = jnp.concatenate(deltas, axis=1)

    def back(key_block, size, dq):
        where = spot(key_block)
        pairs = kv_ref[pl.ds(where, size), :]
        keys = kvt_ref[:HD, pl.ds(where, size)]
        p = s_ref[slot(key_block, size), :] * inverse
        dp = dot(pairs, r_ref[1], ((1,), (0,)))
        ds = (p * (dp - delta)).astype(BF)
        left = jnp.concatenate([ds, p.astype(BF)], axis=1)
        dkv_ref[pl.ds(where, size), :] += dot(left, rt_ref[...], ((1,), (0,)))
        return dq + dot(keys, ds, ((1,), (0,)))

    dq = over_all(back, jnp.zeros((HD, wide), F32)) * HD**-0.5
    for h in range(GROUP):
        part = dq[:, h * BLK : (h + 1) * BLK].astype(BF).astype(F32)
        dq_ref[h * HD : (h + 1) * HD, :] = turn(part, cos_ref[...], sin_ref[...], -1.0).astype(BF)

    @pl.when(block == pl.num_programs(0) - 1)
    def _():
        dmine_ref[...] = dkv_ref[:half, :]
        dtheirs_ref[...] = dkv_ref[half:, :]


def attention(scal, query_t, grad_out, keep, got, pos, cosine, sine, mine, theirs):
    features, tokens = query_t.shape
    blocks, half = tokens // BLK, mine.shape[0]
    tile = pl.BlockSpec((features, BLK), lambda b, s: (0, b))
    small = pl.BlockSpec((8, BLK), lambda b, s: (0, b))

    def whole(rows, columns):
        return pl.BlockSpec((rows, columns), lambda b, s: (0, 0))

    return pl.pallas_call(
        attn_kernel,
        out_shape=(
            jax.ShapeDtypeStruct((features, tokens), BF),
            jax.ShapeDtypeStruct((features, tokens), BF),
            jax.ShapeDtypeStruct((half, 2 * HD), F32),
            jax.ShapeDtypeStruct((half, 2 * HD), F32),
        ),
        grid_spec=pltpu.PrefetchScalarGridSpec(
            num_scalar_prefetch=1,
            grid=(blocks,),
            in_specs=[
                tile,
                pl.BlockSpec((BLK, D), lambda b, s: (b, 0)),
                pl.BlockSpec(memory_space=pltpu.HBM),
                pl.BlockSpec(memory_space=pltpu.HBM),
                small,
                small,
                small,
                pl.BlockSpec(memory_space=pltpu.HBM),
                pl.BlockSpec(memory_space=pltpu.HBM),
            ],
            out_specs=(tile, tile, whole(half, 2 * HD), whole(half, 2 * HD)),
            scratch_shapes=[
                pltpu.VMEM((HALF, HALF), BF),
                pltpu.VMEM((HALF, HALF), BF),
                pltpu.VMEM((2 * half, 2 * HD), BF),
                pltpu.VMEM((2 * HD + 16, 2 * half), BF),
                pltpu.VMEM((2 * half, 2 * HD), F32),
                pltpu.VMEM((features, BLK), BF),
                pltpu.VMEM((DOC + 2 * BLK, GROUP * BLK), F32),
                pltpu.VMEM((2, 2 * HD, GROUP * BLK), BF),
                pltpu.VMEM((2 * GROUP * BLK, 2 * HD), BF),
                pltpu.SemaphoreType.DMA((4,)),
            ],
        ),
        compiler_params=pltpu.CompilerParams(
            dimension_semantics=("arbitrary",), vmem_limit_bytes=48 << 20
        ),
        cost_estimate=pl.CostEstimate(
            flops=12 * features * tokens * DOC * 3 // 4,
            transcendentals=features // HD * tokens * DOC * 3 // 4,
            bytes_accessed=8 * features * tokens,
        ),
        name="attention",
    )(scal, query_t, grad_out, keep, got, pos, cosine, sine, mine, theirs)


def heads_kernel(
    o_ref, dq_ref, h1_ref, grad_ref, gq_ref, keep_out_ref, send_out_ref, sums_ref
):
    core = lax.axis_index("core")
    near = pl.ds(pl.multiple_of(core * HALF, HALF), HALF)
    away = pl.ds(pl.multiple_of((1 - core) * HALF, HALF), HALF)
    send_out_ref[...] = dot(o_ref[...], grad_ref[:, away], ((1,), (0,))).astype(BF)
    keep_out_ref[...] = dot(o_ref[...], grad_ref[:, near], ((1,), (0,))).astype(BF)
    gq_ref[...] = dot(dq_ref[...], h1_ref[...], ((1,), (0,))).T.astype(BF)
    ones = jnp.ones((8, dq_ref.shape[1]), BF)
    sums_ref[...] = jnp.zeros_like(sums_ref)
    sums_ref[0:8, near] = dot(ones, dq_ref[...], ((1,), (1,)))
    count = grad_ref.shape[0] // 2
    sums_ref[8:16, :] = dot(ones[:, :count], grad_ref[:count, :], ((1,), (0,)))


def after_heads(out_t, dq_t, normed, grad_out):
    both = normed.shape[0]
    return pl.pallas_call(
        heads_kernel,
        out_shape=(
            jax.ShapeDtypeStruct((D, HALF), BF),
            jax.ShapeDtypeStruct((HALF, HALF), BF),
            jax.ShapeDtypeStruct((HALF, HALF), BF),
            jax.ShapeDtypeStruct((16, D), F32),
        ),
        compiler_params=pltpu.CompilerParams(vmem_limit_bytes=48 << 20),
        cost_estimate=pl.CostEstimate(
            flops=4 * both * D * HALF, transcendentals=0, bytes_accessed=6 * both * D
        ),
        name="after_heads",
    )(out_t, dq_t, normed, grad_out)


def pairs_kernel(
    own_ref, near_ref, far_ref, h1_ref, w_ref, cos_ref, sin_ref, gw_ref, dh_ref, gbias_ref
):
    total = own_ref[...] + near_ref[...].astype(F32) + far_ref[...].astype(F32)
    total = total.astype(BF).astype(F32).T
    key = turn(total[:HD], cos_ref[...], sin_ref[...], -1.0)
    grad = jnp.concatenate([key, total[HD:]], axis=0).astype(BF)
    gw_ref[...] = dot(grad, h1_ref[...], ((1,), (0,))).T.astype(BF)
    dh_ref[...] = dot(grad.T, w_ref[:, 2 * HALF : 2 * HALF + 2 * HD], ((1,), (1,)))
    ones = jnp.ones((8, grad.shape[1]), BF)
    gbias_ref[...] = dot(ones, grad, ((1,), (1,)))


def after_pairs(pairs, near, far, normed, weights, cosine, sine):
    count = near.shape[0]

    def whole(rows, columns):
        return pl.BlockSpec((rows, columns), lambda i: (0, 0))

    return pl.pallas_call(
        pairs_kernel,
        out_shape=(
            jax.ShapeDtypeStruct((D, 2 * HD), BF),
            jax.ShapeDtypeStruct((count, D), F32),
            jax.ShapeDtypeStruct((8, 2 * HD), F32),
        ),
        grid=(1,),
        in_specs=[
            pl.BlockSpec((count, 2 * HD), lambda i: (pairs.shape[0] // count - 1, 0)),
            whole(count, 2 * HD),
            whole(count, 2 * HD),
            whole(count, D),
            whole(D, weights.shape[1]),
            whole(8, count),
            whole(8, count),
        ],
        out_specs=(whole(D, 2 * HD), whole(count, D), whole(8, 2 * HD)),
        compiler_params=pltpu.CompilerParams(vmem_limit_bytes=32 << 20),
        cost_estimate=pl.CostEstimate(
            flops=8 * count * D * HD, transcendentals=0, bytes_accessed=8 * count * D
        ),
        name="after_pairs",
    )(pairs, near, far, normed, weights, cosine, sine)


def ffn_units(
    placed, h_ref, ht_ref, g_ref, bias_ref, up_ref, down_ref, grad_ref, act_ref, dz_ref
):
    for copy in placed:
        copy.start()
    for copy in placed[: len(placed) // 2]:
        copy.wait()
    z = dot(h_ref[...], up_ref[...], ((1,), (0,))) + bias_ref[...]
    below = 0.5 * (1.0 + lax.erf(z * 0.5**0.5))
    slope = below + z * (jnp.exp(-0.5 * z * z) * (0.5 / math.pi) ** 0.5)
    act = (z * below).astype(BF)
    grad_ref[:, D : 2 * D] = dot(act, g_ref[...], ((0,), (0,))).astype(BF)
    act_ref[...] = act
    for copy in placed[len(placed) // 2 :]:
        copy.wait()
    grad = (dot(g_ref[...], down_ref[...], ((1,), (1,))) * slope).astype(BF)
    dz_ref[...] = grad
    grad_ref[:, :D] = dot(ht_ref[...], grad, ((1,), (0,))).astype(BF)
    return jnp.sum(grad.astype(F32), axis=0, keepdims=True)


def ffn_weights(parts, rest):
    if parts is None:
        return (), rest[0], rest[1], rest[2:]
    up_ref, down_ref, sems = rest[-3:]
    return place_copies(parts, rest[:4], (up_ref, down_ref), sems), up_ref, down_ref, rest[4:-3]


def ffn_first_kernel(parts, h_ref, ht_ref, g_ref, bias_ref, *rest):
    placed, up_ref, down_ref, rest = ffn_weights(parts, rest)
    out_ref, dh_ref, grad_ref, gbias_ref, act_ref, dz_ref = rest
    step = pl.program_id(0)

    @pl.when(step == 0)
    def _():
        gbias_ref[...] = ffn_units(
            placed, h_ref, ht_ref, g_ref, bias_ref, up_ref, down_ref, grad_ref, act_ref, dz_ref
        )

    @pl.when(step > 0)
    def _():
        spot = pl.ds(pl.multiple_of((step - 1) * BLK, BLK), BLK)
        out_ref[...] = dot(act_ref[spot, :], down_ref[...], ((1,), (0,)))
        dh_ref[...] = dot(dz_ref[spot, :], up_ref[...], ((1,), (1,)))


def ffn_second_kernel(parts, h_ref, ht_ref, g_ref, bias_ref, *rest):
    placed, up_ref, down_ref, rest = ffn_weights(parts, rest)
    (
        mlp_ref, dh_in_ref, x_ref, o_ref, dq_ref, w_ref, out_keep_ref, out_got_ref,
        pair_ref, rows_ref, sums_ref, bias0_ref, gpair_ref,
        keep_ref, send_ref, tkeep_ref, tsend_ref, grad_ref,
        act_ref, dz_ref, table_ref,
    ) = rest
    step = pl.program_id(0)
    core = lax.axis_index("core")
    blocks = pl.num_programs(0) - 1

    @pl.when(step == 0)
    def _():
        table_ref[...] = jnp.zeros_like(table_ref)
        table_ref[4:5, :] = sums_ref[0:1, :]
        table_ref[5:6, :] = sums_ref[8:9, :]
        table_ref[6:7, :] = bias0_ref[...]
        grad_ref[:, 2 * D : 2 * D + 2 * HD] = gpair_ref[...]
        table_ref[7:8, :] = ffn_units(
            placed, h_ref, ht_ref, g_ref, bias_ref, up_ref, down_ref, grad_ref, act_ref, dz_ref
        )

    def tokens(first):
        spot = pl.ds(pl.multiple_of((step - 1) * BLK, BLK), BLK)
        heads = o_ref[...].T
        near = dot(heads, out_keep_ref[...], ((1,), (0,)))
        away = dot(heads, out_got_ref[...], ((1,), (0,)))
        low, high = jnp.where(core == 0, near, away), jnp.where(core == 0, away, near)
        out = mlp_ref[...] + dot(act_ref[spot, :], down_ref[...], ((1,), (0,)))
        out = out + jnp.concatenate([low, high], axis=1)
        two = dh_in_ref[...] + dot(dz_ref[spot, :], up_ref[...], ((1,), (1,)))
        one = dot(dq_ref[...].T, w_ref[:, :HALF], ((1,), (1,)))
        if first:
            one = one + pair_ref[...]
        unit, _ = standard(x_ref[...])
        scaled = one * rows_ref[0:1, :] + two * rows_ref[2:3, :]
        refs = (keep_ref, tkeep_ref) if first else (send_ref, tsend_ref)
        refs[0][...], refs[1][...] = out, scaled
        for i, value in enumerate((one * unit, one, two * unit, two)):
            table_ref[i : i + 1, :] += jnp.sum(value, axis=0, keepdims=True)

    @pl.when((step > 0) & (step <= blocks // 2))
    def _():
        tokens(True)

    @pl.when(step > blocks // 2)
    def _():
        tokens(False)

    @pl.when(step == pl.num_programs(0) - 1)
    def _():
        grad_ref[:, 2 * D + 2 * HD :] = table_ref[...].T.astype(BF)


def feed_forward(normed, normed_t, grad_out, bias, parts, held, *more):
    tokens, width = normed.shape
    hidden = bias.shape[1]
    blocks = tokens // BLK

    def whole(rows, columns):
        return pl.BlockSpec((rows, columns), lambda i: (0, 0))

    def block(first, last):
        return pl.BlockSpec((BLK, width), lambda i: (jnp.clip(i - 1 - first, 0, last - first), 0))

    every, own, other = block(0, blocks - 1), block(0, blocks // 2 - 1), block(blocks // 2, blocks - 1)
    across = pl.BlockSpec((HALF, BLK), lambda i: (0, jnp.maximum(i - 1, 0)))
    in_specs = [
        whole(tokens, width),
        whole(width, tokens),
        whole(tokens, width),
        whole(1, hidden),
    ]
    in_specs += (
        [whole(width, hidden), whole(hidden, width)]
        if parts is None
        else [pl.BlockSpec(memory_space=pl.ANY)] * 4
    )
    rows = jax.ShapeDtypeStruct((tokens, width), F32)
    side = jax.ShapeDtypeStruct((tokens // 2, width), F32)
    scratch = [pltpu.VMEM((tokens, hidden), BF), pltpu.VMEM((tokens, hidden), BF)]
    if not more:
        kernel = ffn_first_kernel
        shapes = (
            rows,
            rows,
            jax.ShapeDtypeStruct((width, 2 * width), BF),
            jax.ShapeDtypeStruct((1, hidden), F32),
        )
        out_specs = (every, every, whole(width, 2 * width), whole(1, hidden))
    else:
        kernel = ffn_second_kernel
        in_specs += [
            every,
            every,
            every,
            across,
            across,
            whole(width, more[5].shape[1]),
            whole(HALF, HALF),
            whole(HALF, HALF),
            own,
            whole(8, width),
            whole(16, width),
            whole(1, hidden),
            whole(width, 2 * HD),
        ]
        wide = 2 * width + 2 * HD + 128
        shapes = (side, side, side, side, jax.ShapeDtypeStruct((width, wide), BF))
        out_specs = (own, other, own, other, whole(width, wide))
        scratch.append(pltpu.VMEM((128, width), F32))
    if parts is not None:
        scratch += [
            pltpu.VMEM((width, hidden), BF),
            pltpu.VMEM((hidden, width), BF),
            pltpu.SemaphoreType.DMA((32,)),
        ]
    return pl.pallas_call(
        functools.partial(kernel, parts),
        out_shape=shapes,
        grid=(1 + blocks,),
        in_specs=in_specs,
        out_specs=out_specs,
        scratch_shapes=scratch,
        compiler_params=pltpu.CompilerParams(
            dimension_semantics=("arbitrary",), vmem_limit_bytes=56 << 20
        ),
        cost_estimate=pl.CostEstimate(
            flops=12 * tokens * width * hidden,
            transcendentals=2 * tokens * hidden,
            bytes_accessed=8 * width * hidden + 20 * tokens * width,
        ),
        name="ffn",
    )(normed, normed_t, grad_out, bias, *held, *more)


def shards(
    tokens,
    segments,
    ln1_gain,
    ln1_bias,
    ln2_gain,
    ln2_bias,
    q_weight,
    q_bias,
    kv_weight,
    k_bias,
    out_weight,
    out_bias,
    up_weight,
    up_bias,
    down_weight,
    cotangent,
):
    core, chip = lax.axis_index("core"), lax.axis_index("chip")
    chips = lax.axis_size("rows") * lax.axis_size("chip")
    own = tokens.shape[1]
    both = 2 * own
    rows = q_weight.shape[0]
    hidden = up_bias.shape[0]
    half = hidden // 2
    back_chips = DOC // both
    own_tokens, own_grad = tokens[0], cotangent[0]

    def half_columns(array, which):
        return lax.dynamic_slice_in_dim(
            array, which * (array.shape[1] // 2), array.shape[1] // 2, 1
        )

    def first(which):
        return jnp.concatenate(
            [half_columns(q_weight, which), half_columns(out_weight, which), kv_weight], axis=1
        )

    up_blocks = up_weight

    def up_half(which):
        block = up_blocks.reshape(rows, chips, 2, 2, half)
        block = lax.dynamic_index_in_dim(block, which, 2, keepdims=False)
        return block.transpose(0, 2, 1, 3).reshape(rows, FF // 2)

    flat = (ln1_gain, ln1_bias, ln2_gain, ln2_bias, q_bias, out_bias)
    if square_line():
        vectors = jnp.concatenate(
            [vector.reshape(1, rows) for vector in flat] + [up_bias.reshape(hidden // rows, rows)]
        )
        vectors = jnp.pad(vectors, ((0, 16 - vectors.shape[0]), (0, 0)))
        mine, theirs = pack(q_weight, out_weight, kv_weight, vectors)
        attn_piece = by_core(core, mine, core_swap(theirs), 0)
        segments, up_blocks = after((segments, up_blocks), attn_piece)
        attn_line = jnp.concatenate(gather_line(attn_piece))
        attn_rows = gather_rows(attn_line)
        up_piece = by_core(core, up_half(core), core_swap(up_half(1 - core)), 0)
        ff_piece = jnp.concatenate([up_piece[:, :D], up_piece[:, D:], down_weight], axis=0)
        ff_line = gather_line(after(ff_piece, attn_line))
        other_tokens = core_swap(own_tokens)
        features = jnp.concatenate([own_tokens, other_tokens], axis=0)
        grad_out = jnp.concatenate([own_grad, core_swap(own_grad)], axis=0)
        attn_rows, grad_out, features = lax.optimization_barrier((attn_rows, grad_out, features))
    else:
        weights = gather_whole(by_core(core, first(core), core_swap(first(1 - core)), 0))
        every = ("rows", "chip", "core")
        table = lax.all_gather(jnp.stack(flat), every, axis=1, tiled=True).astype(F32)
        vector_rows = jnp.pad(table, ((0, 2), (0, 0)))
        bias = gather_whole(up_bias).astype(F32).reshape(chips, 2, half)
        hidden_bias = jnp.pad(bias.transpose(1, 0, 2).reshape(2, D), ((0, 6), (0, 0)))

    if not square_line():
        other_tokens = core_swap(own_tokens)
        features = jnp.concatenate([own_tokens, other_tokens], axis=0)
        grad_out = jnp.concatenate([own_grad, core_swap(own_grad)], axis=0)

    ids = lax.broadcasted_iota(jnp.int32, (MAX_SEGS, 1), 0)
    doc_starts = jnp.sum((segments < ids).astype(jnp.int32), axis=1, keepdims=True)
    first_place, second_place = (chip * 2 + core) * own, (chip * 2 + 1 - core) * own
    span = lax.broadcasted_iota(jnp.int32, (1, own), 1)
    places = jnp.concatenate([first_place + span, second_place + span], axis=1)
    segs = jnp.concatenate(
        [
            lax.dynamic_slice(segments, (0, first_place), (1, own)),
            lax.dynamic_slice(segments, (0, second_place), (1, own)),
        ],
        axis=1,
    )
    starts = jnp.sum(jnp.where(segs == ids, doc_starts, 0), axis=0, keepdims=True)
    relative = places - starts
    frequency = 10000.0 ** (-(jnp.arange(ROT // 2, dtype=F32) * 2.0 / ROT))
    angles = relative.astype(F32) * frequency[:, None]
    cosine, sine = jnp.cos(angles), jnp.sin(angles)
    window_start = (chip - back_chips) * both
    pos = jnp.concatenate(
        [starts - window_start, places - window_start, jnp.zeros((6, both), jnp.int32)], axis=0
    )
    firsts, lasts = pos[:, ::BLK], pos[:, BLK - 1 :: BLK]
    scal = jnp.concatenate(
        [
            core.reshape(1),
            jnp.stack([firsts[0] // BLK, lasts[1] // BLK + 1, lasts[0]], axis=1).reshape(-1),
        ]
    ).astype(jnp.int32)


    bias_column = k_bias.astype(F32)[:, None]
    if square_line():
        weights, vector_rows, hidden_bias, *fronts = front(
            attn_rows, own_tokens, other_tokens, bias_column, cosine, sine
        )
    else:
        fronts = front(
            (weights, vector_rows), own_tokens, other_tokens, bias_column, cosine, sine
        )
    normed_one, normed_two, normed_two_t, query_t, own_pairs, keep, send = fronts
    got = core_swap(send)
    mine = jnp.concatenate(
        [chip_shift(own_pairs, k, False) for k in range(back_chips, 0, -1)] + [own_pairs], axis=0
    )
    theirs = core_swap(mine)
    if square_line():
        ff_rows = gather_rows(after(jnp.concatenate(ff_line), attn_rows))

    heads = attention(scal, query_t, grad_out, keep, got, pos, cosine, sine, mine, theirs)
    if square_line():
        heads, ff_rows = lax.optimization_barrier((heads, ff_rows))
    out_t, grad_query_t, pair_mine, pair_theirs = heads
    pair_got = core_swap(pair_theirs)
    grad_query, proj_keep, proj_send, sums = after_heads(
        out_t, grad_query_t, normed_one, grad_out
    )
    proj_got = core_swap(proj_send)
    if square_line():
        pair_got, proj_got = after((pair_got, proj_got), sums)
        parts = [((i * 2 * rows, 2 * rows, 0), ((2 + i) * 2 * rows, 2 * rows, 1)) for i in range(2)]
        held = [ff_rows, ff_rows]
    else:
        up_whole = gather_whole(by_core(core, up_half(core), core_swap(up_half(1 - core)), 0))
        down_whole = gather_whole(down_weight).reshape(chips, 2, half, D)
        down_whole = down_whole.transpose(1, 0, 2, 3).reshape(2, D, D)
        parts = [None, None]
        held = [(up_whole[:, i * D : (i + 1) * D], down_whole[i]) for i in range(2)]
    pair_sum = pair_mine + pair_got
    arrived = [
        chip_shift(
            pair_sum[(back_chips - k) * own : (back_chips - k + 1) * own].astype(BF), -k, False
        )
        for k in range(1, back_chips + 1)
    ]
    grad_proj = by_core(core, proj_keep, proj_got, 0)
    attn_terms = jnp.concatenate([grad_query, grad_proj], axis=1)
    if square_line():
        attn_plane, attn_one = reduce_rows(attn_terms)
    grad_pair, grad_one_pair, key_bias = after_pairs(
        pair_sum, *arrived, normed_one, weights, cosine, sine
    )
    key_bias = key_bias[0, :HD]

    inputs = (normed_two, normed_two_t, grad_out)
    if square_line():
        other_bias = core_swap(key_bias)
    first = feed_forward(*inputs, hidden_bias[0:1], parts[0], held[0])
    if square_line():
        first, other_bias = lax.optimization_barrier((after(first, attn_one), other_bias))
        key_bias = key_bias + other_bias
    mlp, grad_two, terms0, bias0 = first
    if square_line():
        plane0, one0 = reduce_rows(terms0)
        other_bias = line_swap(key_bias, 1)
    part, part_send, scaled, scaled_send, terms1 = second = feed_forward(
        *inputs,
        hidden_bias[1:2],
        parts[1],
        held[1],
        mlp,
        grad_two,
        features,
        out_t,
        grad_query_t,
        weights,
        keep,
        got,
        grad_one_pair,
        vector_rows,
        sums,
        bias0,
        grad_pair,
    )
    part, part_send, scaled, scaled_send, terms1 = second
    if square_line():
        (part, part_send, scaled, scaled_send), one0, other_bias = lax.optimization_barrier(
            ((part, part_send, scaled, scaled_send), one0, other_bias)
        )
        key_bias = key_bias + other_bias
    part_got, scaled_got = core_swap(part_send), core_swap(scaled_send)

    def finish(part_got, scaled_got):
        layer_out = own_tokens.astype(F32) + part + part_got + vector_rows[5:6]
        total = scaled + scaled_got
        unit, spread = standard(own_tokens)
        input_grad = own_grad.astype(F32) + spread * (
            total
            - jnp.mean(total, axis=-1, keepdims=True)
            - unit * jnp.mean(total * unit, axis=-1, keepdims=True)
        )
        return layer_out.astype(BF), input_grad

    def split(value):
        return (
            lax.dynamic_slice_in_dim(value, core * rows, rows, 0),
            core_swap(lax.dynamic_slice_in_dim(value, (1 - core) * rows, rows, 0)),
        )

    def blocks(first_half, second_half):
        return jnp.stack(
            [value.reshape(rows, chips, half) for value in (first_half, second_half)], axis=2
        ).reshape(rows, chips, 1, hidden)

    if square_line():
        plane1, one1 = reduce_rows(terms1)
        other_bias = line_swap(after(key_bias, part_got), 2)
        own0, three0 = reduce_third(plane0, after(one0, part_got, scaled_got))
        layer_out, input_grad = finish(part_got, scaled_got)
        three0, layer_out, input_grad, other_bias = lax.optimization_barrier(
            (three0, layer_out, input_grad, other_bias)
        )
        key_bias = key_bias + other_bias
        attn_own, attn_three = reduce_third(attn_plane, after(attn_one, three0))
        sum0 = reduce_last(own0, three0)
        one1, attn_three, sum0 = lax.optimization_barrier((one1, attn_three, sum0))
        own1, three1 = reduce_third(plane1, one1)
        other_bias = rows_swap(after(key_bias, one1), 1)
        key_bias = key_bias + other_bias
        attn_split = split(reduce_last(attn_own, after(attn_three, other_bias)))
        up_split = split(after(sum0, other_bias)[:, :D])
        key_bias_out = key_bias + rows_swap(key_bias, 2)
        mine, theirs = attn_split
        query_out = by_core(core, mine[:, :HALF], theirs[:, :HALF], 1)
        proj_out = by_core(core, mine[:, HALF:], theirs[:, HALF:], 1)
        three1, up_split, query_out, proj_out, key_bias_out = lax.optimization_barrier(
            (three1, up_split, query_out, proj_out, key_bias_out)
        )
        sum1 = reduce_last(own1, three1)
    else:
        layer_out, input_grad = finish(part_got, scaled_got)
        sum0, sum1 = reduce_whole(terms0), reduce_whole(terms1)
        up_split = split(sum0[:, :D])
        mine, theirs = split(reduce_whole(attn_terms))
        query_out = by_core(core, mine[:, :HALF], theirs[:, :HALF], 1)
        proj_out = by_core(core, mine[:, HALF:], theirs[:, HALF:], 1)
        key_bias_out = lax.psum(key_bias, ("rows", "chip", "core"))
    mine, theirs = split(jnp.concatenate([sum1[:, :D], sum1[:, 2 * D :]], axis=1))
    rest = mine[:, D:] + theirs[:, D:]
    pair_out, vector_out = rest[:, : 2 * HD], rest[:, 2 * HD :]
    up_bias_out = sum1[:, 2 * D + 2 * HD + 6 : 2 * D + 2 * HD + 8].T.reshape(hidden)
    up_out = by_core(
        core, blocks(up_split[0], mine[:, :D]), blocks(up_split[1], theirs[:, :D]), 2
    ).reshape(rows, FF)
    down_out = jnp.concatenate([sum0[:, D:], sum1[:, D : 2 * D]], axis=0)
    return (
        layer_out[None],
        input_grad[None],
        vector_out[:, 0],
        vector_out[:, 1],
        vector_out[:, 2],
        vector_out[:, 3],
        query_out,
        vector_out[:, 4],
        pair_out,
        key_bias_out,
        proj_out,
        vector_out[:, 5],
        up_out,
        up_bias_out,
        down_out,
    )


def solution(mesh):
    devices = mesh.devices.reshape(mesh.shape["rows"], mesh.shape["wide"] // 2, 2)
    every, wide = ("rows", "chip", "core"), ("chip", "core")
    matrix, vector, sequence = P(every, None), P(every), P("rows", wide, None)
    return jax.shard_map(
        shards,
        mesh=Mesh(devices, every),
        in_specs=(
            sequence,
            P("rows", None),
            vector,
            vector,
            vector,
            vector,
            matrix,
            vector,
            matrix,
            P(),
            matrix,
            vector,
            matrix,
            vector,
            matrix,
            sequence,
        ),
        out_specs=(
            sequence,
            sequence,
            vector,
            vector,
            vector,
            vector,
            matrix,
            vector,
            matrix,
            P(),
            matrix,
            vector,
            matrix,
            vector,
            matrix,
        ),
        check_vma=False,
    )
```

```python
import functools
import math

import jax
import jax.numpy as jnp
from jax import lax
from jax.experimental import pallas as pl
from jax.experimental.pallas import tpu as pltpu
from jax.sharding import Mesh, PartitionSpec as P

D = 768
HEADS = 12
HD = 64
ROT = 16
DOC = 2048
FF = 3072
MAX_SEGS = 32
norm_eps = 1e-05
BF = jnp.bfloat16
F32 = jnp.float32
HALF = HEADS // 2 * HD
BLK = 256
GROUP = 6


def dot(left, right, dims):
    return lax.dot_general(left, right, (dims, ((), ())), preferred_element_type=F32)


def core_swap(value):
    return lax.ppermute(value, "core", [(0, 1), (1, 0)])


def rows_swap(value, bit):
    return lax.ppermute(value, "rows", [(r, r ^ bit) for r in range(4)])


def chip_shift(value, by, wrap):
    count = lax.axis_size("chip")
    pairs = [(s, (s + by) % count) for s in range(count) if wrap or 0 <= s + by < count]
    return lax.ppermute(value, "chip", pairs)


def square_line():
    return lax.axis_size("rows") == 4 and lax.axis_size("chip") == 4


def place_copies(parts, sources, outs, sems):
    row, chip = lax.axis_index("rows"), lax.axis_index("chip")
    size = sources[0].shape[0] // 4
    copies = []
    for first, count, out in parts:
        for turn, source in enumerate(sources):
            for step in range(4):
                place = (row ^ turn) * 4 + lax.rem(chip + step, 4)
                copies.append(
                    pltpu.make_async_copy(
                        source.at[pl.ds(step * size + first, count)],
                        outs[out].at[pl.ds(pl.multiple_of(place * count, 8), count)]
                        if isinstance(out, int)
                        else outs[out[0]].at[out[1], pl.ds(pl.multiple_of(place * count, 8), count)],
                        sems.at[len(copies)],
                    )
                )
    return copies


def gather_line(piece):
    return [piece] + [chip_shift(piece, -k, True) for k in (1, 2, 3)]


def gather_rows(lines):
    return lines, rows_swap(lines, 1), rows_swap(lines, 2), rows_swap(lines, 3)


def gather_whole(piece):
    return lax.all_gather(piece, ("rows", "chip"), axis=0, tiled=True)


def reduce_first(terms):
    row = lax.axis_index("rows")
    grid = terms.reshape((4, 4, terms.shape[0] // 16) + terms.shape[1:])
    planes = [lax.dynamic_index_in_dim(grid, row ^ bit, 0, keepdims=False) for bit in range(4)]
    return planes, (rows_swap(planes[3][:2], 1), rows_swap(planes[3][2:], 2))


def reduce_rows(terms):
    row = lax.axis_index("rows")
    grid = terms.reshape((4, 4, terms.shape[0] // 16) + terms.shape[1:])
    planes = [lax.dynamic_index_in_dim(grid, row ^ bit, 0, keepdims=False) for bit in range(4)]
    return planes[0], [rows_swap(planes[bit], bit) for bit in (3, 1, 2)]


def reduce_second(planes, arrived, beside=None):
    _, flat, cross, _ = planes
    from_flat, from_cross = arrived
    to_flat = jnp.concatenate(
        [flat[:2], (flat[2:].astype(F32) + from_cross.astype(F32)).astype(BF)], axis=0
    )
    to_cross = jnp.concatenate(
        [(cross[:2].astype(F32) + from_flat.astype(F32)).astype(BF), cross[2:]], axis=0
    )
    if beside is not None:
        to_flat = jnp.concatenate([to_flat, beside[1]], axis=2)
        to_cross = jnp.concatenate([to_cross, beside[2]], axis=2)
    return rows_swap(to_flat, 1), rows_swap(to_cross, 2)


def reduce_third(*groups):
    chip = lax.axis_index("chip")

    def line(step):
        spot = lax.rem(chip + step, 4)
        sums = []
        for group in groups:
            pick = [
                lax.dynamic_index_in_dim(part, spot, 0, keepdims=False).astype(F32)
                for part in group
            ]
            sums.append(sum(pick[1:], pick[0]))
        return jnp.concatenate(sums, axis=1)

    return line(0), [chip_shift(line(step).astype(BF), step, True) for step in (1, 2, 3)]


def reduce_last(own, arrived):
    return own + arrived[0].astype(F32) + arrived[1].astype(F32) + arrived[2].astype(F32)


def reduce_whole(terms):
    return lax.psum_scatter(terms.astype(F32), ("rows", "chip"), scatter_dimension=0, tiled=True)


def after(value, *others):
    return lax.optimization_barrier((value, others))[0]


def line_swap(value, bit):
    return lax.ppermute(value, "chip", [(s, s ^ bit) for s in range(4)])


def by_core(core, own, other, axis):
    return jnp.where(
        core == 0,
        jnp.concatenate([own, other], axis=axis),
        jnp.concatenate([other, own], axis=axis),
    )


def pack_kernel(q_ref, out_ref, kv_ref, vectors_ref, mine_ref, theirs_ref):
    core = lax.axis_index("core")
    rows = q_ref.shape[0]
    pick = lax.broadcasted_iota(jnp.int32, (16, 128), 0) == lax.broadcasted_iota(
        jnp.int32, (16, 128), 1
    )
    columns = dot(vectors_ref[...], jnp.where(pick, 1.0, 0.0).astype(BF), ((0,), (0,))).astype(BF)
    for which, ref in ((core, mine_ref), (1 - core, theirs_ref)):
        spot = pl.ds(pl.multiple_of(which * HALF, HALF), HALF)
        ref[:, :HALF] = q_ref[:, spot]
        ref[:, HALF : 2 * HALF] = out_ref[:, spot]
        ref[:, 2 * HALF : 2 * HALF + 2 * HD] = kv_ref[...]
        ref[:, 2 * HALF + 2 * HD :] = columns


def pack(q_weight, out_weight, kv_weight, vectors):
    rows = q_weight.shape[0]
    side = jax.ShapeDtypeStruct((rows, 2 * HALF + 2 * HD + 128), BF)
    return pl.pallas_call(
        pack_kernel,
        out_shape=(side, side),
        cost_estimate=pl.CostEstimate(flops=0, transcendentals=0, bytes_accessed=8 * rows * D),
        name="pack",
    )(q_weight, out_weight, kv_weight, vectors)


def turn(values, cosine, sine, direction):
    half = ROT // 2
    a, b = values[:half, :], values[half:ROT, :]
    return jnp.concatenate(
        [a * cosine - direction * b * sine, b * cosine + direction * a * sine, values[ROT:, :]],
        axis=0,
    )


def standard(tokens):
    values = tokens.astype(F32)
    center = values - jnp.mean(values, axis=-1, keepdims=True)
    spread = lax.rsqrt(jnp.mean(center * center, axis=-1, keepdims=True) + norm_eps)
    return center * spread, spread


def front_rest(
    own_ref, other_ref, kbias_ref, cos_ref, sin_ref, w_ref, rows_ref,
    h1_ref, h2_ref, h2t_ref, q_ref, pairs_ref, keep_ref, send_ref,
):
    core = lax.axis_index("core")
    count = own_ref.shape[0]
    gain_one, shift_one, gain_two, shift_two = (rows_ref[i : i + 1, :] for i in range(4))

    def norm(part, ref):
        unit, _ = standard(ref[...])
        spot = pl.ds(part * count, count)
        h1_ref[spot, :] = (unit * gain_one + shift_one).astype(BF)
        normed = (unit * gain_two + shift_two).astype(BF)
        h2_ref[spot, :] = normed
        h2t_ref[:, part * count : (part + 1) * count] = normed.T

    norm(0, own_ref)
    pair = dot(w_ref[:, 2 * HALF : 2 * HALF + 2 * HD], h1_ref[:count, :], ((0,), (1,)))
    key = turn(
        pair[:HD] + kbias_ref[...], cos_ref[:, :count], sin_ref[:, :count], 1.0
    ).astype(BF)
    pairs_ref[...] = jnp.concatenate([key, pair[HD:].astype(BF)], axis=0).T
    norm(1, other_ref)
    query = dot(w_ref[:, :HALF], h1_ref[...], ((0,), (1,)))
    bias = jnp.where(core == 0, rows_ref[4:5, :HALF], rows_ref[4:5, HALF:])
    query = query + jnp.broadcast_to(bias, (8, HALF)).T[:, :1]
    for h in range(HEADS // 2):
        q_ref[h * HD : (h + 1) * HD, :] = turn(
            query[h * HD : (h + 1) * HD, :], cos_ref[...], sin_ref[...], 1.0
        ).astype(BF)
    for index, ref in ((core, keep_ref), (1 - core, send_ref)):
        spot = pl.ds(pl.multiple_of(index * HALF, HALF), HALF)
        ref[...] = w_ref[spot, HALF : 2 * HALF]


def front_kernel(
    lines_ref, flat_ref, cross_ref, far_ref, own_ref, other_ref, kbias_ref, cos_ref, sin_ref,
    w_ref, rows_ref, bias_ref, h1_ref, h2_ref, h2t_ref, q_ref, pairs_ref, keep_ref, send_ref, sems,
):
    core = lax.axis_index("core")
    copies = place_copies(
        ((0, w_ref.shape[0] // 16, 0),), (lines_ref, flat_ref, cross_ref, far_ref), (w_ref,), sems
    )
    for copy in copies:
        copy.start()
    for copy in copies:
        copy.wait()
    table = w_ref[:, 2 * HALF + 2 * HD :].astype(F32).T
    rows_ref[...] = table[:8, :]
    half = lax.rem(lax.broadcasted_iota(jnp.int32, (1, D), 1), 48) // 24
    for k in range(2):
        low, high = table[6 + 2 * k : 7 + 2 * k, :], table[7 + 2 * k : 8 + 2 * k, :]
        first = jnp.where(half == 0, low, pltpu.roll(jnp.broadcast_to(high, (8, D)), 24, 1)[:1])
        second = jnp.where(
            half == 1, high, pltpu.roll(jnp.broadcast_to(low, (8, D)), D - 24, 1)[:1]
        )
        bias_ref[k : k + 1, :] = jnp.where(core == 0, first, second)
    bias_ref[2:8, :] = jnp.zeros((6, D), F32)
    front_rest(
        own_ref, other_ref, kbias_ref, cos_ref, sin_ref, w_ref, rows_ref,
        h1_ref, h2_ref, h2t_ref, q_ref, pairs_ref, keep_ref, send_ref,
    )


def front_plain_kernel(
    w_ref, rows_ref, own_ref, other_ref, kbias_ref, cos_ref, sin_ref, *outs
):
    front_rest(own_ref, other_ref, kbias_ref, cos_ref, sin_ref, w_ref, rows_ref, *outs)


def front(pieces, own, other, k_bias, cosine, sine):
    both = 2 * own.shape[0]
    placed = len(pieces) == 4
    wide = pieces[0].shape[1]
    shapes = (
        jax.ShapeDtypeStruct((both, D), BF),
        jax.ShapeDtypeStruct((both, D), BF),
        jax.ShapeDtypeStruct((D, both), BF),
        jax.ShapeDtypeStruct((HALF, both), BF),
        jax.ShapeDtypeStruct((own.shape[0], 2 * HD), BF),
        jax.ShapeDtypeStruct((HALF, HALF), BF),
        jax.ShapeDtypeStruct((HALF, HALF), BF),
    )
    here = pl.BlockSpec(memory_space=pltpu.VMEM)
    if placed:
        shapes = (
            jax.ShapeDtypeStruct((D, wide), BF),
            jax.ShapeDtypeStruct((8, D), F32),
            jax.ShapeDtypeStruct((8, D), F32),
        ) + shapes
    return pl.pallas_call(
        front_kernel if placed else front_plain_kernel,
        out_shape=shapes,
        in_specs=[pl.BlockSpec(memory_space=pl.ANY) if placed else here] * len(pieces) + [here] * 5,
        out_specs=tuple(here for _ in shapes),
        scratch_shapes=[pltpu.SemaphoreType.DMA((16,))] if placed else [],
        compiler_params=pltpu.CompilerParams(vmem_limit_bytes=48 << 20),
        cost_estimate=pl.CostEstimate(
            flops=2 * both * D * (HALF + 2 * HD), transcendentals=both, bytes_accessed=8 * both * D
        ),
        name="front",
    )(*pieces, own, other, k_bias, cosine, sine)


def attn_kernel(
    scal_ref, q_ref, grad_ref, keep_in_ref, got_in_ref, pos_ref, cos_ref, sin_ref, mine_ref, theirs_ref,
    o_ref, dq_ref, dmine_ref, dtheirs_ref,
    keep_ref, got_ref, kv_ref, kvt_ref, dkv_ref, g_ref, s_ref, r_ref, rt_ref, sems,
):
    block = pl.program_id(0)
    core = scal_ref[0]
    low, high, edge = (scal_ref[1 + 3 * block + i] for i in range(3))
    wide = GROUP * BLK
    half = kv_ref.shape[0] // 2
    own_blocks = pl.num_programs(0) // 2

    @pl.when(block == 0)
    def _():
        dkv_ref[...] = jnp.zeros_like(dkv_ref)
        copies = [
            pltpu.make_async_copy(source, target, sems.at[i])
            for i, (source, target) in enumerate(
                (
                    (mine_ref, kv_ref.at[pl.ds(0, half)]),
                    (theirs_ref, kv_ref.at[pl.ds(half, half)]),
                    (keep_in_ref, keep_ref),
                    (got_in_ref, got_ref),
                )
            )
        ]
        for copy in copies:
            copy.start()
        for copy in copies:
            copy.wait()
        for part in range(2):
            kvt_ref[: 2 * HD, part * half : (part + 1) * half] = kv_ref[
                part * half : (part + 1) * half, :
            ].T
        kvt_ref[2 * HD :, :] = jnp.ones((16, 2 * half), BF)

    def spot(key_block):
        side = lax.rem(key_block // own_blocks, 2) ^ core
        place = (key_block // (2 * own_blocks)) * own_blocks + lax.rem(key_block, own_blocks)
        return pl.multiple_of(side * half + place * BLK, BLK)

    first, pairs_end, single = low // 2, high // 2, lax.rem(high, 2)
    last = pairs_end - 1 + single
    clear = jnp.clip((edge + 2 * BLK - 1) // (2 * BLK), first, last)

    def slot(key_block, size):
        return pl.ds(pl.multiple_of((key_block - 2 * first) * BLK, BLK), size)

    def over_keys(body, carry):
        def double(masked):
            return lambda i, c: body(masked, 2 * i, 2 * BLK, c)

        carry = lax.fori_loop(first, clear, double(True), carry)
        carry = lax.fori_loop(clear, last, double(False), carry)
        carry = lax.fori_loop(last, pairs_end, double(True), carry)
        return lax.fori_loop(
            0, single, lambda i, c: body(True, 2 * pairs_end + i, BLK, c), carry
        )

    def over_all(body, carry):
        carry = lax.fori_loop(first, pairs_end, lambda i, c: body(2 * i, 2 * BLK, c), carry)
        return lax.fori_loop(0, single, lambda i, c: body(2 * pairs_end + i, BLK, c), carry)

    near = pl.ds(pl.multiple_of(core * HALF, HALF), HALF)
    away = pl.ds(pl.multiple_of((1 - core) * HALF, HALF), HALF)
    g_ref[...] = (
        dot(keep_ref[...], grad_ref[:, near], ((1,), (1,)))
        + dot(got_ref[...], grad_ref[:, away], ((1,), (1,)))
    ).astype(BF)
    starts = jnp.concatenate([pos_ref[0:1, :]] * GROUP, axis=1)
    places = jnp.concatenate([pos_ref[1:2, :]] * GROUP, axis=1)
    blank = jnp.zeros((HD, BLK), BF)
    for h in range(GROUP):
        query = (q_ref[h * HD : (h + 1) * HD, :].astype(F32) * HD**-0.5).astype(BF)
        grad = g_ref[h * HD : (h + 1) * HD, :]
        query = jnp.concatenate([query, blank], axis=0)
        grad = jnp.concatenate([blank, grad], axis=0)
        r_ref[0, :, h * BLK : (h + 1) * BLK] = query
        r_ref[1, :, h * BLK : (h + 1) * BLK] = grad
        rt_ref[h * BLK : (h + 1) * BLK, :] = query.T
        rt_ref[(GROUP + h) * BLK : (GROUP + h + 1) * BLK, :] = grad.T

    def scores(masked, key_block, size, peak):
        keys = kv_ref[pl.ds(spot(key_block), size), :]
        s = dot(keys, r_ref[0], ((1,), (0,)))
        if masked:
            key_places = key_block * BLK + lax.broadcasted_iota(jnp.int32, (size, wide), 0)
            s = jnp.where((key_places >= starts) & (key_places <= places), s, -1e30)
        s_ref[slot(key_block, size), :] = s
        return jnp.maximum(peak, jnp.max(s, axis=0, keepdims=True))

    peak = over_keys(scores, jnp.full((1, wide), -1e30, F32))

    def expo(key_block, size, out):
        values = kvt_ref[HD:, pl.ds(spot(key_block), size)]
        e = jnp.exp(s_ref[slot(key_block, size), :] - peak)
        s_ref[slot(key_block, size), :] = e
        return out + dot(values, e.astype(BF), ((1,), (0,)))

    out = over_all(expo, jnp.zeros((HD + 16, wide), F32))
    inverse = 1.0 / out[HD : HD + 1, :]
    out = out[:HD] * inverse
    deltas = []
    for h in range(GROUP):
        part = out[:, h * BLK : (h + 1) * BLK]
        o_ref[h * HD : (h + 1) * HD, :] = part.astype(BF)
        deltas.append(
            jnp.sum(part * g_ref[h * HD : (h + 1) * HD, :].astype(F32), axis=0, keepdims=True)
        )
    delta = jnp.concatenate(deltas, axis=1)

    def back(key_block, size, dq):
        where = spot(key_block)
        pairs = kv_ref[pl.ds(where, size), :]
        keys = kvt_ref[:HD, pl.ds(where, size)]
        p = s_ref[slot(key_block, size), :] * inverse
        dp = dot(pairs, r_ref[1], ((1,), (0,)))
        ds = (p * (dp - delta)).astype(BF)
        left = jnp.concatenate([ds, p.astype(BF)], axis=1)
        dkv_ref[pl.ds(where, size), :] += dot(left, rt_ref[...], ((1,), (0,)))
        return dq + dot(keys, ds, ((1,), (0,)))

    dq = over_all(back, jnp.zeros((HD, wide), F32)) * HD**-0.5
    for h in range(GROUP):
        part = dq[:, h * BLK : (h + 1) * BLK].astype(BF).astype(F32)
        dq_ref[h * HD : (h + 1) * HD, :] = turn(part, cos_ref[...], sin_ref[...], -1.0).astype(BF)

    @pl.when(block == pl.num_programs(0) - 1)
    def _():
        dmine_ref[...] = dkv_ref[:half, :]
        dtheirs_ref[...] = dkv_ref[half:, :]


def attention(scal, query_t, grad_out, keep, got, pos, cosine, sine, mine, theirs):
    features, tokens = query_t.shape
    blocks, half = tokens // BLK, mine.shape[0]
    tile = pl.BlockSpec((features, BLK), lambda b, s: (0, b))
    small = pl.BlockSpec((8, BLK), lambda b, s: (0, b))

    def whole(rows, columns):
        return pl.BlockSpec((rows, columns), lambda b, s: (0, 0))

    return pl.pallas_call(
        attn_kernel,
        out_shape=(
            jax.ShapeDtypeStruct((features, tokens), BF),
            jax.ShapeDtypeStruct((features, tokens), BF),
            jax.ShapeDtypeStruct((half, 2 * HD), F32),
            jax.ShapeDtypeStruct((half, 2 * HD), F32),
        ),
        grid_spec=pltpu.PrefetchScalarGridSpec(
            num_scalar_prefetch=1,
            grid=(blocks,),
            in_specs=[
                tile,
                pl.BlockSpec((BLK, D), lambda b, s: (b, 0)),
                pl.BlockSpec(memory_space=pltpu.HBM),
                pl.BlockSpec(memory_space=pltpu.HBM),
                small,
                small,
                small,
                pl.BlockSpec(memory_space=pltpu.HBM),
                pl.BlockSpec(memory_space=pltpu.HBM),
            ],
            out_specs=(tile, tile, whole(half, 2 * HD), whole(half, 2 * HD)),
            scratch_shapes=[
                pltpu.VMEM((HALF, HALF), BF),
                pltpu.VMEM((HALF, HALF), BF),
                pltpu.VMEM((2 * half, 2 * HD), BF),
                pltpu.VMEM((2 * HD + 16, 2 * half), BF),
                pltpu.VMEM((2 * half, 2 * HD), F32),
                pltpu.VMEM((features, BLK), BF),
                pltpu.VMEM((DOC + 2 * BLK, GROUP * BLK), F32),
                pltpu.VMEM((2, 2 * HD, GROUP * BLK), BF),
                pltpu.VMEM((2 * GROUP * BLK, 2 * HD), BF),
                pltpu.SemaphoreType.DMA((4,)),
            ],
        ),
        compiler_params=pltpu.CompilerParams(
            dimension_semantics=("arbitrary",), vmem_limit_bytes=60 << 20
        ),
        cost_estimate=pl.CostEstimate(
            flops=12 * features * tokens * DOC * 3 // 4,
            transcendentals=features // HD * tokens * DOC * 3 // 4,
            bytes_accessed=8 * features * tokens,
        ),
        name="attention",
    )(scal, query_t, grad_out, keep, got, pos, cosine, sine, mine, theirs)


def heads_kernel(
    o_ref, dq_ref, h1_ref, grad_ref, gq_ref, keep_out_ref, send_out_ref, sums_ref
):
    core = lax.axis_index("core")
    near = pl.ds(pl.multiple_of(core * HALF, HALF), HALF)
    away = pl.ds(pl.multiple_of((1 - core) * HALF, HALF), HALF)
    send_out_ref[...] = dot(o_ref[...], grad_ref[:, away], ((1,), (0,))).astype(BF)
    keep_out_ref[...] = dot(o_ref[...], grad_ref[:, near], ((1,), (0,))).astype(BF)
    gq_ref[...] = dot(dq_ref[...], h1_ref[...], ((1,), (0,))).T.astype(BF)
    ones = jnp.ones((8, dq_ref.shape[1]), BF)
    sums_ref[...] = jnp.zeros_like(sums_ref)
    sums_ref[0:8, near] = dot(ones, dq_ref[...], ((1,), (1,)))
    count = grad_ref.shape[0] // 2
    sums_ref[8:16, :] = dot(ones[:, :count], grad_ref[:count, :], ((1,), (0,)))


def after_heads(out_t, dq_t, normed, grad_out):
    both = normed.shape[0]
    return pl.pallas_call(
        heads_kernel,
        out_shape=(
            jax.ShapeDtypeStruct((D, HALF), BF),
            jax.ShapeDtypeStruct((HALF, HALF), BF),
            jax.ShapeDtypeStruct((HALF, HALF), BF),
            jax.ShapeDtypeStruct((16, D), F32),
        ),
        compiler_params=pltpu.CompilerParams(vmem_limit_bytes=48 << 20),
        cost_estimate=pl.CostEstimate(
            flops=4 * both * D * HALF, transcendentals=0, bytes_accessed=6 * both * D
        ),
        name="after_heads",
    )(out_t, dq_t, normed, grad_out)


def pairs_kernel(
    own_ref, near_ref, far_ref, h1_ref, w_ref, cos_ref, sin_ref, gw_ref, dh_ref, gbias_ref
):
    total = own_ref[...] + near_ref[...].astype(F32) + far_ref[...].astype(F32)
    total = total.astype(BF).astype(F32).T
    key = turn(total[:HD], cos_ref[...], sin_ref[...], -1.0)
    grad = jnp.concatenate([key, total[HD:]], axis=0).astype(BF)
    gw_ref[...] = dot(grad, h1_ref[...], ((1,), (0,))).T.astype(BF)
    dh_ref[...] = dot(grad.T, w_ref[:, 2 * HALF : 2 * HALF + 2 * HD], ((1,), (1,)))
    ones = jnp.ones((8, grad.shape[1]), BF)
    gbias_ref[...] = dot(ones, grad, ((1,), (1,)))


def after_pairs(pairs, near, far, normed, weights, cosine, sine):
    count = near.shape[0]

    def whole(rows, columns):
        return pl.BlockSpec((rows, columns), lambda i: (0, 0))

    return pl.pallas_call(
        pairs_kernel,
        out_shape=(
            jax.ShapeDtypeStruct((D, 2 * HD), BF),
            jax.ShapeDtypeStruct((count, D), F32),
            jax.ShapeDtypeStruct((8, 2 * HD), F32),
        ),
        grid=(1,),
        in_specs=[
            pl.BlockSpec((count, 2 * HD), lambda i: (pairs.shape[0] // count - 1, 0)),
            whole(count, 2 * HD),
            whole(count, 2 * HD),
            whole(count, D),
            whole(D, weights.shape[1]),
            whole(8, count),
            whole(8, count),
        ],
        out_specs=(whole(D, 2 * HD), whole(count, D), whole(8, 2 * HD)),
        compiler_params=pltpu.CompilerParams(vmem_limit_bytes=32 << 20),
        cost_estimate=pl.CostEstimate(
            flops=8 * count * D * HD, transcendentals=0, bytes_accessed=8 * count * D
        ),
        name="after_pairs",
    )(pairs, near, far, normed, weights, cosine, sine)


def ffn_units(
    placed, h_ref, ht_ref, g_ref, bias_ref, up_ref, down_ref, grad_ref, act_ref, dz_ref
):
    for copy in placed:
        copy.start()
    for copy in placed[:16]:
        copy.wait()
    z = dot(h_ref[...], up_ref[...], ((1,), (0,))) + bias_ref[...]
    below = 0.5 * (1.0 + lax.erf(z * 0.5**0.5))
    slope = below + z * (jnp.exp(-0.5 * z * z) * (0.5 / math.pi) ** 0.5)
    act = (z * below).astype(BF)
    grad_ref[:, D : 2 * D] = dot(act, g_ref[...], ((0,), (0,))).astype(BF)
    act_ref[...] = act
    for copy in placed[16:]:
        copy.wait()
    grad = (dot(g_ref[...], down_ref[...], ((1,), (1,))) * slope).astype(BF)
    dz_ref[...] = grad
    grad_ref[:, :D] = dot(ht_ref[...], grad, ((1,), (0,))).astype(BF)
    return jnp.sum(grad.astype(F32), axis=0, keepdims=True)


def ffn_weights(parts, rest):
    if parts is None:
        return (), rest[0], rest[1], rest[2:]
    up_ref, down_ref, sems = rest[-3:]
    return place_copies(parts, rest[:4], (up_ref, down_ref), sems), up_ref, down_ref, rest[4:-3]


def ffn_first_kernel(parts, h_ref, ht_ref, g_ref, bias_ref, *rest):
    placed, up_ref, down_ref, rest = ffn_weights(parts, rest)
    act_ref, dz_ref, grad_ref, gbias_ref = rest
    gbias_ref[...] = ffn_units(
        placed, h_ref, ht_ref, g_ref, bias_ref, up_ref, down_ref, grad_ref, act_ref, dz_ref
    )


def tokens_kernel(
    parts, act0_ref, act1_ref, dz0_ref, dz1_ref, x_ref, o_ref, dq_ref, w_ref, out_keep_ref, out_got_ref,
    pair_ref, rows_ref, sums_ref, bias0_ref, bias1_ref, gpair_ref, *rest
):
    placed, up_ref, down_ref, rest = ffn_weights(parts, rest)
    keep_ref, send_ref, tkeep_ref, tsend_ref, small_ref, table_ref = rest
    step = pl.program_id(0)
    core = lax.axis_index("core")
    blocks = pl.num_programs(0)

    @pl.when(step == 0)
    def _():
        for copy in placed:
            copy.start()
        table_ref[...] = jnp.zeros_like(table_ref)
        table_ref[4:5, :] = sums_ref[0:1, :]
        table_ref[5:6, :] = sums_ref[8:9, :]
        table_ref[6:7, :] = bias0_ref[...]
        table_ref[7:8, :] = bias1_ref[...]
        small_ref[:, : 2 * HD] = gpair_ref[...]
        for copy in placed:
            copy.wait()

    def tokens(first):
        heads = o_ref[...].T
        near = dot(heads, out_keep_ref[...], ((1,), (0,)))
        away = dot(heads, out_got_ref[...], ((1,), (0,)))
        low, high = jnp.where(core == 0, near, away), jnp.where(core == 0, away, near)
        out = dot(act0_ref[...], down_ref[0], ((1,), (0,))) + dot(
            act1_ref[...], down_ref[1], ((1,), (0,))
        )
        out = out + jnp.concatenate([low, high], axis=1)
        two = dot(dz0_ref[...], up_ref[0], ((1,), (1,))) + dot(
            dz1_ref[...], up_ref[1], ((1,), (1,))
        )
        one = dot(dq_ref[...].T, w_ref[:, :HALF], ((1,), (1,)))
        if first:
            one = one + pair_ref[...]
        unit, _ = standard(x_ref[...])
        scaled = one * rows_ref[0:1, :] + two * rows_ref[2:3, :]
        refs = (keep_ref, tkeep_ref) if first else (send_ref, tsend_ref)
        refs[0][...], refs[1][...] = out, scaled
        for i, value in enumerate((one * unit, one, two * unit, two)):
            table_ref[i : i + 1, :] += jnp.sum(value, axis=0, keepdims=True)

    @pl.when(step < blocks // 2)
    def _():
        tokens(True)

    @pl.when(step >= blocks // 2)
    def _():
        tokens(False)

    @pl.when(step == blocks - 1)
    def _():
        small_ref[:, 2 * HD :] = table_ref[...].T.astype(BF)


def feed_forward(normed, normed_t, grad_out, bias, parts, held):
    tokens, width = normed.shape
    hidden = bias.shape[1]
    unit = jax.ShapeDtypeStruct((tokens, hidden), BF)
    here = pl.BlockSpec(memory_space=pltpu.VMEM)
    scratch = [] if parts is None else [
        pltpu.VMEM((width, hidden), BF),
        pltpu.VMEM((hidden, width), BF),
        pltpu.SemaphoreType.DMA((32,)),
    ]
    return pl.pallas_call(
        functools.partial(ffn_first_kernel, parts),
        out_shape=(
            unit,
            unit,
            jax.ShapeDtypeStruct((width, 2 * width), BF),
            jax.ShapeDtypeStruct((1, hidden), F32),
        ),
        in_specs=[here] * 4 + [here if parts is None else pl.BlockSpec(memory_space=pl.ANY)] * len(held),
        out_specs=(here,) * 4,
        scratch_shapes=scratch,
        compiler_params=pltpu.CompilerParams(vmem_limit_bytes=48 << 20),
        cost_estimate=pl.CostEstimate(
            flops=8 * tokens * width * hidden,
            transcendentals=2 * tokens * hidden,
            bytes_accessed=8 * width * hidden + 10 * tokens * width,
        ),
        name="ffn",
    )(normed, normed_t, grad_out, bias, *held)


def after_tokens(parts, held, acts, grads, features, out_t, dq_t, weights, keep, got, pair, rows, sums, biases, gpair):
    tokens, width = features.shape
    hidden = acts[0].shape[1]
    blocks = tokens // BLK

    def whole(rows, columns):
        return pl.BlockSpec((rows, columns), lambda i: (0, 0))

    def block(first, last, columns=width):
        return pl.BlockSpec((BLK, columns), lambda i: (jnp.clip(i - first, 0, last - first), 0))

    every, own, other = block(0, blocks - 1), block(0, blocks // 2 - 1), block(blocks // 2, blocks - 1)
    units = block(0, blocks - 1, hidden)
    across = pl.BlockSpec((HALF, BLK), lambda i: (0, i))
    side = jax.ShapeDtypeStruct((tokens // 2, width), F32)
    scratch = [pltpu.VMEM((128, width), F32)]
    if parts is not None:
        scratch += [
            pltpu.VMEM((2, width, hidden), BF),
            pltpu.VMEM((2, hidden, width), BF),
            pltpu.SemaphoreType.DMA((64,)),
        ]
    return pl.pallas_call(
        functools.partial(tokens_kernel, parts),
        out_shape=(side, side, side, side, jax.ShapeDtypeStruct((width, 2 * HD + 128), BF)),
        grid=(blocks,),
        in_specs=[
            units,
            units,
            units,
            units,
            every,
            across,
            across,
            whole(width, weights.shape[1]),
            whole(HALF, HALF),
            whole(HALF, HALF),
            own,
            whole(8, width),
            whole(16, width),
            whole(1, hidden),
            whole(1, hidden),
            whole(width, 2 * HD),
        ]
        + (
            [pl.BlockSpec((2, width, hidden), lambda i: (0, 0, 0))] * 2
            if parts is None
            else [pl.BlockSpec(memory_space=pl.ANY)] * 4
        ),
        out_specs=(own, other, own, other, whole(width, 2 * HD + 128)),
        scratch_shapes=scratch,
        compiler_params=pltpu.CompilerParams(
            dimension_semantics=("arbitrary",), vmem_limit_bytes=48 << 20
        ),
        cost_estimate=pl.CostEstimate(
            flops=8 * tokens * width * hidden + 4 * tokens * width * HALF,
            transcendentals=0,
            bytes_accessed=8 * width * hidden + 20 * tokens * width,
        ),
        name="after_tokens",
    )(
        *acts, *grads, features, out_t, dq_t, weights, keep, got, pair, rows, sums, *biases, gpair, *held
    )


def shards(
    tokens,
    segments,
    ln1_gain,
    ln1_bias,
    ln2_gain,
    ln2_bias,
    q_weight,
    q_bias,
    kv_weight,
    k_bias,
    out_weight,
    out_bias,
    up_weight,
    up_bias,
    down_weight,
    cotangent,
):
    core, chip = lax.axis_index("core"), lax.axis_index("chip")
    chips = lax.axis_size("rows") * lax.axis_size("chip")
    own = tokens.shape[1]
    both = 2 * own
    rows = q_weight.shape[0]
    hidden = up_bias.shape[0]
    half = hidden // 2
    back_chips = DOC // both
    own_tokens, own_grad = tokens[0], cotangent[0]

    def half_columns(array, which):
        return lax.dynamic_slice_in_dim(
            array, which * (array.shape[1] // 2), array.shape[1] // 2, 1
        )

    def first(which):
        return jnp.concatenate(
            [half_columns(q_weight, which), half_columns(out_weight, which), kv_weight], axis=1
        )

    up_blocks = up_weight

    def up_half(which):
        block = up_blocks.reshape(rows, chips, 2, 2, half)
        block = lax.dynamic_index_in_dim(block, which, 2, keepdims=False)
        return block.transpose(0, 2, 1, 3).reshape(rows, FF // 2)

    flat = (ln1_gain, ln1_bias, ln2_gain, ln2_bias, q_bias, out_bias)
    if square_line():
        vectors = jnp.concatenate(
            [vector.reshape(1, rows) for vector in flat] + [up_bias.reshape(hidden // rows, rows)]
        )
        vectors = jnp.pad(vectors, ((0, 16 - vectors.shape[0]), (0, 0)))
        mine, theirs = pack(q_weight, out_weight, kv_weight, vectors)
        attn_piece = by_core(core, mine, core_swap(theirs), 0)
        segments, up_blocks = after((segments, up_blocks), attn_piece)
        attn_line = jnp.concatenate(gather_line(attn_piece))
        attn_rows = gather_rows(attn_line)
        up_piece = by_core(core, up_half(core), core_swap(up_half(1 - core)), 0)
        ff_piece = jnp.concatenate([up_piece[:, :D], up_piece[:, D:], down_weight], axis=0)
        ff_line = gather_line(after(ff_piece, attn_line))
        other_tokens = core_swap(own_tokens)
        features = jnp.concatenate([own_tokens, other_tokens], axis=0)
        grad_out = jnp.concatenate([own_grad, core_swap(own_grad)], axis=0)
        attn_rows, grad_out, features = lax.optimization_barrier((attn_rows, grad_out, features))
    else:
        weights = gather_whole(by_core(core, first(core), core_swap(first(1 - core)), 0))
        every = ("rows", "chip", "core")
        table = lax.all_gather(jnp.stack(flat), every, axis=1, tiled=True).astype(F32)
        vector_rows = jnp.pad(table, ((0, 2), (0, 0)))
        bias = gather_whole(up_bias).astype(F32).reshape(chips, 2, half)
        hidden_bias = jnp.pad(bias.transpose(1, 0, 2).reshape(2, D), ((0, 6), (0, 0)))

    if not square_line():
        other_tokens = core_swap(own_tokens)
        features = jnp.concatenate([own_tokens, other_tokens], axis=0)
        grad_out = jnp.concatenate([own_grad, core_swap(own_grad)], axis=0)

    ids = lax.broadcasted_iota(jnp.int32, (MAX_SEGS, 1), 0)
    doc_starts = jnp.sum((segments < ids).astype(jnp.int32), axis=1, keepdims=True)
    first_place, second_place = (chip * 2 + core) * own, (chip * 2 + 1 - core) * own
    span = lax.broadcasted_iota(jnp.int32, (1, own), 1)
    places = jnp.concatenate([first_place + span, second_place + span], axis=1)
    segs = jnp.concatenate(
        [
            lax.dynamic_slice(segments, (0, first_place), (1, own)),
            lax.dynamic_slice(segments, (0, second_place), (1, own)),
        ],
        axis=1,
    )
    starts = jnp.sum(jnp.where(segs == ids, doc_starts, 0), axis=0, keepdims=True)
    relative = places - starts
    frequency = 10000.0 ** (-(jnp.arange(ROT // 2, dtype=F32) * 2.0 / ROT))
    angles = relative.astype(F32) * frequency[:, None]
    cosine, sine = jnp.cos(angles), jnp.sin(angles)
    window_start = (chip - back_chips) * both
    pos = jnp.concatenate(
        [starts - window_start, places - window_start, jnp.zeros((6, both), jnp.int32)], axis=0
    )
    firsts, lasts = pos[:, ::BLK], pos[:, BLK - 1 :: BLK]
    scal = jnp.concatenate(
        [
            core.reshape(1),
            jnp.stack([firsts[0] // BLK, lasts[1] // BLK + 1, lasts[0]], axis=1).reshape(-1),
        ]
    ).astype(jnp.int32)


    bias_column = k_bias.astype(F32)[:, None]
    if square_line():
        weights, vector_rows, hidden_bias, *fronts = front(
            attn_rows, own_tokens, other_tokens, bias_column, cosine, sine
        )
    else:
        fronts = front(
            (weights, vector_rows), own_tokens, other_tokens, bias_column, cosine, sine
        )
    normed_one, normed_two, normed_two_t, query_t, own_pairs, keep, send = fronts
    got = core_swap(send)
    mine = jnp.concatenate(
        [chip_shift(own_pairs, k, False) for k in range(back_chips, 0, -1)] + [own_pairs], axis=0
    )
    theirs = core_swap(mine)
    if square_line():
        ff_rows = gather_rows(after(jnp.concatenate(ff_line), attn_rows))

    heads = attention(scal, query_t, grad_out, keep, got, pos, cosine, sine, mine, theirs)
    if square_line():
        heads, ff_rows = lax.optimization_barrier((heads, ff_rows))
    out_t, grad_query_t, pair_mine, pair_theirs = heads
    pair_got = core_swap(pair_theirs)
    grad_query, proj_keep, proj_send, sums = after_heads(
        out_t, grad_query_t, normed_one, grad_out
    )
    proj_got = core_swap(proj_send)
    if square_line():
        pair_got, proj_got = after((pair_got, proj_got), sums)
        step = 2 * rows
        parts = [((i * step, step, 0), ((2 + i) * step, step, 1)) for i in range(2)] + [
            tuple((i * step, step, (i // 2, i % 2)) for i in range(4))
        ]
        held = [ff_rows] * 3
    else:
        up_whole = gather_whole(by_core(core, up_half(core), core_swap(up_half(1 - core)), 0))
        down_whole = gather_whole(down_weight).reshape(chips, 2, half, D)
        down_whole = down_whole.transpose(1, 0, 2, 3).reshape(2, D, D)
        parts = [None] * 3
        ups = jnp.stack([up_whole[:, :D], up_whole[:, D:]])
        held = [(ups[0], down_whole[0]), (ups[1], down_whole[1]), (ups, down_whole)]
    pair_sum = pair_mine + pair_got
    arrived = [
        chip_shift(
            pair_sum[(back_chips - k) * own : (back_chips - k + 1) * own].astype(BF), -k, False
        )
        for k in range(1, back_chips + 1)
    ]
    grad_proj = by_core(core, proj_keep, proj_got, 0)
    attn_terms = jnp.concatenate([grad_query, grad_proj], axis=1)
    if square_line():
        attn_plane, attn_one = reduce_rows(attn_terms)
    grad_pair, grad_one_pair, key_bias = after_pairs(
        pair_sum, *arrived, normed_one, weights, cosine, sine
    )
    key_bias = key_bias[0, :HD]

    inputs = (normed_two, normed_two_t, grad_out)
    act0, dz0, terms0, bias0 = feed_forward(*inputs, hidden_bias[0:1], parts[0], held[0])
    if square_line():
        (act0, dz0, terms0, bias0), attn_one, grad_pair, grad_one_pair, key_bias = lax.optimization_barrier(
            ((act0, dz0, terms0, bias0), attn_one, grad_pair, grad_one_pair, key_bias)
        )
        planes0, one0 = reduce_first(terms0)
        other_bias = core_swap(key_bias)
    act1, dz1, terms1, bias1 = feed_forward(*inputs, hidden_bias[1:2], parts[1], held[1])
    if square_line():
        (act1, dz1, terms1, bias1), one0, other_bias = lax.optimization_barrier(
            ((act1, dz1, terms1, bias1), one0, other_bias)
        )
        two0 = reduce_second(planes0, one0)
        planes1, one1 = reduce_first(terms1)
        key_bias = key_bias + other_bias
        other_bias = line_swap(key_bias, 1)
    part, part_send, scaled, scaled_send, small_terms = after_tokens(
        parts[2],
        held[2],
        (act0, act1),
        (dz0, dz1),
        features,
        out_t,
        grad_query_t,
        weights,
        keep,
        got,
        grad_one_pair,
        vector_rows,
        sums,
        (bias0, bias1),
        grad_pair,
    )
    if square_line():
        (part, part_send, scaled, scaled_send, small_terms), two0, one1, other_bias = (
            lax.optimization_barrier(
                ((part, part_send, scaled, scaled_send, small_terms), two0, one1, other_bias)
            )
        )
        key_bias = key_bias + other_bias
    part_got, scaled_got = core_swap(part_send), core_swap(scaled_send)

    def finish(part_got, scaled_got):
        layer_out = own_tokens.astype(F32) + part + part_got + vector_rows[5:6]
        total = scaled + scaled_got
        unit, spread = standard(own_tokens)
        input_grad = own_grad.astype(F32) + spread * (
            total
            - jnp.mean(total, axis=-1, keepdims=True)
            - unit * jnp.mean(total * unit, axis=-1, keepdims=True)
        )
        return layer_out.astype(BF), input_grad

    def split(value):
        return (
            lax.dynamic_slice_in_dim(value, core * rows, rows, 0),
            core_swap(lax.dynamic_slice_in_dim(value, (1 - core) * rows, rows, 0)),
        )

    def blocks(first_half, second_half):
        return jnp.stack(
            [value.reshape(rows, chips, half) for value in (first_half, second_half)], axis=2
        ).reshape(rows, chips, 1, hidden)

    if square_line():
        small_grid = small_terms.reshape((4, 4, small_terms.shape[0] // 16) + small_terms.shape[1:])
        row = lax.axis_index("rows")
        small_planes = [
            lax.dynamic_index_in_dim(small_grid, row ^ bit, 0, keepdims=False) for bit in range(4)
        ]
        two1 = reduce_second(planes1, one1, small_planes)
        own0, three0 = reduce_third((planes0[0], *two0), (attn_plane, *attn_one))
        small_far = rows_swap(after(small_planes[3], part_got), 3)
        layer_out, input_grad = finish(part_got, scaled_got)
        other_bias = line_swap(after(key_bias, part_got), 2)
        two1, three0, small_far, layer_out, input_grad, other_bias = lax.optimization_barrier(
            (two1, three0, small_far, layer_out, input_grad, other_bias)
        )
        key_bias = key_bias + other_bias
        own1, three1 = reduce_third(
            (planes1[0], *(part[:, :, : 2 * D] for part in two1)),
            (small_planes[0], small_far, *(part[:, :, 2 * D :] for part in two1)),
        )
        other_bias = rows_swap(after(key_bias, two1), 1)
        key_bias = key_bias + other_bias
        sum0 = reduce_last(own0, three0)
        sum0, attn_sum = sum0[:, : 2 * D], sum0[:, 2 * D :]
        attn_split = split(after(attn_sum, other_bias))
        up_split = split(after(sum0, other_bias)[:, :D])
        key_bias_out = key_bias + rows_swap(key_bias, 2)
        mine, theirs = attn_split
        query_out = by_core(core, mine[:, :HALF], theirs[:, :HALF], 1)
        proj_out = by_core(core, mine[:, HALF:], theirs[:, HALF:], 1)
        three1, up_split, query_out, proj_out, key_bias_out = lax.optimization_barrier(
            (three1, up_split, query_out, proj_out, key_bias_out)
        )
        sum1 = reduce_last(own1, three1)
        sum1, small_sum = sum1[:, : 2 * D], sum1[:, 2 * D :]
    else:
        layer_out, input_grad = finish(part_got, scaled_got)
        sum0, sum1, small_sum = (reduce_whole(terms) for terms in (terms0, terms1, small_terms))
        up_split = split(sum0[:, :D])
        mine, theirs = split(reduce_whole(attn_terms))
        query_out = by_core(core, mine[:, :HALF], theirs[:, :HALF], 1)
        proj_out = by_core(core, mine[:, HALF:], theirs[:, HALF:], 1)
        key_bias_out = lax.psum(key_bias, ("rows", "chip", "core"))
    mine, theirs = split(jnp.concatenate([sum1[:, :D], small_sum], axis=1))
    rest = mine[:, D:] + theirs[:, D:]
    pair_out, vector_out = rest[:, : 2 * HD], rest[:, 2 * HD :]
    up_bias_out = small_sum[:, 2 * HD + 6 : 2 * HD + 8].T.reshape(hidden)
    up_out = by_core(
        core, blocks(up_split[0], mine[:, :D]), blocks(up_split[1], theirs[:, :D]), 2
    ).reshape(rows, FF)
    down_out = jnp.concatenate([sum0[:, D:], sum1[:, D : 2 * D]], axis=0)
    return (
        layer_out[None],
        input_grad[None],
        vector_out[:, 0],
        vector_out[:, 1],
        vector_out[:, 2],
        vector_out[:, 3],
        query_out,
        vector_out[:, 4],
        pair_out,
        key_bias_out,
        proj_out,
        vector_out[:, 5],
        up_out,
        up_bias_out,
        down_out,
    )


def solution(mesh):
    devices = mesh.devices.reshape(mesh.shape["rows"], mesh.shape["wide"] // 2, 2)
    every, wide = ("rows", "chip", "core"), ("chip", "core")
    matrix, vector, sequence = P(every, None), P(every), P("rows", wide, None)
    return jax.shard_map(
        shards,
        mesh=Mesh(devices, every),
        in_specs=(
            sequence,
            P("rows", None),
            vector,
            vector,
            vector,
            vector,
            matrix,
            vector,
            matrix,
            P(),
            matrix,
            vector,
            matrix,
            vector,
            matrix,
            sequence,
        ),
        out_specs=(
            sequence,
            sequence,
            vector,
            vector,
            vector,
            vector,
            matrix,
            vector,
            matrix,
            P(),
            matrix,
            vector,
            matrix,
            vector,
            matrix,
        ),
        check_vma=False,
    )
```

```python
import functools
import math

import jax
import jax.numpy as jnp
from jax import lax
from jax.experimental import pallas as pl
from jax.experimental.pallas import tpu as pltpu
from jax.sharding import Mesh, PartitionSpec as P

D = 768
HEADS = 12
HD = 64
ROT = 16
DOC = 2048
FF = 3072
MAX_SEGS = 32
norm_eps = 1e-05
BF = jnp.bfloat16
F32 = jnp.float32
HALF = HEADS // 2 * HD
BLK = 256
GROUP = 6


def dot(left, right, dims):
    return lax.dot_general(left, right, (dims, ((), ())), preferred_element_type=F32)


def core_swap(value):
    return lax.ppermute(value, "core", [(0, 1), (1, 0)])


def rows_swap(value, bit):
    return lax.ppermute(value, "rows", [(r, r ^ bit) for r in range(4)])


def chip_shift(value, by, wrap):
    count = lax.axis_size("chip")
    pairs = [(s, (s + by) % count) for s in range(count) if wrap or 0 <= s + by < count]
    return lax.ppermute(value, "chip", pairs)


def square_line():
    return lax.axis_size("rows") == 4 and lax.axis_size("chip") == 4


def place_copies(parts, sources, outs, sems):
    row, chip = lax.axis_index("rows"), lax.axis_index("chip")
    size = sources[0].shape[0] // 4
    copies = []
    for first, count, out in parts:
        for turn, source in enumerate(sources):
            for step in range(4):
                place = (row ^ turn) * 4 + lax.rem(chip + step, 4)
                copies.append(
                    pltpu.make_async_copy(
                        source.at[pl.ds(step * size + first, count)],
                        outs[out].at[pl.ds(pl.multiple_of(place * count, 8), count)]
                        if isinstance(out, int)
                        else outs[out[0]].at[out[1], pl.ds(pl.multiple_of(place * count, 8), count)],
                        sems.at[len(copies)],
                    )
                )
    return copies


def gather_line(piece):
    return [piece] + [chip_shift(piece, -k, True) for k in (1, 2, 3)]


def gather_rows(lines):
    return lines, rows_swap(lines, 1), rows_swap(lines, 2), rows_swap(lines, 3)


def gather_whole(piece):
    return lax.all_gather(piece, ("rows", "chip"), axis=0, tiled=True)


def reduce_first(terms):
    row = lax.axis_index("rows")
    grid = terms.reshape((4, 4, terms.shape[0] // 16) + terms.shape[1:])
    planes = [lax.dynamic_index_in_dim(grid, row ^ bit, 0, keepdims=False) for bit in range(4)]
    return planes, (rows_swap(planes[3][:2], 1), rows_swap(planes[3][2:], 2))


def reduce_rows(terms):
    row = lax.axis_index("rows")
    grid = terms.reshape((4, 4, terms.shape[0] // 16) + terms.shape[1:])
    planes = [lax.dynamic_index_in_dim(grid, row ^ bit, 0, keepdims=False) for bit in range(4)]
    return planes[0], [rows_swap(planes[bit], bit) for bit in (3, 1, 2)]


def reduce_second(planes, arrived, beside=None):
    _, flat, cross, _ = planes
    from_flat, from_cross = arrived
    to_flat = jnp.concatenate(
        [flat[:2], (flat[2:].astype(F32) + from_cross.astype(F32)).astype(BF)], axis=0
    )
    to_cross = jnp.concatenate(
        [(cross[:2].astype(F32) + from_flat.astype(F32)).astype(BF), cross[2:]], axis=0
    )
    if beside is not None:
        to_flat = jnp.concatenate([to_flat, beside[1]], axis=2)
        to_cross = jnp.concatenate([to_cross, beside[2]], axis=2)
    return rows_swap(to_flat, 1), rows_swap(to_cross, 2)


def reduce_third(*groups):
    chip = lax.axis_index("chip")

    def line(step):
        spot = lax.rem(chip + step, 4)
        sums = []
        for group in groups:
            pick = [
                lax.dynamic_index_in_dim(part, spot, 0, keepdims=False).astype(F32)
                for part in group
            ]
            sums.append(sum(pick[1:], pick[0]))
        return jnp.concatenate(sums, axis=1)

    return line(0), [chip_shift(line(step).astype(BF), step, True) for step in (1, 2, 3)]


def reduce_last(own, arrived):
    return own + arrived[0].astype(F32) + arrived[1].astype(F32) + arrived[2].astype(F32)


def reduce_whole(terms):
    return lax.psum_scatter(terms.astype(F32), ("rows", "chip"), scatter_dimension=0, tiled=True)


def after(value, *others):
    return lax.optimization_barrier((value, others))[0]


def line_swap(value, bit):
    return lax.ppermute(value, "chip", [(s, s ^ bit) for s in range(4)])


def by_core(core, own, other, axis):
    return jnp.where(
        core == 0,
        jnp.concatenate([own, other], axis=axis),
        jnp.concatenate([other, own], axis=axis),
    )


def pack_kernel(q_ref, out_ref, kv_ref, vectors_ref, mine_ref, theirs_ref):
    core = lax.axis_index("core")
    rows = q_ref.shape[0]
    pick = lax.broadcasted_iota(jnp.int32, (16, 128), 0) == lax.broadcasted_iota(
        jnp.int32, (16, 128), 1
    )
    columns = dot(vectors_ref[...], jnp.where(pick, 1.0, 0.0).astype(BF), ((0,), (0,))).astype(BF)
    for which, ref in ((core, mine_ref), (1 - core, theirs_ref)):
        spot = pl.ds(pl.multiple_of(which * HALF, HALF), HALF)
        ref[:, :HALF] = q_ref[:, spot]
        ref[:, HALF : 2 * HALF] = out_ref[:, spot]
        ref[:, 2 * HALF : 2 * HALF + 2 * HD] = kv_ref[...]
        ref[:, 2 * HALF + 2 * HD :] = columns


def pack(q_weight, out_weight, kv_weight, vectors):
    rows = q_weight.shape[0]
    side = jax.ShapeDtypeStruct((rows, 2 * HALF + 2 * HD + 128), BF)
    return pl.pallas_call(
        pack_kernel,
        out_shape=(side, side),
        cost_estimate=pl.CostEstimate(flops=0, transcendentals=0, bytes_accessed=8 * rows * D),
        name="pack",
    )(q_weight, out_weight, kv_weight, vectors)


def turn(values, cosine, sine, direction):
    half = ROT // 2
    a, b = values[:half, :], values[half:ROT, :]
    return jnp.concatenate(
        [a * cosine - direction * b * sine, b * cosine + direction * a * sine, values[ROT:, :]],
        axis=0,
    )


def standard(tokens):
    values = tokens.astype(F32)
    center = values - jnp.mean(values, axis=-1, keepdims=True)
    spread = lax.rsqrt(jnp.mean(center * center, axis=-1, keepdims=True) + norm_eps)
    return center * spread, spread


def front_rest(
    own_ref, other_ref, kbias_ref, cos_ref, sin_ref, w_ref, rows_ref,
    h1_ref, h2_ref, h2t_ref, q_ref, pairs_ref, keep_ref, send_ref,
):
    core = lax.axis_index("core")
    count = own_ref.shape[0]
    gain_one, shift_one, gain_two, shift_two = (rows_ref[i : i + 1, :] for i in range(4))

    def norm(part, ref):
        unit, _ = standard(ref[...])
        spot = pl.ds(part * count, count)
        h1_ref[spot, :] = (unit * gain_one + shift_one).astype(BF)
        normed = (unit * gain_two + shift_two).astype(BF)
        h2_ref[spot, :] = normed
        h2t_ref[:, part * count : (part + 1) * count] = normed.T

    norm(0, own_ref)
    pair = dot(w_ref[:, 2 * HALF : 2 * HALF + 2 * HD], h1_ref[:count, :], ((0,), (1,)))
    key = turn(
        pair[:HD] + kbias_ref[...], cos_ref[:, :count], sin_ref[:, :count], 1.0
    ).astype(BF)
    pairs_ref[...] = jnp.concatenate([key, pair[HD:].astype(BF)], axis=0).T
    norm(1, other_ref)
    query = dot(w_ref[:, :HALF], h1_ref[...], ((0,), (1,)))
    bias = jnp.where(core == 0, rows_ref[4:5, :HALF], rows_ref[4:5, HALF:])
    query = query + jnp.broadcast_to(bias, (8, HALF)).T[:, :1]
    for h in range(HEADS // 2):
        q_ref[h * HD : (h + 1) * HD, :] = turn(
            query[h * HD : (h + 1) * HD, :], cos_ref[...], sin_ref[...], 1.0
        ).astype(BF)
    for index, ref in ((core, keep_ref), (1 - core, send_ref)):
        spot = pl.ds(pl.multiple_of(index * HALF, HALF), HALF)
        ref[...] = w_ref[spot, HALF : 2 * HALF]


def front_kernel(
    lines_ref, flat_ref, cross_ref, far_ref, own_ref, other_ref, kbias_ref, cos_ref, sin_ref,
    w_ref, rows_ref, bias_ref, h1_ref, h2_ref, h2t_ref, q_ref, pairs_ref, keep_ref, send_ref, sems,
):
    core = lax.axis_index("core")
    copies = place_copies(
        ((0, w_ref.shape[0] // 16, 0),), (lines_ref, flat_ref, cross_ref, far_ref), (w_ref,), sems
    )
    for copy in copies:
        copy.start()
    for copy in copies:
        copy.wait()
    table = w_ref[:, 2 * HALF + 2 * HD :].astype(F32).T
    rows_ref[...] = table[:8, :]
    half = lax.rem(lax.broadcasted_iota(jnp.int32, (1, D), 1), 48) // 24
    for k in range(2):
        low, high = table[6 + 2 * k : 7 + 2 * k, :], table[7 + 2 * k : 8 + 2 * k, :]
        first = jnp.where(half == 0, low, pltpu.roll(jnp.broadcast_to(high, (8, D)), 24, 1)[:1])
        second = jnp.where(
            half == 1, high, pltpu.roll(jnp.broadcast_to(low, (8, D)), D - 24, 1)[:1]
        )
        bias_ref[k : k + 1, :] = jnp.where(core == 0, first, second)
    bias_ref[2:8, :] = jnp.zeros((6, D), F32)
    front_rest(
        own_ref, other_ref, kbias_ref, cos_ref, sin_ref, w_ref, rows_ref,
        h1_ref, h2_ref, h2t_ref, q_ref, pairs_ref, keep_ref, send_ref,
    )


def front_plain_kernel(
    w_ref, rows_ref, own_ref, other_ref, kbias_ref, cos_ref, sin_ref, *outs
):
    front_rest(own_ref, other_ref, kbias_ref, cos_ref, sin_ref, w_ref, rows_ref, *outs)


def front(pieces, own, other, k_bias, cosine, sine):
    both = 2 * own.shape[0]
    placed = len(pieces) == 4
    wide = pieces[0].shape[1]
    shapes = (
        jax.ShapeDtypeStruct((both, D), BF),
        jax.ShapeDtypeStruct((both, D), BF),
        jax.ShapeDtypeStruct((D, both), BF),
        jax.ShapeDtypeStruct((HALF, both), BF),
        jax.ShapeDtypeStruct((own.shape[0], 2 * HD), BF),
        jax.ShapeDtypeStruct((HALF, HALF), BF),
        jax.ShapeDtypeStruct((HALF, HALF), BF),
    )
    here = pl.BlockSpec(memory_space=pltpu.VMEM)
    if placed:
        shapes = (
            jax.ShapeDtypeStruct((D, wide), BF),
            jax.ShapeDtypeStruct((8, D), F32),
            jax.ShapeDtypeStruct((8, D), F32),
        ) + shapes
    return pl.pallas_call(
        front_kernel if placed else front_plain_kernel,
        out_shape=shapes,
        in_specs=[pl.BlockSpec(memory_space=pl.ANY) if placed else here] * len(pieces) + [here] * 5,
        out_specs=tuple(here for _ in shapes),
        scratch_shapes=[pltpu.SemaphoreType.DMA((16,))] if placed else [],
        compiler_params=pltpu.CompilerParams(vmem_limit_bytes=48 << 20),
        cost_estimate=pl.CostEstimate(
            flops=2 * both * D * (HALF + 2 * HD), transcendentals=both, bytes_accessed=8 * both * D
        ),
        name="front",
    )(*pieces, own, other, k_bias, cosine, sine)


def attn_kernel(
    scal_ref, q_ref, grad_ref, keep_in_ref, got_in_ref, pos_ref, cos_ref, sin_ref, mine_ref, theirs_ref,
    o_ref, dq_ref, dmine_ref, dtheirs_ref,
    keep_ref, got_ref, kv_ref, kvt_ref, dkv_ref, g_ref, s_ref, r_ref, rt_ref, sems,
):
    block = pl.program_id(0)
    core = scal_ref[0]
    low, high, edge = (scal_ref[1 + 3 * block + i] for i in range(3))
    wide = GROUP * BLK
    half = kv_ref.shape[0] // 2
    own_blocks = pl.num_programs(0) // 2

    @pl.when(block == 0)
    def _():
        dkv_ref[...] = jnp.zeros_like(dkv_ref)
        copies = [
            pltpu.make_async_copy(source, target, sems.at[i])
            for i, (source, target) in enumerate(
                (
                    (mine_ref, kv_ref.at[pl.ds(0, half)]),
                    (theirs_ref, kv_ref.at[pl.ds(half, half)]),
                    (keep_in_ref, keep_ref),
                    (got_in_ref, got_ref),
                )
            )
        ]
        for copy in copies:
            copy.start()
        for copy in copies:
            copy.wait()
        for part in range(2):
            kvt_ref[: 2 * HD, part * half : (part + 1) * half] = kv_ref[
                part * half : (part + 1) * half, :
            ].T
        kvt_ref[2 * HD :, :] = jnp.ones((16, 2 * half), BF)

    def spot(key_block):
        side = lax.rem(key_block // own_blocks, 2) ^ core
        place = (key_block // (2 * own_blocks)) * own_blocks + lax.rem(key_block, own_blocks)
        return pl.multiple_of(side * half + place * BLK, BLK)

    first, pairs_end, single = low // 2, high // 2, lax.rem(high, 2)
    last = pairs_end - 1 + single
    clear = jnp.clip((edge + 2 * BLK - 1) // (2 * BLK), first, last)

    def slot(key_block, size):
        return pl.ds(pl.multiple_of((key_block - 2 * first) * BLK, BLK), size)

    def over_keys(body, carry):
        def double(masked):
            return lambda i, c: body(masked, 2 * i, 2 * BLK, c)

        carry = lax.fori_loop(first, clear, double(True), carry)
        carry = lax.fori_loop(clear, last, double(False), carry)
        carry = lax.fori_loop(last, pairs_end, double(True), carry)
        return lax.fori_loop(
            0, single, lambda i, c: body(True, 2 * pairs_end + i, BLK, c), carry
        )

    def over_all(body, carry):
        carry = lax.fori_loop(first, pairs_end, lambda i, c: body(2 * i, 2 * BLK, c), carry)
        return lax.fori_loop(0, single, lambda i, c: body(2 * pairs_end + i, BLK, c), carry)

    near = pl.ds(pl.multiple_of(core * HALF, HALF), HALF)
    away = pl.ds(pl.multiple_of((1 - core) * HALF, HALF), HALF)
    g_ref[...] = (
        dot(keep_ref[...], grad_ref[:, near], ((1,), (1,)))
        + dot(got_ref[...], grad_ref[:, away], ((1,), (1,)))
    ).astype(BF)
    starts = jnp.concatenate([pos_ref[0:1, :]] * GROUP, axis=1)
    places = jnp.concatenate([pos_ref[1:2, :]] * GROUP, axis=1)
    blank = jnp.zeros((HD, BLK), BF)
    for h in range(GROUP):
        query = (q_ref[h * HD : (h + 1) * HD, :].astype(F32) * HD**-0.5).astype(BF)
        grad = g_ref[h * HD : (h + 1) * HD, :]
        query = jnp.concatenate([query, blank], axis=0)
        grad = jnp.concatenate([blank, grad], axis=0)
        r_ref[0, :, h * BLK : (h + 1) * BLK] = query
        r_ref[1, :, h * BLK : (h + 1) * BLK] = grad
        rt_ref[h * BLK : (h + 1) * BLK, :] = query.T
        rt_ref[(GROUP + h) * BLK : (GROUP + h + 1) * BLK, :] = grad.T

    def scores(masked, key_block, size, peak):
        keys = kv_ref[pl.ds(spot(key_block), size), :]
        s = dot(keys, r_ref[0], ((1,), (0,)))
        if masked:
            key_places = key_block * BLK + lax.broadcasted_iota(jnp.int32, (size, wide), 0)
            s = jnp.where((key_places >= starts) & (key_places <= places), s, -1e30)
        s_ref[slot(key_block, size), :] = s
        return jnp.maximum(peak, jnp.max(s, axis=0, keepdims=True))

    peak = over_keys(scores, jnp.full((1, wide), -1e30, F32))

    def expo(key_block, size, out):
        values = kvt_ref[HD:, pl.ds(spot(key_block), size)]
        e = jnp.exp(s_ref[slot(key_block, size), :] - peak)
        s_ref[slot(key_block, size), :] = e
        return out + dot(values, e.astype(BF), ((1,), (0,)))

    out = over_all(expo, jnp.zeros((HD + 16, wide), F32))
    inverse = 1.0 / out[HD : HD + 1, :]
    out = out[:HD] * inverse
    deltas = []
    for h in range(GROUP):
        part = out[:, h * BLK : (h + 1) * BLK]
        o_ref[h * HD : (h + 1) * HD, :] = part.astype(BF)
        deltas.append(
            jnp.sum(part * g_ref[h * HD : (h + 1) * HD, :].astype(F32), axis=0, keepdims=True)
        )
    delta = jnp.concatenate(deltas, axis=1)

    def back(key_block, size, dq):
        where = spot(key_block)
        pairs = kv_ref[pl.ds(where, size), :]
        keys = kvt_ref[:HD, pl.ds(where, size)]
        p = s_ref[slot(key_block, size), :] * inverse
        dp = dot(pairs, r_ref[1], ((1,), (0,)))
        ds = (p * (dp - delta)).astype(BF)
        left = jnp.concatenate([ds, p.astype(BF)], axis=1)
        dkv_ref[pl.ds(where, size), :] += dot(left, rt_ref[...], ((1,), (0,)))
        return dq + dot(keys, ds, ((1,), (0,)))

    dq = over_all(back, jnp.zeros((HD, wide), F32)) * HD**-0.5
    for h in range(GROUP):
        part = dq[:, h * BLK : (h + 1) * BLK].astype(BF).astype(F32)
        dq_ref[h * HD : (h + 1) * HD, :] = turn(part, cos_ref[...], sin_ref[...], -1.0).astype(BF)

    @pl.when(block == pl.num_programs(0) - 1)
    def _():
        dmine_ref[...] = dkv_ref[:half, :]
        dtheirs_ref[...] = dkv_ref[half:, :]


def attention(scal, query_t, grad_out, keep, got, pos, cosine, sine, mine, theirs):
    features, tokens = query_t.shape
    blocks, half = tokens // BLK, mine.shape[0]
    tile = pl.BlockSpec((features, BLK), lambda b, s: (0, b))
    small = pl.BlockSpec((8, BLK), lambda b, s: (0, b))

    def whole(rows, columns):
        return pl.BlockSpec((rows, columns), lambda b, s: (0, 0))

    return pl.pallas_call(
        attn_kernel,
        out_shape=(
            jax.ShapeDtypeStruct((features, tokens), BF),
            jax.ShapeDtypeStruct((features, tokens), BF),
            jax.ShapeDtypeStruct((half, 2 * HD), F32),
            jax.ShapeDtypeStruct((half, 2 * HD), F32),
        ),
        grid_spec=pltpu.PrefetchScalarGridSpec(
            num_scalar_prefetch=1,
            grid=(blocks,),
            in_specs=[
                tile,
                pl.BlockSpec((BLK, D), lambda b, s: (b, 0)),
                pl.BlockSpec(memory_space=pltpu.HBM),
                pl.BlockSpec(memory_space=pltpu.HBM),
                small,
                small,
                small,
                pl.BlockSpec(memory_space=pltpu.HBM),
                pl.BlockSpec(memory_space=pltpu.HBM),
            ],
            out_specs=(tile, tile, whole(half, 2 * HD), whole(half, 2 * HD)),
            scratch_shapes=[
                pltpu.VMEM((HALF, HALF), BF),
                pltpu.VMEM((HALF, HALF), BF),
                pltpu.VMEM((2 * half, 2 * HD), BF),
                pltpu.VMEM((2 * HD + 16, 2 * half), BF),
                pltpu.VMEM((2 * half, 2 * HD), F32),
                pltpu.VMEM((features, BLK), BF),
                pltpu.VMEM((DOC + 2 * BLK, GROUP * BLK), F32),
                pltpu.VMEM((2, 2 * HD, GROUP * BLK), BF),
                pltpu.VMEM((2 * GROUP * BLK, 2 * HD), BF),
                pltpu.SemaphoreType.DMA((4,)),
            ],
        ),
        compiler_params=pltpu.CompilerParams(
            dimension_semantics=("arbitrary",), vmem_limit_bytes=36 << 20
        ),
        cost_estimate=pl.CostEstimate(
            flops=12 * features * tokens * DOC * 3 // 4,
            transcendentals=features // HD * tokens * DOC * 3 // 4,
            bytes_accessed=8 * features * tokens,
        ),
        name="attention",
    )(scal, query_t, grad_out, keep, got, pos, cosine, sine, mine, theirs)


def heads_kernel(
    o_ref, dq_ref, h1_ref, grad_ref, gq_ref, keep_out_ref, send_out_ref, sums_ref
):
    core = lax.axis_index("core")
    near = pl.ds(pl.multiple_of(core * HALF, HALF), HALF)
    away = pl.ds(pl.multiple_of((1 - core) * HALF, HALF), HALF)
    send_out_ref[...] = dot(o_ref[...], grad_ref[:, away], ((1,), (0,))).astype(BF)
    keep_out_ref[...] = dot(o_ref[...], grad_ref[:, near], ((1,), (0,))).astype(BF)
    gq_ref[...] = dot(dq_ref[...], h1_ref[...], ((1,), (0,))).T.astype(BF)
    ones = jnp.ones((8, dq_ref.shape[1]), BF)
    sums_ref[...] = jnp.zeros_like(sums_ref)
    sums_ref[0:8, near] = dot(ones, dq_ref[...], ((1,), (1,)))
    count = grad_ref.shape[0] // 2
    sums_ref[8:16, :] = dot(ones[:, :count], grad_ref[:count, :], ((1,), (0,)))


def after_heads(out_t, dq_t, normed, grad_out):
    both = normed.shape[0]
    return pl.pallas_call(
        heads_kernel,
        out_shape=(
            jax.ShapeDtypeStruct((D, HALF), BF),
            jax.ShapeDtypeStruct((HALF, HALF), BF),
            jax.ShapeDtypeStruct((HALF, HALF), BF),
            jax.ShapeDtypeStruct((16, D), F32),
        ),
        compiler_params=pltpu.CompilerParams(vmem_limit_bytes=48 << 20),
        cost_estimate=pl.CostEstimate(
            flops=4 * both * D * HALF, transcendentals=0, bytes_accessed=6 * both * D
        ),
        name="after_heads",
    )(out_t, dq_t, normed, grad_out)


def pairs_kernel(
    own_ref, near_ref, far_ref, h1_ref, w_ref, cos_ref, sin_ref, gw_ref, dh_ref, gbias_ref
):
    total = own_ref[...] + near_ref[...].astype(F32) + far_ref[...].astype(F32)
    total = total.astype(BF).astype(F32).T
    key = turn(total[:HD], cos_ref[...], sin_ref[...], -1.0)
    grad = jnp.concatenate([key, total[HD:]], axis=0).astype(BF)
    gw_ref[...] = dot(grad, h1_ref[...], ((1,), (0,))).T.astype(BF)
    dh_ref[...] = dot(grad.T, w_ref[:, 2 * HALF : 2 * HALF + 2 * HD], ((1,), (1,)))
    ones = jnp.ones((8, grad.shape[1]), BF)
    gbias_ref[...] = dot(ones, grad, ((1,), (1,)))


def after_pairs(pairs, near, far, normed, weights, cosine, sine):
    count = near.shape[0]

    def whole(rows, columns):
        return pl.BlockSpec((rows, columns), lambda i: (0, 0))

    return pl.pallas_call(
        pairs_kernel,
        out_shape=(
            jax.ShapeDtypeStruct((D, 2 * HD), BF),
            jax.ShapeDtypeStruct((count, D), F32),
            jax.ShapeDtypeStruct((8, 2 * HD), F32),
        ),
        grid=(1,),
        in_specs=[
            pl.BlockSpec((count, 2 * HD), lambda i: (pairs.shape[0] // count - 1, 0)),
            whole(count, 2 * HD),
            whole(count, 2 * HD),
            whole(count, D),
            whole(D, weights.shape[1]),
            whole(8, count),
            whole(8, count),
        ],
        out_specs=(whole(D, 2 * HD), whole(count, D), whole(8, 2 * HD)),
        compiler_params=pltpu.CompilerParams(vmem_limit_bytes=32 << 20),
        cost_estimate=pl.CostEstimate(
            flops=8 * count * D * HD, transcendentals=0, bytes_accessed=8 * count * D
        ),
        name="after_pairs",
    )(pairs, near, far, normed, weights, cosine, sine)


def ffn_units(
    placed, h_ref, ht_ref, g_ref, bias_ref, up_ref, down_ref, grad_ref, act_ref, dz_ref
):
    for copy in placed:
        copy.start()
    for copy in placed[:16]:
        copy.wait()
    z = dot(h_ref[...], up_ref[...], ((1,), (0,))) + bias_ref[...]
    below = 0.5 * (1.0 + lax.erf(z * 0.5**0.5))
    slope = below + z * (jnp.exp(-0.5 * z * z) * (0.5 / math.pi) ** 0.5)
    act = (z * below).astype(BF)
    grad_ref[:, D : 2 * D] = dot(act, g_ref[...], ((0,), (0,))).astype(BF)
    act_ref[...] = act
    for copy in placed[16:]:
        copy.wait()
    grad = (dot(g_ref[...], down_ref[...], ((1,), (1,))) * slope).astype(BF)
    dz_ref[...] = grad
    grad_ref[:, :D] = dot(ht_ref[...], grad, ((1,), (0,))).astype(BF)
    return jnp.sum(grad.astype(F32), axis=0, keepdims=True)


def ffn_weights(parts, rest):
    if parts is None:
        return (), rest[0], rest[1], rest[2:]
    up_ref, down_ref, sems = rest[-3:]
    return place_copies(parts, rest[:4], (up_ref, down_ref), sems), up_ref, down_ref, rest[4:-3]


def ffn_first_kernel(parts, h_ref, ht_ref, g_ref, bias_ref, *rest):
    placed, up_ref, down_ref, rest = ffn_weights(parts, rest)
    act_ref, dz_ref, grad_ref, gbias_ref = rest
    gbias_ref[...] = ffn_units(
        placed, h_ref, ht_ref, g_ref, bias_ref, up_ref, down_ref, grad_ref, act_ref, dz_ref
    )


def tokens_kernel(
    parts, act0_ref, act1_ref, dz0_ref, dz1_ref, x_ref, o_ref, dq_ref, w_ref, out_keep_ref, out_got_ref,
    pair_ref, rows_ref, sums_ref, bias0_ref, bias1_ref, gpair_ref, *rest
):
    placed, up_ref, down_ref, rest = ffn_weights(parts, rest)
    keep_ref, send_ref, tkeep_ref, tsend_ref, small_ref, table_ref = rest
    step = pl.program_id(0)
    core = lax.axis_index("core")
    blocks = pl.num_programs(0)

    @pl.when(step == 0)
    def _():
        for copy in placed:
            copy.start()
        table_ref[...] = jnp.zeros_like(table_ref)
        table_ref[4:5, :] = sums_ref[0:1, :]
        table_ref[5:6, :] = sums_ref[8:9, :]
        table_ref[6:7, :] = bias0_ref[...]
        table_ref[7:8, :] = bias1_ref[...]
        small_ref[:, : 2 * HD] = gpair_ref[...]
        for copy in placed:
            copy.wait()

    def tokens(first):
        heads = o_ref[...].T
        near = dot(heads, out_keep_ref[...], ((1,), (0,)))
        away = dot(heads, out_got_ref[...], ((1,), (0,)))
        low, high = jnp.where(core == 0, near, away), jnp.where(core == 0, away, near)
        out = dot(act0_ref[...], down_ref[0], ((1,), (0,))) + dot(
            act1_ref[...], down_ref[1], ((1,), (0,))
        )
        out = out + jnp.concatenate([low, high], axis=1)
        two = dot(dz0_ref[...], up_ref[0], ((1,), (1,))) + dot(
            dz1_ref[...], up_ref[1], ((1,), (1,))
        )
        one = dot(dq_ref[...].T, w_ref[:, :HALF], ((1,), (1,)))
        if first:
            one = one + pair_ref[...]
        unit, _ = standard(x_ref[...])
        scaled = one * rows_ref[0:1, :] + two * rows_ref[2:3, :]
        refs = (keep_ref, tkeep_ref) if first else (send_ref, tsend_ref)
        refs[0][...], refs[1][...] = out, scaled
        for i, value in enumerate((one * unit, one, two * unit, two)):
            table_ref[i : i + 1, :] += jnp.sum(value, axis=0, keepdims=True)

    @pl.when(step < blocks // 2)
    def _():
        tokens(True)

    @pl.when(step >= blocks // 2)
    def _():
        tokens(False)

    @pl.when(step == blocks - 1)
    def _():
        small_ref[:, 2 * HD :] = table_ref[...].T.astype(BF)


def feed_forward(normed, normed_t, grad_out, bias, parts, held):
    tokens, width = normed.shape
    hidden = bias.shape[1]
    unit = jax.ShapeDtypeStruct((tokens, hidden), BF)
    here = pl.BlockSpec(memory_space=pltpu.VMEM)
    scratch = [] if parts is None else [
        pltpu.VMEM((width, hidden), BF),
        pltpu.VMEM((hidden, width), BF),
        pltpu.SemaphoreType.DMA((32,)),
    ]
    return pl.pallas_call(
        functools.partial(ffn_first_kernel, parts),
        out_shape=(
            unit,
            unit,
            jax.ShapeDtypeStruct((width, 2 * width), BF),
            jax.ShapeDtypeStruct((1, hidden), F32),
        ),
        in_specs=[here] * 4 + [here if parts is None else pl.BlockSpec(memory_space=pl.ANY)] * len(held),
        out_specs=(here,) * 4,
        scratch_shapes=scratch,
        compiler_params=pltpu.CompilerParams(vmem_limit_bytes=36 << 20),
        cost_estimate=pl.CostEstimate(
            flops=8 * tokens * width * hidden,
            transcendentals=2 * tokens * hidden,
            bytes_accessed=8 * width * hidden + 10 * tokens * width,
        ),
        name="ffn",
    )(normed, normed_t, grad_out, bias, *held)


def after_tokens(parts, held, acts, grads, features, out_t, dq_t, weights, keep, got, pair, rows, sums, biases, gpair):
    tokens, width = features.shape
    hidden = acts[0].shape[1]
    blocks = tokens // BLK

    def whole(rows, columns):
        return pl.BlockSpec((rows, columns), lambda i: (0, 0))

    def block(first, last, columns=width):
        return pl.BlockSpec((BLK, columns), lambda i: (jnp.clip(i - first, 0, last - first), 0))

    every, own, other = block(0, blocks - 1), block(0, blocks // 2 - 1), block(blocks // 2, blocks - 1)
    units = block(0, blocks - 1, hidden)
    across = pl.BlockSpec((HALF, BLK), lambda i: (0, i))
    side = jax.ShapeDtypeStruct((tokens // 2, width), F32)
    scratch = [pltpu.VMEM((128, width), F32)]
    if parts is not None:
        scratch += [
            pltpu.VMEM((2, width, hidden), BF),
            pltpu.VMEM((2, hidden, width), BF),
            pltpu.SemaphoreType.DMA((64,)),
        ]
    return pl.pallas_call(
        functools.partial(tokens_kernel, parts),
        out_shape=(side, side, side, side, jax.ShapeDtypeStruct((width, 2 * HD + 128), BF)),
        grid=(blocks,),
        in_specs=[
            units,
            units,
            units,
            units,
            every,
            across,
            across,
            whole(width, weights.shape[1]),
            whole(HALF, HALF),
            whole(HALF, HALF),
            own,
            whole(8, width),
            whole(16, width),
            whole(1, hidden),
            whole(1, hidden),
            whole(width, 2 * HD),
        ]
        + (
            [pl.BlockSpec((2, width, hidden), lambda i: (0, 0, 0))] * 2
            if parts is None
            else [pl.BlockSpec(memory_space=pl.ANY)] * 4
        ),
        out_specs=(own, other, own, other, whole(width, 2 * HD + 128)),
        scratch_shapes=scratch,
        compiler_params=pltpu.CompilerParams(
            dimension_semantics=("arbitrary",), vmem_limit_bytes=48 << 20
        ),
        cost_estimate=pl.CostEstimate(
            flops=8 * tokens * width * hidden + 4 * tokens * width * HALF,
            transcendentals=0,
            bytes_accessed=8 * width * hidden + 20 * tokens * width,
        ),
        name="after_tokens",
    )(
        *acts, *grads, features, out_t, dq_t, weights, keep, got, pair, rows, sums, *biases, gpair, *held
    )


def shards(
    tokens,
    segments,
    ln1_gain,
    ln1_bias,
    ln2_gain,
    ln2_bias,
    q_weight,
    q_bias,
    kv_weight,
    k_bias,
    out_weight,
    out_bias,
    up_weight,
    up_bias,
    down_weight,
    cotangent,
):
    core, chip = lax.axis_index("core"), lax.axis_index("chip")
    chips = lax.axis_size("rows") * lax.axis_size("chip")
    own = tokens.shape[1]
    both = 2 * own
    rows = q_weight.shape[0]
    hidden = up_bias.shape[0]
    half = hidden // 2
    back_chips = DOC // both
    own_tokens, own_grad = tokens[0], cotangent[0]

    def half_columns(array, which):
        return lax.dynamic_slice_in_dim(
            array, which * (array.shape[1] // 2), array.shape[1] // 2, 1
        )

    def first(which):
        return jnp.concatenate(
            [half_columns(q_weight, which), half_columns(out_weight, which), kv_weight], axis=1
        )

    up_blocks = up_weight

    def up_half(which):
        block = up_blocks.reshape(rows, chips, 2, 2, half)
        block = lax.dynamic_index_in_dim(block, which, 2, keepdims=False)
        return block.transpose(0, 2, 1, 3).reshape(rows, FF // 2)

    flat = (ln1_gain, ln1_bias, ln2_gain, ln2_bias, q_bias, out_bias)
    if square_line():
        vectors = jnp.concatenate(
            [vector.reshape(1, rows) for vector in flat] + [up_bias.reshape(hidden // rows, rows)]
        )
        vectors = jnp.pad(vectors, ((0, 16 - vectors.shape[0]), (0, 0)))
        mine, theirs = pack(q_weight, out_weight, kv_weight, vectors)
        attn_piece = by_core(core, mine, core_swap(theirs), 0)
        segments, up_blocks = after((segments, up_blocks), attn_piece)
        attn_line = jnp.concatenate(gather_line(attn_piece))
        attn_rows = gather_rows(attn_line)
        up_piece = by_core(core, up_half(core), core_swap(up_half(1 - core)), 0)
        ff_piece = jnp.concatenate([up_piece[:, :D], up_piece[:, D:], down_weight], axis=0)
        ff_line = gather_line(after(ff_piece, attn_line))
        other_tokens = core_swap(own_tokens)
        features = jnp.concatenate([own_tokens, other_tokens], axis=0)
        grad_out = jnp.concatenate([own_grad, core_swap(own_grad)], axis=0)
        attn_rows, grad_out, features = lax.optimization_barrier((attn_rows, grad_out, features))
    else:
        weights = gather_whole(by_core(core, first(core), core_swap(first(1 - core)), 0))
        every = ("rows", "chip", "core")
        table = lax.all_gather(jnp.stack(flat), every, axis=1, tiled=True).astype(F32)
        vector_rows = jnp.pad(table, ((0, 2), (0, 0)))
        bias = gather_whole(up_bias).astype(F32).reshape(chips, 2, half)
        hidden_bias = jnp.pad(bias.transpose(1, 0, 2).reshape(2, D), ((0, 6), (0, 0)))

    if not square_line():
        other_tokens = core_swap(own_tokens)
        features = jnp.concatenate([own_tokens, other_tokens], axis=0)
        grad_out = jnp.concatenate([own_grad, core_swap(own_grad)], axis=0)

    ids = lax.broadcasted_iota(jnp.int32, (MAX_SEGS, 1), 0)
    doc_starts = jnp.sum((segments < ids).astype(jnp.int32), axis=1, keepdims=True)
    first_place, second_place = (chip * 2 + core) * own, (chip * 2 + 1 - core) * own
    span = lax.broadcasted_iota(jnp.int32, (1, own), 1)
    places = jnp.concatenate([first_place + span, second_place + span], axis=1)
    segs = jnp.concatenate(
        [
            lax.dynamic_slice(segments, (0, first_place), (1, own)),
            lax.dynamic_slice(segments, (0, second_place), (1, own)),
        ],
        axis=1,
    )
    starts = jnp.sum(jnp.where(segs == ids, doc_starts, 0), axis=0, keepdims=True)
    relative = places - starts
    frequency = 10000.0 ** (-(jnp.arange(ROT // 2, dtype=F32) * 2.0 / ROT))
    angles = relative.astype(F32) * frequency[:, None]
    cosine, sine = jnp.cos(angles), jnp.sin(angles)
    window_start = (chip - back_chips) * both
    pos = jnp.concatenate(
        [starts - window_start, places - window_start, jnp.zeros((6, both), jnp.int32)], axis=0
    )
    firsts, lasts = pos[:, ::BLK], pos[:, BLK - 1 :: BLK]
    scal = jnp.concatenate(
        [
            core.reshape(1),
            jnp.stack([firsts[0] // BLK, lasts[1] // BLK + 1, lasts[0]], axis=1).reshape(-1),
        ]
    ).astype(jnp.int32)


    bias_column = k_bias.astype(F32)[:, None]
    if square_line():
        weights, vector_rows, hidden_bias, *fronts = front(
            attn_rows, own_tokens, other_tokens, bias_column, cosine, sine
        )
    else:
        fronts = front(
            (weights, vector_rows), own_tokens, other_tokens, bias_column, cosine, sine
        )
    normed_one, normed_two, normed_two_t, query_t, own_pairs, keep, send = fronts
    got = core_swap(send)
    mine = jnp.concatenate(
        [chip_shift(own_pairs, k, False) for k in range(back_chips, 0, -1)] + [own_pairs], axis=0
    )
    theirs = core_swap(mine)
    if square_line():
        ff_rows = gather_rows(after(jnp.concatenate(ff_line), attn_rows))

    heads = attention(scal, query_t, grad_out, keep, got, pos, cosine, sine, mine, theirs)
    if square_line():
        heads, ff_rows = lax.optimization_barrier((heads, ff_rows))
    out_t, grad_query_t, pair_mine, pair_theirs = heads
    pair_got = core_swap(pair_theirs)
    grad_query, proj_keep, proj_send, sums = after_heads(
        out_t, grad_query_t, normed_one, grad_out
    )
    proj_got = core_swap(proj_send)
    if square_line():
        pair_got, proj_got = after((pair_got, proj_got), sums)
        step = 2 * rows
        parts = [((i * step, step, 0), ((2 + i) * step, step, 1)) for i in range(2)] + [
            tuple((i * step, step, (i // 2, i % 2)) for i in range(4))
        ]
        held = [ff_rows] * 3
    else:
        up_whole = gather_whole(by_core(core, up_half(core), core_swap(up_half(1 - core)), 0))
        down_whole = gather_whole(down_weight).reshape(chips, 2, half, D)
        down_whole = down_whole.transpose(1, 0, 2, 3).reshape(2, D, D)
        parts = [None] * 3
        ups = jnp.stack([up_whole[:, :D], up_whole[:, D:]])
        held = [(ups[0], down_whole[0]), (ups[1], down_whole[1]), (ups, down_whole)]
    pair_sum = pair_mine + pair_got
    arrived = [
        chip_shift(
            pair_sum[(back_chips - k) * own : (back_chips - k + 1) * own].astype(BF), -k, False
        )
        for k in range(1, back_chips + 1)
    ]
    grad_proj = by_core(core, proj_keep, proj_got, 0)
    attn_terms = jnp.concatenate([grad_query, grad_proj], axis=1)
    if square_line():
        attn_plane, attn_one = reduce_rows(attn_terms)
    grad_pair, grad_one_pair, key_bias = after_pairs(
        pair_sum, *arrived, normed_one, weights, cosine, sine
    )
    key_bias = key_bias[0, :HD]

    inputs = (normed_two, normed_two_t, grad_out)
    act0, dz0, terms0, bias0 = feed_forward(*inputs, hidden_bias[0:1], parts[0], held[0])
    if square_line():
        (act0, dz0, terms0, bias0), attn_one, grad_pair, grad_one_pair, key_bias = lax.optimization_barrier(
            ((act0, dz0, terms0, bias0), attn_one, grad_pair, grad_one_pair, key_bias)
        )
        planes0, one0 = reduce_first(terms0)
        other_bias = core_swap(key_bias)
    act1, dz1, terms1, bias1 = feed_forward(*inputs, hidden_bias[1:2], parts[1], held[1])
    if square_line():
        (act1, dz1, terms1, bias1), one0, other_bias = lax.optimization_barrier(
            ((act1, dz1, terms1, bias1), one0, other_bias)
        )
        two0 = reduce_second(planes0, one0)
        planes1, one1 = reduce_first(terms1)
        key_bias = key_bias + other_bias
        other_bias = line_swap(key_bias, 1)
    part, part_send, scaled, scaled_send, small_terms = after_tokens(
        parts[2],
        held[2],
        (act0, act1),
        (dz0, dz1),
        features,
        out_t,
        grad_query_t,
        weights,
        keep,
        got,
        grad_one_pair,
        vector_rows,
        sums,
        (bias0, bias1),
        grad_pair,
    )
    if square_line():
        (part, part_send, scaled, scaled_send, small_terms), two0, one1, other_bias = (
            lax.optimization_barrier(
                ((part, part_send, scaled, scaled_send, small_terms), two0, one1, other_bias)
            )
        )
        key_bias = key_bias + other_bias
    part_got, scaled_got = core_swap(part_send), core_swap(scaled_send)

    def finish(part_got, scaled_got):
        layer_out = own_tokens.astype(F32) + part + part_got + vector_rows[5:6]
        total = scaled + scaled_got
        unit, spread = standard(own_tokens)
        input_grad = own_grad.astype(F32) + spread * (
            total
            - jnp.mean(total, axis=-1, keepdims=True)
            - unit * jnp.mean(total * unit, axis=-1, keepdims=True)
        )
        return layer_out.astype(BF), input_grad

    def split(value):
        return (
            lax.dynamic_slice_in_dim(value, core * rows, rows, 0),
            core_swap(lax.dynamic_slice_in_dim(value, (1 - core) * rows, rows, 0)),
        )

    def blocks(first_half, second_half):
        return jnp.stack(
            [value.reshape(rows, chips, half) for value in (first_half, second_half)], axis=2
        ).reshape(rows, chips, 1, hidden)

    if square_line():
        small_grid = small_terms.reshape((4, 4, small_terms.shape[0] // 16) + small_terms.shape[1:])
        row = lax.axis_index("rows")
        small_planes = [
            lax.dynamic_index_in_dim(small_grid, row ^ bit, 0, keepdims=False) for bit in range(4)
        ]
        two1 = reduce_second(planes1, one1, small_planes)
        own0, three0 = reduce_third((planes0[0], *two0), (attn_plane, *attn_one))
        small_far = rows_swap(after(small_planes[3], part_got), 3)
        layer_out, input_grad = finish(part_got, scaled_got)
        other_bias = line_swap(after(key_bias, part_got), 2)
        two1, three0, small_far, layer_out, input_grad, other_bias = lax.optimization_barrier(
            (two1, three0, small_far, layer_out, input_grad, other_bias)
        )
        key_bias = key_bias + other_bias
        own1, three1 = reduce_third(
            (planes1[0], *(part[:, :, : 2 * D] for part in two1)),
            (small_planes[0], small_far, *(part[:, :, 2 * D :] for part in two1)),
        )
        other_bias = rows_swap(after(key_bias, two1), 1)
        key_bias = key_bias + other_bias
        sum0 = reduce_last(own0, three0)
        sum0, attn_sum = sum0[:, : 2 * D], sum0[:, 2 * D :]
        attn_split = split(after(attn_sum, other_bias))
        up_split = split(after(sum0, other_bias)[:, :D])
        key_bias_out = key_bias + rows_swap(key_bias, 2)
        mine, theirs = attn_split
        query_out = by_core(core, mine[:, :HALF], theirs[:, :HALF], 1)
        proj_out = by_core(core, mine[:, HALF:], theirs[:, HALF:], 1)
        three1, up_split, query_out, proj_out, key_bias_out = lax.optimization_barrier(
            (three1, up_split, query_out, proj_out, key_bias_out)
        )
        sum1 = reduce_last(own1, three1)
        sum1, small_sum = sum1[:, : 2 * D], sum1[:, 2 * D :]
    else:
        layer_out, input_grad = finish(part_got, scaled_got)
        sum0, sum1, small_sum = (reduce_whole(terms) for terms in (terms0, terms1, small_terms))
        up_split = split(sum0[:, :D])
        mine, theirs = split(reduce_whole(attn_terms))
        query_out = by_core(core, mine[:, :HALF], theirs[:, :HALF], 1)
        proj_out = by_core(core, mine[:, HALF:], theirs[:, HALF:], 1)
        key_bias_out = lax.psum(key_bias, ("rows", "chip", "core"))
    mine, theirs = split(jnp.concatenate([sum1[:, :D], small_sum], axis=1))
    rest = mine[:, D:] + theirs[:, D:]
    pair_out, vector_out = rest[:, : 2 * HD], rest[:, 2 * HD :]
    up_bias_out = small_sum[:, 2 * HD + 6 : 2 * HD + 8].T.reshape(hidden)
    up_out = by_core(
        core, blocks(up_split[0], mine[:, :D]), blocks(up_split[1], theirs[:, :D]), 2
    ).reshape(rows, FF)
    down_out = jnp.concatenate([sum0[:, D:], sum1[:, D : 2 * D]], axis=0)
    return (
        layer_out[None],
        input_grad[None],
        vector_out[:, 0],
        vector_out[:, 1],
        vector_out[:, 2],
        vector_out[:, 3],
        query_out,
        vector_out[:, 4],
        pair_out,
        key_bias_out,
        proj_out,
        vector_out[:, 5],
        up_out,
        up_bias_out,
        down_out,
    )


def solution(mesh):
    devices = mesh.devices.reshape(mesh.shape["rows"], mesh.shape["wide"] // 2, 2)
    every, wide = ("rows", "chip", "core"), ("chip", "core")
    matrix, vector, sequence = P(every, None), P(every), P("rows", wide, None)
    return jax.shard_map(
        shards,
        mesh=Mesh(devices, every),
        in_specs=(
            sequence,
            P("rows", None),
            vector,
            vector,
            vector,
            vector,
            matrix,
            vector,
            matrix,
            P(),
            matrix,
            vector,
            matrix,
            vector,
            matrix,
            sequence,
        ),
        out_specs=(
            sequence,
            sequence,
            vector,
            vector,
            vector,
            vector,
            matrix,
            vector,
            matrix,
            P(),
            matrix,
            vector,
            matrix,
            vector,
            matrix,
        ),
        check_vma=False,
    )
```

```python
import functools
import math

import jax
import jax.numpy as jnp
from jax import lax
from jax.experimental import pallas as pl
from jax.experimental.pallas import tpu as pltpu
from jax.sharding import Mesh, PartitionSpec as P

D = 768
HEADS = 12
HD = 64
ROT = 16
DOC = 2048
FF = 3072
MAX_SEGS = 32
norm_eps = 1e-05
BF = jnp.bfloat16
F32 = jnp.float32
HALF = HEADS // 2 * HD
BLK = 256
GROUP = 6


def dot(left, right, dims):
    return lax.dot_general(left, right, (dims, ((), ())), preferred_element_type=F32)


def core_swap(value):
    return lax.ppermute(value, "core", [(0, 1), (1, 0)])


def rows_swap(value, bit):
    return lax.ppermute(value, "rows", [(r, r ^ bit) for r in range(4)])


def chip_shift(value, by, wrap):
    count = lax.axis_size("chip")
    pairs = [(s, (s + by) % count) for s in range(count) if wrap or 0 <= s + by < count]
    return lax.ppermute(value, "chip", pairs)


def square_line():
    return lax.axis_size("rows") == 4 and lax.axis_size("chip") == 4


def place_copies(parts, sources, outs, sems):
    row, chip = lax.axis_index("rows"), lax.axis_index("chip")
    size = sources[0].shape[0] // 4
    copies = []
    for first, count, out in parts:
        for turn, source in enumerate(sources):
            for step in range(4):
                place = (row ^ turn) * 4 + lax.rem(chip + step, 4)
                copies.append(
                    pltpu.make_async_copy(
                        source.at[pl.ds(step * size + first, count)],
                        outs[out].at[pl.ds(pl.multiple_of(place * count, 8), count)]
                        if isinstance(out, int)
                        else outs[out[0]].at[out[1], pl.ds(pl.multiple_of(place * count, 8), count)],
                        sems.at[len(copies)],
                    )
                )
    return copies


def gather_line(piece):
    return [piece] + [chip_shift(piece, -k, True) for k in (1, 2, 3)]


def gather_rows(lines):
    return lines, rows_swap(lines, 1), rows_swap(lines, 2), rows_swap(lines, 3)


def gather_whole(piece):
    return lax.all_gather(piece, ("rows", "chip"), axis=0, tiled=True)


def reduce_first(terms):
    row = lax.axis_index("rows")
    grid = terms.reshape((4, 4, terms.shape[0] // 16) + terms.shape[1:])
    planes = [lax.dynamic_index_in_dim(grid, row ^ bit, 0, keepdims=False) for bit in range(4)]
    return planes, (rows_swap(planes[3][:2], 1), rows_swap(planes[3][2:], 2))


def reduce_rows(terms):
    row = lax.axis_index("rows")
    grid = terms.reshape((4, 4, terms.shape[0] // 16) + terms.shape[1:])
    planes = [lax.dynamic_index_in_dim(grid, row ^ bit, 0, keepdims=False) for bit in range(4)]
    return planes[0], [rows_swap(planes[bit], bit) for bit in (3, 1, 2)]


def reduce_second(planes, arrived, beside=None):
    _, flat, cross, _ = planes
    from_flat, from_cross = arrived
    to_flat = jnp.concatenate(
        [flat[:2], (flat[2:].astype(F32) + from_cross.astype(F32)).astype(BF)], axis=0
    )
    to_cross = jnp.concatenate(
        [(cross[:2].astype(F32) + from_flat.astype(F32)).astype(BF), cross[2:]], axis=0
    )
    if beside is not None:
        to_flat = jnp.concatenate([to_flat, beside[1]], axis=2)
        to_cross = jnp.concatenate([to_cross, beside[2]], axis=2)
    return rows_swap(to_flat, 1), rows_swap(to_cross, 2)


def reduce_third(*groups):
    chip = lax.axis_index("chip")

    def line(step):
        spot = lax.rem(chip + step, 4)
        sums = []
        for group in groups:
            pick = [
                lax.dynamic_index_in_dim(part, spot, 0, keepdims=False).astype(F32)
                for part in group
            ]
            sums.append(sum(pick[1:], pick[0]))
        return jnp.concatenate(sums, axis=1)

    return line(0), [chip_shift(line(step).astype(BF), step, True) for step in (1, 2, 3)]


def reduce_last(own, arrived):
    return own + arrived[0].astype(F32) + arrived[1].astype(F32) + arrived[2].astype(F32)


def reduce_whole(terms):
    return lax.psum_scatter(terms.astype(F32), ("rows", "chip"), scatter_dimension=0, tiled=True)


def after(value, *others):
    return lax.optimization_barrier((value, others))[0]


def line_swap(value, bit):
    return lax.ppermute(value, "chip", [(s, s ^ bit) for s in range(4)])


def by_core(core, own, other, axis):
    return jnp.where(
        core == 0,
        jnp.concatenate([own, other], axis=axis),
        jnp.concatenate([other, own], axis=axis),
    )


def pack_kernel(q_ref, out_ref, kv_ref, vectors_ref, mine_ref, theirs_ref):
    core = lax.axis_index("core")
    rows = q_ref.shape[0]
    pick = lax.broadcasted_iota(jnp.int32, (16, 128), 0) == lax.broadcasted_iota(
        jnp.int32, (16, 128), 1
    )
    columns = dot(vectors_ref[...], jnp.where(pick, 1.0, 0.0).astype(BF), ((0,), (0,))).astype(BF)
    for which, ref in ((core, mine_ref), (1 - core, theirs_ref)):
        spot = pl.ds(pl.multiple_of(which * HALF, HALF), HALF)
        ref[:, :HALF] = q_ref[:, spot]
        ref[:, HALF : 2 * HALF] = out_ref[:, spot]
        ref[:, 2 * HALF : 2 * HALF + 2 * HD] = kv_ref[...]
        ref[:, 2 * HALF + 2 * HD :] = columns


def pack(q_weight, out_weight, kv_weight, vectors):
    rows = q_weight.shape[0]
    side = jax.ShapeDtypeStruct((rows, 2 * HALF + 2 * HD + 128), BF)
    return pl.pallas_call(
        pack_kernel,
        out_shape=(side, side),
        cost_estimate=pl.CostEstimate(flops=0, transcendentals=0, bytes_accessed=8 * rows * D),
        name="pack",
    )(q_weight, out_weight, kv_weight, vectors)


def turn(values, cosine, sine, direction):
    half = ROT // 2
    a, b = values[:half, :], values[half:ROT, :]
    return jnp.concatenate(
        [a * cosine - direction * b * sine, b * cosine + direction * a * sine, values[ROT:, :]],
        axis=0,
    )


def standard(tokens):
    values = tokens.astype(F32)
    center = values - jnp.mean(values, axis=-1, keepdims=True)
    spread = lax.rsqrt(jnp.mean(center * center, axis=-1, keepdims=True) + norm_eps)
    return center * spread, spread


def front_rest(
    own_ref, other_ref, kbias_ref, cos_ref, sin_ref, w_ref, rows_ref,
    h1_ref, h2_ref, h2t_ref, q_ref, pairs_ref, keep_ref, send_ref,
):
    core = lax.axis_index("core")
    count = own_ref.shape[0]
    gain_one, shift_one, gain_two, shift_two = (rows_ref[i : i + 1, :] for i in range(4))

    def norm(part, ref):
        unit, _ = standard(ref[...])
        spot = pl.ds(part * count, count)
        h1_ref[spot, :] = (unit * gain_one + shift_one).astype(BF)
        normed = (unit * gain_two + shift_two).astype(BF)
        h2_ref[spot, :] = normed
        h2t_ref[:, part * count : (part + 1) * count] = normed.T

    norm(0, own_ref)
    pair = dot(w_ref[:, 2 * HALF : 2 * HALF + 2 * HD], h1_ref[:count, :], ((0,), (1,)))
    key = turn(
        pair[:HD] + kbias_ref[...], cos_ref[:, :count], sin_ref[:, :count], 1.0
    ).astype(BF)
    pairs_ref[...] = jnp.concatenate([key, pair[HD:].astype(BF)], axis=0).T
    norm(1, other_ref)
    query = dot(w_ref[:, :HALF], h1_ref[...], ((0,), (1,)))
    bias = jnp.where(core == 0, rows_ref[4:5, :HALF], rows_ref[4:5, HALF:])
    query = query + jnp.broadcast_to(bias, (8, HALF)).T[:, :1]
    for h in range(HEADS // 2):
        q_ref[h * HD : (h + 1) * HD, :] = turn(
            query[h * HD : (h + 1) * HD, :], cos_ref[...], sin_ref[...], 1.0
        ).astype(BF)
    for index, ref in ((core, keep_ref), (1 - core, send_ref)):
        spot = pl.ds(pl.multiple_of(index * HALF, HALF), HALF)
        ref[...] = w_ref[spot, HALF : 2 * HALF]


def front_kernel(
    lines_ref, flat_ref, cross_ref, far_ref, own_ref, other_ref, kbias_ref, cos_ref, sin_ref,
    w_ref, rows_ref, bias_ref, h1_ref, h2_ref, h2t_ref, q_ref, pairs_ref, keep_ref, send_ref, sems,
):
    core = lax.axis_index("core")
    copies = place_copies(
        ((0, w_ref.shape[0] // 16, 0),), (lines_ref, flat_ref, cross_ref, far_ref), (w_ref,), sems
    )
    for copy in copies:
        copy.start()
    for copy in copies:
        copy.wait()
    table = w_ref[:, 2 * HALF + 2 * HD :].astype(F32).T
    rows_ref[...] = table[:8, :]
    half = lax.rem(lax.broadcasted_iota(jnp.int32, (1, D), 1), 48) // 24
    for k in range(2):
        low, high = table[6 + 2 * k : 7 + 2 * k, :], table[7 + 2 * k : 8 + 2 * k, :]
        first = jnp.where(half == 0, low, pltpu.roll(jnp.broadcast_to(high, (8, D)), 24, 1)[:1])
        second = jnp.where(
            half == 1, high, pltpu.roll(jnp.broadcast_to(low, (8, D)), D - 24, 1)[:1]
        )
        bias_ref[k : k + 1, :] = jnp.where(core == 0, first, second)
    bias_ref[2:8, :] = jnp.zeros((6, D), F32)
    front_rest(
        own_ref, other_ref, kbias_ref, cos_ref, sin_ref, w_ref, rows_ref,
        h1_ref, h2_ref, h2t_ref, q_ref, pairs_ref, keep_ref, send_ref,
    )


def front_plain_kernel(
    w_ref, rows_ref, own_ref, other_ref, kbias_ref, cos_ref, sin_ref, *outs
):
    front_rest(own_ref, other_ref, kbias_ref, cos_ref, sin_ref, w_ref, rows_ref, *outs)


def front(pieces, own, other, k_bias, cosine, sine):
    both = 2 * own.shape[0]
    placed = len(pieces) == 4
    wide = pieces[0].shape[1]
    shapes = (
        jax.ShapeDtypeStruct((both, D), BF),
        jax.ShapeDtypeStruct((both, D), BF),
        jax.ShapeDtypeStruct((D, both), BF),
        jax.ShapeDtypeStruct((HALF, both), BF),
        jax.ShapeDtypeStruct((own.shape[0], 2 * HD), BF),
        jax.ShapeDtypeStruct((HALF, HALF), BF),
        jax.ShapeDtypeStruct((HALF, HALF), BF),
    )
    here = pl.BlockSpec(memory_space=pltpu.VMEM)
    if placed:
        shapes = (
            jax.ShapeDtypeStruct((D, wide), BF),
            jax.ShapeDtypeStruct((8, D), F32),
            jax.ShapeDtypeStruct((8, D), F32),
        ) + shapes
    return pl.pallas_call(
        front_kernel if placed else front_plain_kernel,
        out_shape=shapes,
        in_specs=[pl.BlockSpec(memory_space=pl.ANY) if placed else here] * len(pieces) + [here] * 5,
        out_specs=tuple(here for _ in shapes),
        scratch_shapes=[pltpu.SemaphoreType.DMA((16,))] if placed else [],
        compiler_params=pltpu.CompilerParams(vmem_limit_bytes=48 << 20),
        cost_estimate=pl.CostEstimate(
            flops=2 * both * D * (HALF + 2 * HD), transcendentals=both, bytes_accessed=8 * both * D
        ),
        name="front",
    )(*pieces, own, other, k_bias, cosine, sine)


def attn_kernel(
    scal_ref, q_ref, grad_ref, keep_in_ref, got_in_ref, pos_ref, cos_ref, sin_ref, mine_ref, theirs_ref,
    o_ref, dq_ref, dmine_ref, dtheirs_ref,
    keep_ref, got_ref, kv_ref, kvt_ref, dkv_ref, g_ref, s_ref, r_ref, rt_ref, sems,
):
    block = pl.program_id(0)
    core = scal_ref[0]
    low, high, edge = (scal_ref[1 + 3 * block + i] for i in range(3))
    wide = GROUP * BLK
    half = kv_ref.shape[0] // 2
    own_blocks = pl.num_programs(0) // 2

    @pl.when(block == 0)
    def _():
        dkv_ref[...] = jnp.zeros_like(dkv_ref)
        copies = [
            pltpu.make_async_copy(source, target, sems.at[i])
            for i, (source, target) in enumerate(
                (
                    (mine_ref, kv_ref.at[pl.ds(0, half)]),
                    (theirs_ref, kv_ref.at[pl.ds(half, half)]),
                    (keep_in_ref, keep_ref),
                    (got_in_ref, got_ref),
                )
            )
        ]
        for copy in copies:
            copy.start()
        for copy in copies:
            copy.wait()
        for part in range(2):
            kvt_ref[: 2 * HD, part * half : (part + 1) * half] = kv_ref[
                part * half : (part + 1) * half, :
            ].T
        kvt_ref[2 * HD :, :] = jnp.ones((16, 2 * half), BF)

    def spot(key_block):
        side = lax.rem(key_block // own_blocks, 2) ^ core
        place = (key_block // (2 * own_blocks)) * own_blocks + lax.rem(key_block, own_blocks)
        return pl.multiple_of(side * half + place * BLK, BLK)

    first, pairs_end, single = low // 2, high // 2, lax.rem(high, 2)
    last = pairs_end - 1 + single
    clear = jnp.clip((edge + 2 * BLK - 1) // (2 * BLK), first, last)

    def slot(key_block, size):
        return pl.ds(pl.multiple_of((key_block - 2 * first) * BLK, BLK), size)

    def over_keys(body, carry):
        def double(masked):
            return lambda i, c: body(masked, 2 * i, 2 * BLK, c)

        carry = lax.fori_loop(first, clear, double(True), carry)
        carry = lax.fori_loop(clear, last, double(False), carry)
        carry = lax.fori_loop(last, pairs_end, double(True), carry)
        return lax.fori_loop(
            0, single, lambda i, c: body(True, 2 * pairs_end + i, BLK, c), carry
        )

    def over_all(body, carry):
        carry = lax.fori_loop(first, pairs_end, lambda i, c: body(2 * i, 2 * BLK, c), carry)
        return lax.fori_loop(0, single, lambda i, c: body(2 * pairs_end + i, BLK, c), carry)

    near = pl.ds(pl.multiple_of(core * HALF, HALF), HALF)
    away = pl.ds(pl.multiple_of((1 - core) * HALF, HALF), HALF)
    g_ref[...] = (
        dot(keep_ref[...], grad_ref[:, near], ((1,), (1,)))
        + dot(got_ref[...], grad_ref[:, away], ((1,), (1,)))
    ).astype(BF)
    starts = jnp.concatenate([pos_ref[0:1, :]] * GROUP, axis=1)
    places = jnp.concatenate([pos_ref[1:2, :]] * GROUP, axis=1)
    blank = jnp.zeros((HD, BLK), BF)
    for h in range(GROUP):
        query = (q_ref[h * HD : (h + 1) * HD, :].astype(F32) * HD**-0.5).astype(BF)
        grad = g_ref[h * HD : (h + 1) * HD, :]
        query = jnp.concatenate([query, blank], axis=0)
        grad = jnp.concatenate([blank, grad], axis=0)
        r_ref[0, :, h * BLK : (h + 1) * BLK] = query
        r_ref[1, :, h * BLK : (h + 1) * BLK] = grad
        rt_ref[h * BLK : (h + 1) * BLK, :] = query.T
        rt_ref[(GROUP + h) * BLK : (GROUP + h + 1) * BLK, :] = grad.T

    def scores(masked, key_block, size, peak):
        keys = kv_ref[pl.ds(spot(key_block), size), :]
        s = dot(keys, r_ref[0], ((1,), (0,)))
        if masked:
            key_places = key_block * BLK + lax.broadcasted_iota(jnp.int32, (size, wide), 0)
            s = jnp.where((key_places >= starts) & (key_places <= places), s, -1e30)
        s_ref[slot(key_block, size), :] = s
        return jnp.maximum(peak, jnp.max(s, axis=0, keepdims=True))

    peak = over_keys(scores, jnp.full((1, wide), -1e30, F32))

    def expo(key_block, size, out):
        values = kvt_ref[HD:, pl.ds(spot(key_block), size)]
        e = jnp.exp(s_ref[slot(key_block, size), :] - peak)
        s_ref[slot(key_block, size), :] = e
        return out + dot(values, e.astype(BF), ((1,), (0,)))

    out = over_all(expo, jnp.zeros((HD + 16, wide), F32))
    inverse = 1.0 / out[HD : HD + 1, :]
    out = out[:HD] * inverse
    deltas = []
    for h in range(GROUP):
        part = out[:, h * BLK : (h + 1) * BLK]
        o_ref[h * HD : (h + 1) * HD, :] = part.astype(BF)
        deltas.append(
            jnp.sum(part * g_ref[h * HD : (h + 1) * HD, :].astype(F32), axis=0, keepdims=True)
        )
    delta = jnp.concatenate(deltas, axis=1)

    def back(key_block, size, dq):
        where = spot(key_block)
        pairs = kv_ref[pl.ds(where, size), :]
        keys = kvt_ref[:HD, pl.ds(where, size)]
        p = s_ref[slot(key_block, size), :] * inverse
        dp = dot(pairs, r_ref[1], ((1,), (0,)))
        ds = (p * (dp - delta)).astype(BF)
        left = jnp.concatenate([ds, p.astype(BF)], axis=1)
        dkv_ref[pl.ds(where, size), :] += dot(left, rt_ref[...], ((1,), (0,)))
        return dq + dot(keys, ds, ((1,), (0,)))

    dq = over_all(back, jnp.zeros((HD, wide), F32)) * HD**-0.5
    for h in range(GROUP):
        part = dq[:, h * BLK : (h + 1) * BLK].astype(BF).astype(F32)
        dq_ref[h * HD : (h + 1) * HD, :] = turn(part, cos_ref[...], sin_ref[...], -1.0).astype(BF)

    @pl.when(block == pl.num_programs(0) - 1)
    def _():
        dmine_ref[...] = dkv_ref[:half, :]
        dtheirs_ref[...] = dkv_ref[half:, :]


def attention(scal, query_t, grad_out, keep, got, pos, cosine, sine, mine, theirs):
    features, tokens = query_t.shape
    blocks, half = tokens // BLK, mine.shape[0]
    tile = pl.BlockSpec((features, BLK), lambda b, s: (0, b))
    small = pl.BlockSpec((8, BLK), lambda b, s: (0, b))

    def whole(rows, columns):
        return pl.BlockSpec((rows, columns), lambda b, s: (0, 0))

    return pl.pallas_call(
        attn_kernel,
        out_shape=(
            jax.ShapeDtypeStruct((features, tokens), BF),
            jax.ShapeDtypeStruct((features, tokens), BF),
            jax.ShapeDtypeStruct((half, 2 * HD), F32),
            jax.ShapeDtypeStruct((half, 2 * HD), F32),
        ),
        grid_spec=pltpu.PrefetchScalarGridSpec(
            num_scalar_prefetch=1,
            grid=(blocks,),
            in_specs=[
                tile,
                pl.BlockSpec((BLK, D), lambda b, s: (b, 0)),
                pl.BlockSpec(memory_space=pltpu.HBM),
                pl.BlockSpec(memory_space=pltpu.HBM),
                small,
                small,
                small,
                pl.BlockSpec(memory_space=pltpu.HBM),
                pl.BlockSpec(memory_space=pltpu.HBM),
            ],
            out_specs=(tile, tile, whole(half, 2 * HD), whole(half, 2 * HD)),
            scratch_shapes=[
                pltpu.VMEM((HALF, HALF), BF),
                pltpu.VMEM((HALF, HALF), BF),
                pltpu.VMEM((2 * half, 2 * HD), BF),
                pltpu.VMEM((2 * HD + 16, 2 * half), BF),
                pltpu.VMEM((2 * half, 2 * HD), F32),
                pltpu.VMEM((features, BLK), BF),
                pltpu.VMEM((DOC + 2 * BLK, GROUP * BLK), F32),
                pltpu.VMEM((2, 2 * HD, GROUP * BLK), BF),
                pltpu.VMEM((2 * GROUP * BLK, 2 * HD), BF),
                pltpu.SemaphoreType.DMA((4,)),
            ],
        ),
        compiler_params=pltpu.CompilerParams(
            dimension_semantics=("arbitrary",), vmem_limit_bytes=36 << 20
        ),
        cost_estimate=pl.CostEstimate(
            flops=12 * features * tokens * DOC * 3 // 4,
            transcendentals=features // HD * tokens * DOC * 3 // 4,
            bytes_accessed=8 * features * tokens,
        ),
        name="attention",
    )(scal, query_t, grad_out, keep, got, pos, cosine, sine, mine, theirs)


def heads_kernel(
    o_ref, dq_ref, h1_ref, grad_ref, gq_ref, keep_out_ref, send_out_ref, sums_ref
):
    core = lax.axis_index("core")
    near = pl.ds(pl.multiple_of(core * HALF, HALF), HALF)
    away = pl.ds(pl.multiple_of((1 - core) * HALF, HALF), HALF)
    send_out_ref[...] = dot(o_ref[...], grad_ref[:, away], ((1,), (0,))).astype(BF)
    keep_out_ref[...] = dot(o_ref[...], grad_ref[:, near], ((1,), (0,))).astype(BF)
    gq_ref[...] = dot(dq_ref[...], h1_ref[...], ((1,), (0,))).T.astype(BF)
    ones = jnp.ones((8, dq_ref.shape[1]), BF)
    sums_ref[...] = jnp.zeros_like(sums_ref)
    sums_ref[0:8, near] = dot(ones, dq_ref[...], ((1,), (1,)))
    count = grad_ref.shape[0] // 2
    sums_ref[8:16, :] = dot(ones[:, :count], grad_ref[:count, :], ((1,), (0,)))


def after_heads(out_t, dq_t, normed, grad_out):
    both = normed.shape[0]
    return pl.pallas_call(
        heads_kernel,
        out_shape=(
            jax.ShapeDtypeStruct((D, HALF), BF),
            jax.ShapeDtypeStruct((HALF, HALF), BF),
            jax.ShapeDtypeStruct((HALF, HALF), BF),
            jax.ShapeDtypeStruct((16, D), F32),
        ),
        compiler_params=pltpu.CompilerParams(vmem_limit_bytes=48 << 20),
        cost_estimate=pl.CostEstimate(
            flops=4 * both * D * HALF, transcendentals=0, bytes_accessed=6 * both * D
        ),
        name="after_heads",
    )(out_t, dq_t, normed, grad_out)


def pairs_kernel(
    own_ref, near_ref, far_ref, h1_ref, w_ref, cos_ref, sin_ref, gw_ref, dh_ref, gbias_ref
):
    total = own_ref[...] + near_ref[...].astype(F32) + far_ref[...].astype(F32)
    total = total.astype(BF).astype(F32).T
    key = turn(total[:HD], cos_ref[...], sin_ref[...], -1.0)
    grad = jnp.concatenate([key, total[HD:]], axis=0).astype(BF)
    gw_ref[...] = dot(grad, h1_ref[...], ((1,), (0,))).T.astype(BF)
    dh_ref[...] = dot(grad.T, w_ref[:, 2 * HALF : 2 * HALF + 2 * HD], ((1,), (1,)))
    ones = jnp.ones((8, grad.shape[1]), BF)
    gbias_ref[...] = dot(ones, grad, ((1,), (1,)))


def after_pairs(pairs, near, far, normed, weights, cosine, sine):
    count = near.shape[0]

    def whole(rows, columns):
        return pl.BlockSpec((rows, columns), lambda i: (0, 0))

    return pl.pallas_call(
        pairs_kernel,
        out_shape=(
            jax.ShapeDtypeStruct((D, 2 * HD), BF),
            jax.ShapeDtypeStruct((count, D), F32),
            jax.ShapeDtypeStruct((8, 2 * HD), F32),
        ),
        grid=(1,),
        in_specs=[
            pl.BlockSpec((count, 2 * HD), lambda i: (pairs.shape[0] // count - 1, 0)),
            whole(count, 2 * HD),
            whole(count, 2 * HD),
            whole(count, D),
            whole(D, weights.shape[1]),
            whole(8, count),
            whole(8, count),
        ],
        out_specs=(whole(D, 2 * HD), whole(count, D), whole(8, 2 * HD)),
        compiler_params=pltpu.CompilerParams(vmem_limit_bytes=32 << 20),
        cost_estimate=pl.CostEstimate(
            flops=8 * count * D * HD, transcendentals=0, bytes_accessed=8 * count * D
        ),
        name="after_pairs",
    )(pairs, near, far, normed, weights, cosine, sine)


def ffn_units(
    placed, h_ref, ht_ref, g_ref, bias_ref, up_ref, down_ref, grad_ref, act_ref, dz_ref
):
    for copy in placed:
        copy.start()
    for copy in placed[:16]:
        copy.wait()
    z = dot(h_ref[...], up_ref[...], ((1,), (0,))) + bias_ref[...]
    below = 0.5 * (1.0 + lax.erf(z * 0.5**0.5))
    slope = below + z * (jnp.exp(-0.5 * z * z) * (0.5 / math.pi) ** 0.5)
    act = (z * below).astype(BF)
    grad_ref[:, D : 2 * D] = dot(act, g_ref[...], ((0,), (0,))).astype(BF)
    act_ref[...] = act
    for copy in placed[16:]:
        copy.wait()
    grad = (dot(g_ref[...], down_ref[...], ((1,), (1,))) * slope).astype(BF)
    dz_ref[...] = grad
    grad_ref[:, :D] = dot(ht_ref[...], grad, ((1,), (0,))).astype(BF)
    return jnp.sum(grad.astype(F32), axis=0, keepdims=True)


def ffn_weights(parts, rest):
    if parts is None:
        return (), rest[0], rest[1], rest[2:]
    up_ref, down_ref, sems = rest[-3:]
    return place_copies(parts, rest[:4], (up_ref, down_ref), sems), up_ref, down_ref, rest[4:-3]


def ffn_first_kernel(parts, h_ref, ht_ref, g_ref, bias_ref, *rest):
    placed, up_ref, down_ref, rest = ffn_weights(parts, rest)
    act_ref, dz_ref, grad_ref, gbias_ref = rest
    gbias_ref[...] = ffn_units(
        placed, h_ref, ht_ref, g_ref, bias_ref, up_ref, down_ref, grad_ref, act_ref, dz_ref
    )


def tokens_kernel(
    parts, act0_ref, act1_ref, dz0_ref, dz1_ref, x_ref, o_ref, dq_ref, w_ref, out_keep_ref, out_got_ref,
    pair_ref, rows_ref, sums_ref, bias0_ref, bias1_ref, gpair_ref, *rest
):
    placed, up_ref, down_ref, rest = ffn_weights(parts, rest)
    keep_ref, send_ref, tkeep_ref, tsend_ref, small_ref, table_ref = rest
    step = pl.program_id(0)
    core = lax.axis_index("core")
    blocks = pl.num_programs(0)

    @pl.when(step == 0)
    def _():
        for copy in placed:
            copy.start()
        table_ref[...] = jnp.zeros_like(table_ref)
        table_ref[4:5, :] = sums_ref[0:1, :]
        table_ref[5:6, :] = sums_ref[8:9, :]
        table_ref[6:7, :] = bias0_ref[...]
        table_ref[7:8, :] = bias1_ref[...]
        small_ref[:, : 2 * HD] = gpair_ref[...]
        for copy in placed:
            copy.wait()

    def tokens(first):
        heads = o_ref[...].T
        near = dot(heads, out_keep_ref[...], ((1,), (0,)))
        away = dot(heads, out_got_ref[...], ((1,), (0,)))
        low, high = jnp.where(core == 0, near, away), jnp.where(core == 0, away, near)
        out = dot(act0_ref[...], down_ref[0], ((1,), (0,))) + dot(
            act1_ref[...], down_ref[1], ((1,), (0,))
        )
        out = out + jnp.concatenate([low, high], axis=1)
        two = dot(dz0_ref[...], up_ref[0], ((1,), (1,))) + dot(
            dz1_ref[...], up_ref[1], ((1,), (1,))
        )
        one = dot(dq_ref[...].T, w_ref[:, :HALF], ((1,), (1,)))
        if first:
            one = one + pair_ref[...]
        unit, _ = standard(x_ref[...])
        scaled = one * rows_ref[0:1, :] + two * rows_ref[2:3, :]
        refs = (keep_ref, tkeep_ref) if first else (send_ref, tsend_ref)
        refs[0][...], refs[1][...] = out, scaled
        for i, value in enumerate((one * unit, one, two * unit, two)):
            table_ref[i : i + 1, :] += jnp.sum(value, axis=0, keepdims=True)

    @pl.when(step < blocks // 2)
    def _():
        tokens(True)

    @pl.when(step >= blocks // 2)
    def _():
        tokens(False)

    @pl.when(step == blocks - 1)
    def _():
        small_ref[:, 2 * HD :] = table_ref[...].T.astype(BF)


def feed_forward(normed, normed_t, grad_out, bias, parts, held):
    tokens, width = normed.shape
    hidden = bias.shape[1]
    unit = jax.ShapeDtypeStruct((tokens, hidden), BF)
    here = pl.BlockSpec(memory_space=pltpu.VMEM)
    scratch = [] if parts is None else [
        pltpu.VMEM((width, hidden), BF),
        pltpu.VMEM((hidden, width), BF),
        pltpu.SemaphoreType.DMA((32,)),
    ]
    return pl.pallas_call(
        functools.partial(ffn_first_kernel, parts),
        out_shape=(
            unit,
            unit,
            jax.ShapeDtypeStruct((width, 2 * width), BF),
            jax.ShapeDtypeStruct((1, hidden), F32),
        ),
        in_specs=[here] * 4 + [here if parts is None else pl.BlockSpec(memory_space=pl.ANY)] * len(held),
        out_specs=(here,) * 4,
        scratch_shapes=scratch,
        compiler_params=pltpu.CompilerParams(vmem_limit_bytes=36 << 20),
        cost_estimate=pl.CostEstimate(
            flops=8 * tokens * width * hidden,
            transcendentals=2 * tokens * hidden,
            bytes_accessed=8 * width * hidden + 10 * tokens * width,
        ),
        name="ffn",
    )(normed, normed_t, grad_out, bias, *held)


def after_tokens(parts, held, acts, grads, features, out_t, dq_t, weights, keep, got, pair, rows, sums, biases, gpair):
    tokens, width = features.shape
    hidden = acts[0].shape[1]
    blocks = tokens // BLK

    def whole(rows, columns):
        return pl.BlockSpec((rows, columns), lambda i: (0, 0))

    def block(first, last, columns=width):
        return pl.BlockSpec((BLK, columns), lambda i: (jnp.clip(i - first, 0, last - first), 0))

    every, own, other = block(0, blocks - 1), block(0, blocks // 2 - 1), block(blocks // 2, blocks - 1)
    units = block(0, blocks - 1, hidden)
    across = pl.BlockSpec((HALF, BLK), lambda i: (0, i))
    side = jax.ShapeDtypeStruct((tokens // 2, width), F32)
    scratch = [pltpu.VMEM((128, width), F32)]
    if parts is not None:
        scratch += [
            pltpu.VMEM((2, width, hidden), BF),
            pltpu.VMEM((2, hidden, width), BF),
            pltpu.SemaphoreType.DMA((64,)),
        ]
    return pl.pallas_call(
        functools.partial(tokens_kernel, parts),
        out_shape=(side, side, side, side, jax.ShapeDtypeStruct((width, 2 * HD + 128), BF)),
        grid=(blocks,),
        in_specs=[
            units,
            units,
            units,
            units,
            every,
            across,
            across,
            whole(width, weights.shape[1]),
            whole(HALF, HALF),
            whole(HALF, HALF),
            own,
            whole(8, width),
            whole(16, width),
            whole(1, hidden),
            whole(1, hidden),
            whole(width, 2 * HD),
        ]
        + (
            [pl.BlockSpec((2, width, hidden), lambda i: (0, 0, 0))] * 2
            if parts is None
            else [pl.BlockSpec(memory_space=pl.ANY)] * 4
        ),
        out_specs=(own, other, own, other, whole(width, 2 * HD + 128)),
        scratch_shapes=scratch,
        compiler_params=pltpu.CompilerParams(
            dimension_semantics=("arbitrary",), vmem_limit_bytes=48 << 20
        ),
        cost_estimate=pl.CostEstimate(
            flops=8 * tokens * width * hidden + 4 * tokens * width * HALF,
            transcendentals=0,
            bytes_accessed=8 * width * hidden + 20 * tokens * width,
        ),
        name="after_tokens",
    )(
        *acts, *grads, features, out_t, dq_t, weights, keep, got, pair, rows, sums, *biases, gpair, *held
    )


def shards(
    tokens,
    segments,
    ln1_gain,
    ln1_bias,
    ln2_gain,
    ln2_bias,
    q_weight,
    q_bias,
    kv_weight,
    k_bias,
    out_weight,
    out_bias,
    up_weight,
    up_bias,
    down_weight,
    cotangent,
):
    core, chip = lax.axis_index("core"), lax.axis_index("chip")
    chips = lax.axis_size("rows") * lax.axis_size("chip")
    own = tokens.shape[1]
    both = 2 * own
    rows = q_weight.shape[0]
    hidden = up_bias.shape[0]
    half = hidden // 2
    back_chips = DOC // both
    own_tokens, own_grad = tokens[0], cotangent[0]

    def half_columns(array, which):
        return lax.dynamic_slice_in_dim(
            array, which * (array.shape[1] // 2), array.shape[1] // 2, 1
        )

    def first(which):
        return jnp.concatenate(
            [half_columns(q_weight, which), half_columns(out_weight, which), kv_weight], axis=1
        )

    up_blocks = up_weight

    def up_half(which):
        block = up_blocks.reshape(rows, chips, 2, 2, half)
        block = lax.dynamic_index_in_dim(block, which, 2, keepdims=False)
        return block.transpose(0, 2, 1, 3).reshape(rows, FF // 2)

    flat = (ln1_gain, ln1_bias, ln2_gain, ln2_bias, q_bias, out_bias)
    if square_line():
        vectors = jnp.concatenate(
            [vector.reshape(1, rows) for vector in flat] + [up_bias.reshape(hidden // rows, rows)]
        )
        vectors = jnp.pad(vectors, ((0, 16 - vectors.shape[0]), (0, 0)))
        mine, theirs = pack(q_weight, out_weight, kv_weight, vectors)
        attn_piece = by_core(core, mine, core_swap(theirs), 0)
        segments, up_blocks = after((segments, up_blocks), attn_piece)
        attn_line = jnp.concatenate(gather_line(attn_piece))
        attn_rows = gather_rows(attn_line)
        up_piece = by_core(core, up_half(core), core_swap(up_half(1 - core)), 0)
        ff_piece = jnp.concatenate([up_piece[:, :D], up_piece[:, D:], down_weight], axis=0)
        ff_line = gather_line(ff_piece)
        other_tokens = core_swap(own_tokens)
        features = jnp.concatenate([own_tokens, other_tokens], axis=0)
        grad_out = jnp.concatenate([own_grad, core_swap(own_grad)], axis=0)
        attn_rows, grad_out, features = lax.optimization_barrier((attn_rows, grad_out, features))
    else:
        weights = gather_whole(by_core(core, first(core), core_swap(first(1 - core)), 0))
        every = ("rows", "chip", "core")
        table = lax.all_gather(jnp.stack(flat), every, axis=1, tiled=True).astype(F32)
        vector_rows = jnp.pad(table, ((0, 2), (0, 0)))
        bias = gather_whole(up_bias).astype(F32).reshape(chips, 2, half)
        hidden_bias = jnp.pad(bias.transpose(1, 0, 2).reshape(2, D), ((0, 6), (0, 0)))

    if not square_line():
        other_tokens = core_swap(own_tokens)
        features = jnp.concatenate([own_tokens, other_tokens], axis=0)
        grad_out = jnp.concatenate([own_grad, core_swap(own_grad)], axis=0)

    ids = lax.broadcasted_iota(jnp.int32, (MAX_SEGS, 1), 0)
    doc_starts = jnp.sum((segments < ids).astype(jnp.int32), axis=1, keepdims=True)
    first_place, second_place = (chip * 2 + core) * own, (chip * 2 + 1 - core) * own
    span = lax.broadcasted_iota(jnp.int32, (1, own), 1)
    places = jnp.concatenate([first_place + span, second_place + span], axis=1)
    segs = jnp.concatenate(
        [
            lax.dynamic_slice(segments, (0, first_place), (1, own)),
            lax.dynamic_slice(segments, (0, second_place), (1, own)),
        ],
        axis=1,
    )
    starts = jnp.sum(jnp.where(segs == ids, doc_starts, 0), axis=0, keepdims=True)
    relative = places - starts
    frequency = 10000.0 ** (-(jnp.arange(ROT // 2, dtype=F32) * 2.0 / ROT))
    angles = relative.astype(F32) * frequency[:, None]
    cosine, sine = jnp.cos(angles), jnp.sin(angles)
    window_start = (chip - back_chips) * both
    pos = jnp.concatenate(
        [starts - window_start, places - window_start, jnp.zeros((6, both), jnp.int32)], axis=0
    )
    firsts, lasts = pos[:, ::BLK], pos[:, BLK - 1 :: BLK]
    scal = jnp.concatenate(
        [
            core.reshape(1),
            jnp.stack([firsts[0] // BLK, lasts[1] // BLK + 1, lasts[0]], axis=1).reshape(-1),
        ]
    ).astype(jnp.int32)


    bias_column = k_bias.astype(F32)[:, None]
    if square_line():
        weights, vector_rows, hidden_bias, *fronts = front(
            attn_rows, own_tokens, other_tokens, bias_column, cosine, sine
        )
    else:
        fronts = front(
            (weights, vector_rows), own_tokens, other_tokens, bias_column, cosine, sine
        )
    normed_one, normed_two, normed_two_t, query_t, own_pairs, keep, send = fronts
    got = core_swap(send)
    mine = jnp.concatenate(
        [chip_shift(own_pairs, k, False) for k in range(back_chips, 0, -1)] + [own_pairs], axis=0
    )
    theirs = core_swap(mine)
    if square_line():
        ff_rows = gather_rows(after(jnp.concatenate(ff_line), attn_rows))

    heads = attention(scal, query_t, grad_out, keep, got, pos, cosine, sine, mine, theirs)
    if square_line():
        heads, ff_rows = lax.optimization_barrier((heads, ff_rows))
    out_t, grad_query_t, pair_mine, pair_theirs = heads
    pair_got = core_swap(pair_theirs)
    grad_query, proj_keep, proj_send, sums = after_heads(
        out_t, grad_query_t, normed_one, grad_out
    )
    proj_got = core_swap(proj_send)
    if square_line():
        pair_got, proj_got = after((pair_got, proj_got), sums)
        step = 2 * rows
        parts = [((i * step, step, 0), ((2 + i) * step, step, 1)) for i in range(2)] + [
            tuple((i * step, step, (i // 2, i % 2)) for i in range(4))
        ]
        held = [ff_rows] * 3
    else:
        up_whole = gather_whole(by_core(core, up_half(core), core_swap(up_half(1 - core)), 0))
        down_whole = gather_whole(down_weight).reshape(chips, 2, half, D)
        down_whole = down_whole.transpose(1, 0, 2, 3).reshape(2, D, D)
        parts = [None] * 3
        ups = jnp.stack([up_whole[:, :D], up_whole[:, D:]])
        held = [(ups[0], down_whole[0]), (ups[1], down_whole[1]), (ups, down_whole)]
    pair_sum = pair_mine + pair_got
    arrived = [
        chip_shift(
            pair_sum[(back_chips - k) * own : (back_chips - k + 1) * own].astype(BF), -k, False
        )
        for k in range(1, back_chips + 1)
    ]
    grad_proj = by_core(core, proj_keep, proj_got, 0)
    attn_terms = jnp.concatenate([grad_query, grad_proj], axis=1)
    if square_line():
        attn_plane, attn_one = reduce_rows(attn_terms)
    grad_pair, grad_one_pair, key_bias = after_pairs(
        pair_sum, *arrived, normed_one, weights, cosine, sine
    )
    key_bias = key_bias[0, :HD]

    inputs = (normed_two, normed_two_t, grad_out)
    act0, dz0, terms0, bias0 = feed_forward(*inputs, hidden_bias[0:1], parts[0], held[0])
    if square_line():
        (act0, dz0, terms0, bias0), attn_one, grad_pair, grad_one_pair, key_bias = lax.optimization_barrier(
            ((act0, dz0, terms0, bias0), attn_one, grad_pair, grad_one_pair, key_bias)
        )
        planes0, one0 = reduce_first(terms0)
        other_bias = core_swap(key_bias)
    act1, dz1, terms1, bias1 = feed_forward(*inputs, hidden_bias[1:2], parts[1], held[1])
    if square_line():
        (act1, dz1, terms1, bias1), one0, other_bias = lax.optimization_barrier(
            ((act1, dz1, terms1, bias1), one0, other_bias)
        )
        two0 = reduce_second(planes0, one0)
        planes1, one1 = reduce_first(terms1)
        key_bias = key_bias + other_bias
        other_bias = line_swap(key_bias, 1)
    part, part_send, scaled, scaled_send, small_terms = after_tokens(
        parts[2],
        held[2],
        (act0, act1),
        (dz0, dz1),
        features,
        out_t,
        grad_query_t,
        weights,
        keep,
        got,
        grad_one_pair,
        vector_rows,
        sums,
        (bias0, bias1),
        grad_pair,
    )
    if square_line():
        (part, part_send, scaled, scaled_send, small_terms), two0, one1, other_bias = (
            lax.optimization_barrier(
                ((part, part_send, scaled, scaled_send, small_terms), two0, one1, other_bias)
            )
        )
        key_bias = key_bias + other_bias
    part_got, scaled_got = core_swap(part_send), core_swap(scaled_send)

    def finish(part_got, scaled_got):
        layer_out = own_tokens.astype(F32) + part + part_got + vector_rows[5:6]
        total = scaled + scaled_got
        unit, spread = standard(own_tokens)
        input_grad = own_grad.astype(F32) + spread * (
            total
            - jnp.mean(total, axis=-1, keepdims=True)
            - unit * jnp.mean(total * unit, axis=-1, keepdims=True)
        )
        return layer_out.astype(BF), input_grad

    def split(value):
        return (
            lax.dynamic_slice_in_dim(value, core * rows, rows, 0),
            core_swap(lax.dynamic_slice_in_dim(value, (1 - core) * rows, rows, 0)),
        )

    def blocks(first_half, second_half):
        return jnp.stack(
            [value.reshape(rows, chips, half) for value in (first_half, second_half)], axis=2
        ).reshape(rows, chips, 1, hidden)

    if square_line():
        small_grid = small_terms.reshape((4, 4, small_terms.shape[0] // 16) + small_terms.shape[1:])
        row = lax.axis_index("rows")
        small_planes = [
            lax.dynamic_index_in_dim(small_grid, row ^ bit, 0, keepdims=False) for bit in range(4)
        ]
        two1 = reduce_second(planes1, one1, small_planes)
        own0, three0 = reduce_third((planes0[0], *two0), (attn_plane, *attn_one))
        small_far = rows_swap(after(small_planes[3], part_got), 3)
        layer_out, input_grad = finish(part_got, scaled_got)
        other_bias = line_swap(after(key_bias, part_got), 2)
        two1, three0, small_far, layer_out, input_grad, other_bias = lax.optimization_barrier(
            (two1, three0, small_far, layer_out, input_grad, other_bias)
        )
        key_bias = key_bias + other_bias
        own1, three1 = reduce_third(
            (planes1[0], *(part[:, :, : 2 * D] for part in two1)),
            (small_planes[0], small_far, *(part[:, :, 2 * D :] for part in two1)),
        )
        other_bias = rows_swap(after(key_bias, two1), 1)
        key_bias = key_bias + other_bias
        sum0 = reduce_last(own0, three0)
        sum0, attn_sum = sum0[:, : 2 * D], sum0[:, 2 * D :]
        attn_split = split(after(attn_sum, other_bias))
        up_split = split(after(sum0, other_bias)[:, :D])
        key_bias_out = key_bias + rows_swap(key_bias, 2)
        mine, theirs = attn_split
        query_out = by_core(core, mine[:, :HALF], theirs[:, :HALF], 1)
        proj_out = by_core(core, mine[:, HALF:], theirs[:, HALF:], 1)
        three1, up_split, query_out, proj_out, key_bias_out = lax.optimization_barrier(
            (three1, up_split, query_out, proj_out, key_bias_out)
        )
        sum1 = reduce_last(own1, three1)
        sum1, small_sum = sum1[:, : 2 * D], sum1[:, 2 * D :]
    else:
        layer_out, input_grad = finish(part_got, scaled_got)
        sum0, sum1, small_sum = (reduce_whole(terms) for terms in (terms0, terms1, small_terms))
        up_split = split(sum0[:, :D])
        mine, theirs = split(reduce_whole(attn_terms))
        query_out = by_core(core, mine[:, :HALF], theirs[:, :HALF], 1)
        proj_out = by_core(core, mine[:, HALF:], theirs[:, HALF:], 1)
        key_bias_out = lax.psum(key_bias, ("rows", "chip", "core"))
    mine, theirs = split(jnp.concatenate([sum1[:, :D], small_sum], axis=1))
    rest = mine[:, D:] + theirs[:, D:]
    pair_out, vector_out = rest[:, : 2 * HD], rest[:, 2 * HD :]
    up_bias_out = small_sum[:, 2 * HD + 6 : 2 * HD + 8].T.reshape(hidden)
    up_out = by_core(
        core, blocks(up_split[0], mine[:, :D]), blocks(up_split[1], theirs[:, :D]), 2
    ).reshape(rows, FF)
    down_out = jnp.concatenate([sum0[:, D:], sum1[:, D : 2 * D]], axis=0)
    return (
        layer_out[None],
        input_grad[None],
        vector_out[:, 0],
        vector_out[:, 1],
        vector_out[:, 2],
        vector_out[:, 3],
        query_out,
        vector_out[:, 4],
        pair_out,
        key_bias_out,
        proj_out,
        vector_out[:, 5],
        up_out,
        up_bias_out,
        down_out,
    )


def solution(mesh):
    devices = mesh.devices.reshape(mesh.shape["rows"], mesh.shape["wide"] // 2, 2)
    every, wide = ("rows", "chip", "core"), ("chip", "core")
    matrix, vector, sequence = P(every, None), P(every), P("rows", wide, None)
    return jax.shard_map(
        shards,
        mesh=Mesh(devices, every),
        in_specs=(
            sequence,
            P("rows", None),
            vector,
            vector,
            vector,
            vector,
            matrix,
            vector,
            matrix,
            P(),
            matrix,
            vector,
            matrix,
            vector,
            matrix,
            sequence,
        ),
        out_specs=(
            sequence,
            sequence,
            vector,
            vector,
            vector,
            vector,
            matrix,
            vector,
            matrix,
            P(),
            matrix,
            vector,
            matrix,
            vector,
            matrix,
        ),
        check_vma=False,
    )
```
